256 devices in a mesh: section: 4 (over y), seq: 64 (over z, x, core).
Axes of the slice: x: 4, y: 4, z: 8, core: 2. Of those that a mesh axis runs over, the one named last changes fastest.
Arguments:
- queries: bfloat16 [4, 8192, 2048], P('section', 'seq'), may hold values from -6 to 6
- key_rows: bfloat16 [4, 8192, 2048], P('section', 'seq'), may hold values from -6 to 6
- value_rows: bfloat16 [4, 8192, 2048], P('section', 'seq'), may hold values from -6 to 6
- grad_out: bfloat16 [4, 8192, 2048], P('section', 'seq'), may hold values from -24 to 24
- log_sums: bfloat16 [4, 16, 8192], P('section', None, 'seq'), may hold values from 4 to 6
- deltas: bfloat16 [4, 16, 8192], P('section', None, 'seq'), may hold values from -96 to 96
- offsets: int32 [64, 16], P('seq'), may hold values from 0 to 7
Outputs:
- grad_query: bfloat16 [4, 8192, 2048], P('section', 'seq')
- grad_key: bfloat16 [4, 8192, 2048], P('section', 'seq')
- grad_value: bfloat16 [4, 8192, 2048], P('section', 'seq')
The draws below stay inside these ranges and needn't reach their ends.
All inputs are finite; a program needn't handle non-finite values.
Results may differ from the reference program's by a relative error of at most 0.012.
Values may be sent and summed in bfloat16 or wider, within the bound.
No kernel may reach another device: no remote copies, remote signals or barrier semaphores. Data moves between devices by JAX's collectives and lax.ppermute only.
A program may use at most 128 MiB of HBM per device.

```python
import jax
import jax.numpy as jnp
from jax import lax

TOK_DEV = 128
PICK = 16
HEADS = 16
HD = 128
RATE = 8
SECTIONS = 4
SHARDS = 64
TOKENS = 8192
PICKED = 1024


def set_ends(array, own_key, low, top_value):
    place = [jax.random.randint(jax.random.fold_in(own_key, axis), (), 0, length) for axis, length in enumerate(array.shape)]
    main_axis = array.shape.index(max(array.shape))
    next_to = place[:main_axis] + [(place[main_axis] + 1) % array.shape[main_axis]] + place[main_axis + 1:]
    return array.at[tuple(place)].set(low).at[tuple(next_to)].set(top_value)


def levels(own_key, extent, split, least, high):
    loudness, own = 1.0, jax.random.fold_in(own_key, 6)
    for position, parts in split:
        steps = jnp.exp(jax.random.uniform(jax.random.fold_in(own, position), (parts,), jnp.float32, least / len(split), high / len(split)))
        loudness = loudness * jnp.repeat(steps, extent[position] // parts).reshape([-1 if axis == position else 1 for axis in range(len(extent))])
    return loudness


def centred(own_key, extent, scale, bound, split=(), kind=jnp.bfloat16):
    array = jax.random.normal(own_key, extent, jnp.float32) * scale
    if len(split) > 0:
        array = levels(own_key, extent, split, -0.22, 0.18) * array
    return jnp.clip(array, min=-bound, max=bound).astype(kind)


def setup_inputs(seed: int = 0) -> dict:
    streams_of = jax.random.split(jax.random.key(seed), 8)
    return {
        "queries": centred(streams_of[0], (SECTIONS, TOKENS, HEADS * HD), 1.0, 6.0, ((0, 4), (1, 64))),
        "key_rows": centred(streams_of[1], (SECTIONS, TOKENS, HEADS * HD), 1.0, 6.0, ((0, 4), (1, 64))),
        "value_rows": centred(streams_of[2], (SECTIONS, TOKENS, HEADS * HD), 1.0, 6.0, ((0, 4), (1, 64))),
        "grad_out": centred(streams_of[3], (SECTIONS, TOKENS, HEADS * HD), 4.0, 24.0, ((0, 4), (1, 64))),
        "log_sums": jnp.clip(4.0 + 2.0 * jax.random.uniform(streams_of[4], (SECTIONS, HEADS, TOKENS), jnp.float32) ** levels(streams_of[4], (SECTIONS, HEADS, TOKENS), ((0, 4), (2, 64)), -0.2, 0.2), 4.0, 6.0).astype(jnp.bfloat16),
        "deltas": centred(streams_of[5], (SECTIONS, HEADS, TOKENS), 16.0, 96.0, ((0, 4), (2, 64))),
        "offsets": set_ends(jax.random.randint(streams_of[6], (SHARDS, HEADS), 0, RATE), jax.random.fold_in(streams_of[6], 1), 0, RATE - 1).astype(jnp.int32),
    }


def pick_rows(block, offsets):
    width = block.shape[-1]
    shaped = block.reshape(SHARDS, PICK, RATE, HEADS, width)
    index = jnp.broadcast_to(offsets.astype(jnp.int32)[:, None, None, :, None], (SHARDS, PICK, 1, HEADS, width))
    return jnp.take_along_axis(shaped, index, axis=2)[:, :, 0].reshape(PICKED, HEADS, width)


def pick_stats(stats, offsets):
    shaped = stats.reshape(HEADS, SHARDS, PICK, RATE)
    index = jnp.broadcast_to(offsets.astype(jnp.int32).T[:, :, None, None], (HEADS, SHARDS, PICK, 1))
    return jnp.take_along_axis(shaped, index, axis=3)[:, :, :, 0].reshape(HEADS, PICKED)


def attention_grads(query, key_part, value, grad, lse, delta):
    scale = HD ** -0.5
    scores = jnp.einsum('qhd,khd->hqk', query, key_part) * scale
    probs = jnp.exp(scores - lse[:, :, None])
    dprob = jnp.einsum('qhd,khd->hqk', grad, value)
    dscore = probs * (dprob - delta[:, :, None])
    probs_low = lax.optimization_barrier(probs.astype(jnp.bfloat16)).astype(jnp.float32)
    dscore_low = lax.optimization_barrier(dscore.astype(jnp.bfloat16)).astype(jnp.float32)
    grad_v = jnp.einsum('hqk,qhd->khd', probs_low, grad)
    grad_q = jnp.einsum('hqk,khd->qhd', dscore_low, key_part) * scale
    grad_k = jnp.einsum('hqk,qhd->khd', dscore_low, query) * scale
    return grad_q, grad_k, grad_v


def reference(queries, key_rows, value_rows, grad_out, log_sums, deltas, offsets):
    grad_next = jnp.roll(grad_out, -1, axis=0)
    mask = jnp.arange(RATE, dtype=jnp.int32)[None, :, None] == offsets.astype(jnp.int32)[:, None, :]

    def one_section(stacked):
        query, key_part, value, grad, lse, delta = stacked

        def shaped(block):
            return block.astype(jnp.float32).reshape(SHARDS, TOK_DEV, HEADS, HD)

        q_four, k_four, v_four, g_four = shaped(query), shaped(key_part), shaped(value), shaped(grad)
        lse_all = lse.astype(jnp.float32)
        delta_all = delta.astype(jnp.float32)
        lse_shard = lse_all.reshape(HEADS, SHARDS, TOK_DEV).transpose(1, 0, 2)
        delta_shard = delta_all.reshape(HEADS, SHARDS, TOK_DEV).transpose(1, 0, 2)
        local_q, local_k, local_v = lax.map(lambda blk: attention_grads(*blk), (q_four, k_four, v_four, g_four, lse_shard, delta_shard))
        wide_q, wide_k, wide_v = attention_grads(pick_rows(q_four, offsets), pick_rows(k_four, offsets), pick_rows(v_four, offsets), pick_rows(g_four, offsets), pick_stats(lse_all, offsets), pick_stats(delta_all, offsets))

        def combine(local_part, wide_part):
            spread = jnp.where(mask[:, None, :, :, None], wide_part.reshape(SHARDS, PICK, 1, HEADS, HD), 0.0)
            total = local_part.reshape(SHARDS, PICK, RATE, HEADS, HD) + spread
            return total.reshape(TOKENS, HEADS * HD).astype(jnp.bfloat16)

        return combine(local_q, wide_q), combine(local_k, wide_k), combine(local_v, wide_v)

    grad_query, grad_key, grad_value = lax.map(one_section, (queries, key_rows, value_rows, grad_next, log_sums, deltas))
    return (grad_query, grad_key, grad_value)
```

```python
import functools

import jax
import jax.numpy as jnp
from jax import lax
from jax.experimental import pallas as pl
from jax.experimental.pallas import tpu as pltpu
from jax.sharding import PartitionSpec as P


HEADS = 16
HD = 128
PICK = 16
RATE = 8
TOK = 128
NZ, NX, NC = 8, 4, 2
ROWS = 72
GROUP = NZ * NC
SCALE = HD ** (-0.5)
BF = jnp.bfloat16
F32 = jnp.float32

VM = pl.BlockSpec(memory_space=pltpu.VMEM)
SM = pl.BlockSpec(memory_space=pltpu.SMEM)


def dot(a, b):
    return lax.dot_general(a, b, (((1,), (0,)), ((), ())), preferred_element_type=F32)


def dot_t(a, b):
    return lax.dot_general(a, b, (((1,), (1,)), ((), ())), preferred_element_type=F32)


def dot_l(a, b):
    return lax.dot_general(a, b, (((0,), (0,)), ((), ())), preferred_element_type=F32)


def pick(x, off):
    t = x.astype(F32).reshape(PICK, RATE, HD)
    row = lax.broadcasted_iota(jnp.int32, (PICK, RATE, HD), 1)
    return jnp.sum(jnp.where(row == off, t, 0.0), axis=1).astype(BF)


def pick_grad_kernel(off_ref, g_ref, o_ref):
    base = pl.program_id(0) * 4
    for i in range(4):
        o_ref[i] = pick(g_ref[:, i * HD:(i + 1) * HD], off_ref[0, base + i])


def pick_kernel(off_ref, pos_ref, q_ref, k_ref, v_ref, g_ref, l_ref, d_ref, o_ref, st_ref):
    step = pl.program_id(0)
    base = step * 4
    n = pos_ref[0]

    @pl.when(step == 0)
    def _():
        head = lax.broadcasted_iota(jnp.int32, (HEADS, TOK), 0)
        lane = lax.broadcasted_iota(jnp.int32, (HEADS, TOK), 1)
        off = jnp.zeros((HEADS, TOK), jnp.int32)
        for h in range(HEADS):
            off = jnp.where(head == h, off_ref[0, h], off)
        hit = (lane % RATE) == off
        src = lax.broadcasted_iota(jnp.int32, (TOK, TOK), 0)
        dst = lax.broadcasted_iota(jnp.int32, (TOK, TOK), 1)
        place = jnp.where(dst == (n % 8) * PICK + src // RATE, 1.0, 0.0).astype(BF)
        lse = jnp.where(hit, l_ref[0].astype(F32), 0.0).astype(BF)
        dlt = jnp.where(hit, d_ref[0].astype(F32), 0.0).astype(BF)
        st_ref[0] = dot(lse, place)
        st_ref[1] = dot(dlt, place)

    row = lax.broadcasted_iota(jnp.int32, (8, HD), 0)
    lses = st_ref[0, pl.ds(pl.multiple_of(base, 4), 4), :]
    dlts = st_ref[1, pl.ds(pl.multiple_of(base, 4), 4), :]
    for i in range(4):
        off = off_ref[0, base + i]
        cols = slice(i * HD, (i + 1) * HD)
        o_ref[i, 0:16] = pick(q_ref[0, :, cols], off)
        o_ref[i, 16:32] = pick(k_ref[0, :, cols], off)
        o_ref[i, 32:48] = pick(v_ref[0, :, cols], off)
        o_ref[i, 48:64] = g_ref[i]
        lse = jnp.broadcast_to(lses[i:i + 1], (8, HD))
        dlt = jnp.broadcast_to(dlts[i:i + 1], (8, HD))
        stats = jnp.where(row == n // 8, lse, jnp.where(row == 2 + n // 8, dlt, 0.0))
        o_ref[i, 64:72] = stats.astype(BF)


def pick_grad(offsets, grad):
    return pl.pallas_call(
        pick_grad_kernel,
        grid=(4,),
        in_specs=[SM, pl.BlockSpec((None, TOK, 4 * HD), lambda i: (0, 0, i))],
        out_specs=pl.BlockSpec((4, PICK, HD), lambda i: (i, 0, 0)),
        out_shape=jax.ShapeDtypeStruct((HEADS, PICK, HD), BF),
        name="pick_grad",
    )(offsets, grad)


def pick_all(offsets, pos, query, key, value, grad, lse, delta):
    wide = pl.BlockSpec((1, TOK, 4 * HD), lambda i: (0, 0, i))
    whole = pl.BlockSpec((1, HEADS, TOK), lambda i: (0, 0, 0))
    return pl.pallas_call(
        pick_kernel,
        grid=(4,),
        in_specs=[SM, SM, wide, wide, wide, pl.BlockSpec((4, PICK, HD), lambda i: (i, 0, 0)), whole, whole],
        out_specs=pl.BlockSpec((4, ROWS, HD), lambda i: (i, 0, 0)),
        out_shape=jax.ShapeDtypeStruct((HEADS, ROWS, HD), BF),
        scratch_shapes=[pltpu.VMEM((2, HEADS, HD), F32)],
        name="pick_all",
    )(offsets, pos, query, key, value, grad, lse, delta)


def local_kernel(q_ref, k_ref, v_ref, g_ref, l_ref, d_ref, dq_ref, dk_ref, dv_ref):
    base = pl.program_id(0) * 4
    for i in range(4):
        cols = slice(i * HD, (i + 1) * HD)
        q, k, v, g = q_ref[0, :, cols], k_ref[0, :, cols], v_ref[0, :, cols], g_ref[0, :, cols]
        lse = l_ref[i].astype(F32)
        dlt = d_ref[i].astype(F32)
        p = jnp.exp(dot_t(k, q) * SCALE - lse)
        ds = (p * (dot_t(v, g) - dlt)).astype(BF)
        dv_ref[:, cols] = dot(p.astype(BF), g).astype(BF)
        dk_ref[:, cols] = (dot(ds, q) * SCALE).astype(BF)
        dq_ref[:, cols] = (dot_l(ds, k) * SCALE).astype(BF)


def local_grads(query, key, value, grad, lse, delta):
    wide = pl.BlockSpec((1, TOK, 4 * HD), lambda i: (0, 0, i))
    out = pl.BlockSpec((TOK, 4 * HD), lambda i: (0, i))
    stat = pl.BlockSpec((4, 1, TOK), lambda i: (i, 0, 0))
    shape = jax.ShapeDtypeStruct((TOK, HEADS * HD), BF)
    return pl.pallas_call(
        local_kernel,
        grid=(4,),
        in_specs=[wide, wide, wide, wide, stat, stat],
        out_specs=[out, out, out],
        out_shape=[shape, shape, shape],
        cost_estimate=pl.CostEstimate(flops=16 * 5 * 2 * 128 ** 3 * 4, bytes_accessed=3670016, transcendentals=262144),
        name="local_grads",
    )(query, key, value, grad, lse.reshape(HEADS, 1, TOK), delta.reshape(HEADS, 1, TOK))


def rows_of(ref, part, count):
    return ref[:, part * PICK:(part + 1) * PICK, :].reshape(count * PICK, HD)


def stats_of(ref):
    return jnp.sum(ref[:, 64:72, :].astype(F32), axis=0)


def wide_kernel(own_ref, left_ref, right_ref, far0_ref, far1_ref, o_ref):
    count = GROUP
    q, k, v, g = (rows_of(own_ref, part, count) for part in range(4))
    own_stats = stats_of(own_ref)
    turned = jnp.transpose(jnp.concatenate([own_stats, jnp.zeros((HD - 8, HD), F32)], axis=0))
    lse_col = jnp.concatenate([turned[:, 0:1], turned[:, 1:2]], axis=0)
    dlt_col = jnp.concatenate([turned[:, 2:3], turned[:, 3:4]], axis=0)
    dq = jnp.zeros((count * PICK, HD), F32)
    dk = jnp.zeros((count * PICK, HD), F32)
    dv = jnp.zeros((count * PICK, HD), F32)
    far_stats = stats_of(far0_ref) + stats_of(far1_ref)
    both = [(own_ref, own_stats), (left_ref, stats_of(left_ref)), (right_ref, stats_of(right_ref)), (None, far_stats)]
    for ref, st in both:
        if ref is None:
            qx, kx, vx, gx = (
                jnp.concatenate([rows_of(far0_ref, part, count // 2), rows_of(far1_ref, part, count // 2)], axis=0)
                for part in range(4)
            )
        else:
            qx, kx, vx, gx = (rows_of(ref, part, count) for part in range(4))
        p = jnp.exp(dot_t(q, kx) * SCALE - lse_col)
        ds = (p * (dot_t(g, vx) - dlt_col)).astype(BF)
        dq = dq + dot(ds, kx)
        lse_row = jnp.concatenate([st[0:1], st[1:2]], axis=1)
        dlt_row = jnp.concatenate([st[2:3], st[3:4]], axis=1)
        p2 = jnp.exp(dot_t(k, qx) * SCALE - lse_row)
        ds2 = (p2 * (dot_t(v, gx) - dlt_row)).astype(BF)
        dk = dk + dot(ds2, qx)
        dv = dv + dot(p2.astype(BF), gx)
    o_ref[:, 0:16, :] = (dq * SCALE).astype(BF).reshape(count, PICK, HD)
    o_ref[:, 16:32, :] = (dk * SCALE).astype(BF).reshape(count, PICK, HD)
    o_ref[:, 32:48, :] = dv.astype(BF).reshape(count, PICK, HD)


def wide_grads(own, left, right, far0, far1):
    return pl.pallas_call(
        wide_kernel,
        in_specs=[VM] * 5,
        out_specs=VM,
        out_shape=jax.ShapeDtypeStruct((GROUP, 3 * PICK, HD), BF),
        name="wide_grads",
    )(own, left, right, far0, far1)


def combine_kernel(off_ref, w_ref, q_ref, k_ref, v_ref, oq_ref, ok_ref, ov_ref):
    base = pl.program_id(0) * 4
    row = lax.broadcasted_iota(jnp.int32, (PICK, RATE, HD), 1)
    for i in range(4):
        cols = slice(i * HD, (i + 1) * HD)
        hit = row == off_ref[0, base + i]
        for part, (src, out) in enumerate(((q_ref, oq_ref), (k_ref, ok_ref), (v_ref, ov_ref))):
            w = w_ref[i, part * PICK:(part + 1) * PICK, :].astype(F32)
            local = src[:, cols].astype(F32).reshape(PICK, RATE, HD)
            total = local + jnp.where(hit, w[:, None, :], 0.0)
            out[0, :, cols] = total.reshape(TOK, HD).astype(BF)


def combine(offsets, wide, dq, dk, dv):
    src = pl.BlockSpec((TOK, 4 * HD), lambda i: (0, i))
    out = pl.BlockSpec((1, TOK, 4 * HD), lambda i: (0, 0, i))
    shape = jax.ShapeDtypeStruct((1, TOK, HEADS * HD), BF)
    return pl.pallas_call(
        combine_kernel,
        grid=(4,),
        in_specs=[SM, pl.BlockSpec((4, 3 * PICK, HD), lambda i: (i, 0, 0)), src, src, src],
        out_specs=[out, out, out],
        out_shape=[shape, shape, shape],
        name="combine",
    )(offsets, wide, dq, dk, dv)


def place_of(z, x, c):
    return (z * NX + x) * NC + c


GROUPS = [[place_of(z, x, c) for z in range(NZ) for c in range(NC)] for x in range(NX)]


def shift_x(value, steps):
    pairs = [
        (place_of(z, x, c), place_of(z, (x + steps) % NX, c))
        for z in range(NZ) for x in range(NX) for c in range(NC)
    ]
    return lax.ppermute(value, "seq", pairs)


def from_next(value):
    count = lax.axis_size("section")
    return lax.ppermute(value, "section", [((s + 1) % count, s) for s in range(count)])


def per_device(queries, key_rows, value_rows, grad_out, log_sums, deltas, offsets):
    seat = lax.axis_index("seq")
    pos = ((seat // (NX * NC)) * NC + seat % NC).astype(jnp.int32).reshape(1)
    picked_grad = from_next(pick_grad(offsets, grad_out))
    grad_src, picked_grad = lax.optimization_barrier((grad_out, picked_grad))
    grad = from_next(grad_src)
    sends = pick_all(offsets, pos, queries, key_rows, value_rows, picked_grad, log_sums, deltas)
    own = lax.all_to_all(sends, "seq", 0, 0, axis_index_groups=GROUPS, tiled=True)
    left = shift_x(own, 1)
    right = shift_x(own, -1)
    far0 = shift_x(left[:GROUP // 2], 1)
    far1 = shift_x(right[GROUP // 2:], -1)
    local_q, local_k, local_v = local_grads(queries, key_rows, value_rows, grad, log_sums, deltas)
    wide = wide_grads(own, left, right, far0, far1)
    back = lax.all_to_all(wide, "seq", 0, 0, axis_index_groups=GROUPS, tiled=True)
    return tuple(combine(offsets, back, local_q, local_k, local_v))


def solution(mesh):
    rows = P("section", "seq", None)
    stats = P("section", None, "seq")
    return jax.shard_map(
        per_device,
        mesh=mesh,
        in_specs=(rows, rows, rows, rows, stats, stats, P("seq", None)),
        out_specs=(rows, rows, rows),
        check_vma=False,
    )
```

```python
import jax
import jax.numpy as jnp
from jax import lax
from jax.experimental import pallas as pl
from jax.experimental.pallas import tpu as pltpu
from jax.sharding import PartitionSpec as P


HEADS = 16
HD = 128
PICK = 16
RATE = 8
TOK = 128
NZ, NX, NC = 8, 4, 2
QG_ROWS = 40
GROUP = NZ * NC
SCALE = HD ** (-0.5)
BF = jnp.bfloat16
F32 = jnp.float32

VM = pl.BlockSpec(memory_space=pltpu.VMEM)
SM = pl.BlockSpec(memory_space=pltpu.SMEM)


def dot(a, b):
    return lax.dot_general(a, b, (((1,), (0,)), ((), ())), preferred_element_type=F32)


def dot_t(a, b):
    return lax.dot_general(a, b, (((1,), (1,)), ((), ())), preferred_element_type=F32)


def dot_l(a, b):
    return lax.dot_general(a, b, (((0,), (0,)), ((), ())), preferred_element_type=F32)


def pick(x, off):
    t = x.astype(F32).reshape(PICK, RATE, HD)
    row = lax.broadcasted_iota(jnp.int32, (PICK, RATE, HD), 1)
    return jnp.sum(jnp.where(row == off, t, 0.0), axis=1).astype(BF)


def small(mib=12):
    return pltpu.CompilerParams(vmem_limit_bytes=mib << 20)


def pick_grad_kernel(off_ref, g_ref, o_ref):
    for h in range(HEADS):
        o_ref[h] = pick(g_ref[0, :, h * HD:(h + 1) * HD], off_ref[0, h])


def pick_kv_kernel(off_ref, k_ref, v_ref, o_ref):
    for h in range(HEADS):
        cols = slice(h * HD, (h + 1) * HD)
        o_ref[h, 0:16] = pick(k_ref[0, :, cols], off_ref[0, h])
        o_ref[h, 16:32] = pick(v_ref[0, :, cols], off_ref[0, h])


def pick_q_kernel(off_ref, pos_ref, q_ref, g_ref, l_ref, d_ref, o_ref):
    n = pos_ref[0]
    head = lax.broadcasted_iota(jnp.int32, (HEADS, TOK), 0)
    lane = lax.broadcasted_iota(jnp.int32, (HEADS, TOK), 1)
    off = jnp.zeros((HEADS, TOK), jnp.int32)
    for h in range(HEADS):
        off = jnp.where(head == h, off_ref[0, h], off)
    hit = (lane % RATE) == off
    src = lax.broadcasted_iota(jnp.int32, (TOK, TOK), 0)
    dst = lax.broadcasted_iota(jnp.int32, (TOK, TOK), 1)
    place = jnp.where(dst == (n % 8) * PICK + src // RATE, 1.0, 0.0).astype(BF)
    lses = dot(jnp.where(hit, l_ref[0].astype(F32), 0.0).astype(BF), place)
    dlts = dot(jnp.where(hit, d_ref[0].astype(F32), 0.0).astype(BF), place)
    row = lax.broadcasted_iota(jnp.int32, (8, HD), 0)
    for h in range(HEADS):
        o_ref[h, 0:16] = pick(q_ref[0, :, h * HD:(h + 1) * HD], off_ref[0, h])
        o_ref[h, 16:32] = g_ref[h]
        lse = jnp.broadcast_to(lses[h:h + 1], (8, HD))
        dlt = jnp.broadcast_to(dlts[h:h + 1], (8, HD))
        stats = jnp.where(row == n // 8, lse, jnp.where(row == 2 + n // 8, dlt, 0.0))
        o_ref[h, 32:40] = stats.astype(BF)


def pick_grad(offsets, grad):
    return pl.pallas_call(
        pick_grad_kernel,
        in_specs=[SM, VM],
        out_specs=VM,
        out_shape=jax.ShapeDtypeStruct((HEADS, PICK, HD), BF),
        compiler_params=small(),
        name="pick_grad",
    )(offsets, grad)


def pick_kv(offsets, key, value):
    return pl.pallas_call(
        pick_kv_kernel,
        in_specs=[SM, VM, VM],
        out_specs=VM,
        out_shape=jax.ShapeDtypeStruct((HEADS, 2 * PICK, HD), BF),
        compiler_params=small(),
        name="pick_kv",
    )(offsets, key, value)


def pick_q(offsets, pos, query, grad, lse, delta):
    return pl.pallas_call(
        pick_q_kernel,
        in_specs=[SM, SM, VM, VM, VM, VM],
        out_specs=VM,
        out_shape=jax.ShapeDtypeStruct((HEADS, QG_ROWS, HD), BF),
        compiler_params=small(),
        name="pick_q",
    )(offsets, pos, query, grad, lse, delta)


def local_kernel(q_ref, k_ref, v_ref, g_ref, l_ref, d_ref, dq_ref, dk_ref, dv_ref, st_ref):
    step = pl.program_id(0)

    @pl.when(step == 0)
    def _():
        st_ref[0] = l_ref[0].astype(F32)
        st_ref[1] = d_ref[0].astype(F32)

    base = pl.multiple_of(step * 4, 4)
    lses = st_ref[0, pl.ds(base, 4), :]
    dlts = st_ref[1, pl.ds(base, 4), :]
    for i in range(4):
        cols = slice(i * HD, (i + 1) * HD)
        q, k, v, g = q_ref[0, :, cols], k_ref[0, :, cols], v_ref[0, :, cols], g_ref[0, :, cols]
        p = jnp.exp(dot_t(k, q) * SCALE - lses[i:i + 1])
        ds = (p * (dot_t(v, g) - dlts[i:i + 1])).astype(BF)
        dv_ref[:, cols] = dot(p.astype(BF), g).astype(BF)
        dk_ref[:, cols] = (dot(ds, q) * SCALE).astype(BF)
        dq_ref[:, cols] = (dot_l(ds, k) * SCALE).astype(BF)


def local_grads(query, key, value, grad, lse, delta):
    wide = pl.BlockSpec((1, TOK, 4 * HD), lambda i: (0, 0, i))
    out = pl.BlockSpec((TOK, 4 * HD), lambda i: (0, i))
    stat = pl.BlockSpec((1, HEADS, TOK), lambda i: (0, 0, 0))
    shape = jax.ShapeDtypeStruct((TOK, HEADS * HD), BF)
    return pl.pallas_call(
        local_kernel,
        grid=(4,),
        in_specs=[wide, wide, wide, wide, stat, stat],
        out_specs=[out, out, out],
        out_shape=[shape, shape, shape],
        scratch_shapes=[pltpu.VMEM((2, HEADS, TOK), F32)],
        compiler_params=small(),
        cost_estimate=pl.CostEstimate(flops=16 * 5 * 2 * 128 ** 3 * 4, bytes_accessed=3670016, transcendentals=262144),
        name="local_grads",
    )(query, key, value, grad, lse, delta)


def rows_of(ref, part):
    count = ref.shape[0]
    return ref[:, part * PICK:(part + 1) * PICK, :].reshape(count * PICK, HD)


def both_halves(a, b, part):
    return jnp.concatenate([rows_of(a, part), rows_of(b, part)], axis=0)


def stats_of(ref):
    return jnp.sum(ref[:, 32:40, :].astype(F32), axis=0)


def key_side(k, v, q, g, stats):
    lse = jnp.concatenate([stats[0:1], stats[1:2]], axis=1)
    dlt = jnp.concatenate([stats[2:3], stats[3:4]], axis=1)
    p = jnp.exp(dot_t(k, q) * SCALE - lse)
    ds = (p * (dot_t(v, g) - dlt)).astype(BF)
    return dot(ds, q), dot(p.astype(BF), g)


def wide_kernel(qg_ref, kv_ref, lkv_ref, rkv_ref, akv_ref, bkv_ref, lqg_ref, rqg_ref, dq_ref, dk_ref, dv_ref):
    q, g, k, v = rows_of(qg_ref, 0), rows_of(qg_ref, 1), rows_of(kv_ref, 0), rows_of(kv_ref, 1)
    stats = stats_of(qg_ref)
    turned = jnp.transpose(jnp.concatenate([stats, jnp.zeros((HD - 8, HD), F32)], axis=0))
    lse = jnp.concatenate([turned[:, 0:1], turned[:, 1:2]], axis=0)
    dlt = jnp.concatenate([turned[:, 2:3], turned[:, 3:4]], axis=0)
    dq = None
    for kx, vx in (
        (k, v),
        (rows_of(lkv_ref, 0), rows_of(lkv_ref, 1)),
        (rows_of(rkv_ref, 0), rows_of(rkv_ref, 1)),
        (both_halves(akv_ref, bkv_ref, 0), both_halves(akv_ref, bkv_ref, 1)),
    ):
        p = jnp.exp(dot_t(q, kx) * SCALE - lse)
        ds = (p * (dot_t(g, vx) - dlt)).astype(BF)
        part = dot(ds, kx)
        dq = part if dq is None else dq + part
    dq_ref[...] = (dq * SCALE).astype(BF).reshape(GROUP, PICK, HD)
    dk, dv = key_side(k, v, q, g, stats)
    for ref in (lqg_ref, rqg_ref):
        more_k, more_v = key_side(k, v, rows_of(ref, 0), rows_of(ref, 1), stats_of(ref))
        dk, dv = dk + more_k, dv + more_v
    dk_ref[...] = dk
    dv_ref[...] = dv


def wide_grads(*args):
    part = jax.ShapeDtypeStruct((GROUP * PICK, HD), F32)
    return pl.pallas_call(
        wide_kernel,
        in_specs=[VM] * 8,
        out_specs=[VM] * 3,
        out_shape=[jax.ShapeDtypeStruct((GROUP, PICK, HD), BF), part, part],
        compiler_params=small(),
        cost_estimate=pl.CostEstimate(flops=14 * 2 * 256 * 256 * 128 * 2, bytes_accessed=1572864, transcendentals=524288),
        name="wide_grads",
    )(*args)


def last_kernel(kv_ref, aqg_ref, bqg_ref, dq_ref, dk_ref, dv_ref, o_ref):
    k, v = rows_of(kv_ref, 0), rows_of(kv_ref, 1)
    q, g = both_halves(aqg_ref, bqg_ref, 0), both_halves(aqg_ref, bqg_ref, 1)
    dk, dv = key_side(k, v, q, g, stats_of(aqg_ref) + stats_of(bqg_ref))
    o_ref[:, 0:16, :] = dq_ref[...]
    o_ref[:, 16:32, :] = ((dk_ref[...] + dk) * SCALE).astype(BF).reshape(GROUP, PICK, HD)
    o_ref[:, 32:48, :] = (dv_ref[...] + dv).astype(BF).reshape(GROUP, PICK, HD)


def last_grads(*args):
    return pl.pallas_call(
        last_kernel,
        in_specs=[VM] * 6,
        out_specs=VM,
        out_shape=jax.ShapeDtypeStruct((GROUP, 3 * PICK, HD), BF),
        compiler_params=small(),
        name="last_grads",
    )(*args)


def combine_kernel(off_ref, w_ref, *refs):
    row = lax.broadcasted_iota(jnp.int32, (PICK, RATE, HD), 1)
    for h in range(HEADS):
        hit = row == off_ref[0, h]
        for part in range(3):
            w = w_ref[h, part * PICK:(part + 1) * PICK, :].astype(F32)
            local = refs[part][:, h * HD:(h + 1) * HD].astype(F32).reshape(PICK, RATE, HD)
            total = local + jnp.where(hit, w[:, None, :], 0.0)
            refs[3 + part][0, :, h * HD:(h + 1) * HD] = total.reshape(TOK, HD).astype(BF)


def combine(offsets, wide, local):
    shape = jax.ShapeDtypeStruct((1, TOK, HEADS * HD), BF)
    return pl.pallas_call(
        combine_kernel,
        in_specs=[SM] + [VM] * 4,
        out_specs=[VM] * 3,
        out_shape=[shape, shape, shape],
        compiler_params=small(),
        name="combine",
    )(offsets, wide, *local)


def place_of(z, x, c):
    return (z * NX + x) * NC + c


GROUPS = [[place_of(z, x, c) for z in range(NZ) for c in range(NC)] for x in range(NX)]


def shift_x(value, steps):
    pairs = [
        (place_of(z, x, c), place_of(z, (x + steps) % NX, c))
        for z in range(NZ) for x in range(NX) for c in range(NC)
    ]
    return lax.ppermute(value, "seq", pairs)


def from_next(value):
    count = lax.axis_size("section")
    return lax.ppermute(value, "section", [((s + 1) % count, s) for s in range(count)])


def swap(value):
    return lax.all_to_all(value, "seq", 0, 0, axis_index_groups=GROUPS, tiled=True)


def body(queries, key_rows, value_rows, grad_out, log_sums, deltas, offsets):
    seat = lax.axis_index("seq")
    pos = ((seat // (NX * NC)) * NC + seat % NC).astype(jnp.int32).reshape(1)
    grad_rows = pick_grad(offsets, grad_out)
    picked_grad = from_next(grad_rows)
    kv_rows = pick_kv(offsets, key_rows, value_rows)
    kv = swap(kv_rows)
    grad_src, picked_grad = lax.optimization_barrier((grad_out, picked_grad))
    grad = from_next(grad_src)
    qg_rows = pick_q(offsets, pos, queries, picked_grad, log_sums, deltas)
    qg_rows, _ = lax.optimization_barrier((qg_rows, kv))
    qg = swap(qg_rows)
    half = GROUP // 2
    left_kv = shift_x(kv, 1)
    right_kv = shift_x(kv, -1)
    left_qg = shift_x(qg, 1)
    right_qg = shift_x(qg, -1)
    left_far_kv = shift_x(left_kv[:half], 1)
    right_far_kv = shift_x(right_kv[half:], -1)
    far_kv = (left_far_kv, right_far_kv)
    far_qg = (shift_x(left_qg[:half], 1), shift_x(right_qg[half:], -1))
    local = local_grads(queries, key_rows, value_rows, grad, log_sums, deltas)
    dq, dk, dv = wide_grads(qg, kv, left_kv, right_kv, *far_kv, left_qg, right_qg)
    back = swap(last_grads(kv, *far_qg, dq, dk, dv))
    return tuple(combine(offsets, back, local))


def solution(mesh):
    rows = P("section", "seq", None)
    stats = P("section", None, "seq")
    return jax.shard_map(
        body,
        mesh=mesh,
        in_specs=(rows, rows, rows, rows, stats, stats, P("seq", None)),
        out_specs=(rows, rows, rows),
        check_vma=False,
    )
```

```python
import jax
import jax.numpy as jnp
from jax import lax
from jax.experimental import pallas as pl
from jax.experimental.pallas import tpu as pltpu
from jax.sharding import PartitionSpec as P


HEADS = 16
HD = 128
PICK = 16
RATE = 8
TOK = 128
NZ, NX, NC = 8, 4, 2
ROWS = 72
GROUP = NZ * NC
SCALE = HD ** (-0.5)
BF = jnp.bfloat16
F32 = jnp.float32

VM = pl.BlockSpec(memory_space=pltpu.VMEM)
SM = pl.BlockSpec(memory_space=pltpu.SMEM)


def dot(a, b):
    return lax.dot_general(a, b, (((1,), (0,)), ((), ())), preferred_element_type=F32)


def dot_t(a, b):
    return lax.dot_general(a, b, (((1,), (1,)), ((), ())), preferred_element_type=F32)


def dot_l(a, b):
    return lax.dot_general(a, b, (((0,), (0,)), ((), ())), preferred_element_type=F32)


def pick(x, off):
    t = x.astype(F32).reshape(PICK, RATE, HD)
    row = lax.broadcasted_iota(jnp.int32, (PICK, RATE, HD), 1)
    return jnp.sum(jnp.where(row == off, t, 0.0), axis=1).astype(BF)


def small(mib=12):
    return pltpu.CompilerParams(vmem_limit_bytes=mib << 20)


def pick_grad_kernel(off_ref, g_ref, o_ref):
    for h in range(HEADS):
        o_ref[h] = pick(g_ref[0, :, h * HD:(h + 1) * HD], off_ref[0, h])


def pick_kernel(off_ref, pos_ref, q_ref, k_ref, v_ref, l_ref, d_ref, o_ref):
    n = pos_ref[0]
    head = lax.broadcasted_iota(jnp.int32, (HEADS, TOK), 0)
    lane = lax.broadcasted_iota(jnp.int32, (HEADS, TOK), 1)
    off = jnp.zeros((HEADS, TOK), jnp.int32)
    for h in range(HEADS):
        off = jnp.where(head == h, off_ref[0, h], off)
    hit = (lane % RATE) == off
    src = lax.broadcasted_iota(jnp.int32, (TOK, TOK), 0)
    dst = lax.broadcasted_iota(jnp.int32, (TOK, TOK), 1)
    place = jnp.where(dst == (n % 8) * PICK + src // RATE, 1.0, 0.0).astype(BF)
    lses = dot(jnp.where(hit, l_ref[0].astype(F32), 0.0).astype(BF), place)
    dlts = dot(jnp.where(hit, d_ref[0].astype(F32), 0.0).astype(BF), place)
    row = lax.broadcasted_iota(jnp.int32, (8, HD), 0)
    for h in range(HEADS):
        cols = slice(h * HD, (h + 1) * HD)
        o_ref[h, 0:16] = pick(q_ref[0, :, cols], off_ref[0, h])
        o_ref[h, 16:32] = pick(k_ref[0, :, cols], off_ref[0, h])
        o_ref[h, 32:48] = pick(v_ref[0, :, cols], off_ref[0, h])
        lse = jnp.broadcast_to(lses[h:h + 1], (8, HD))
        dlt = jnp.broadcast_to(dlts[h:h + 1], (8, HD))
        stats = jnp.where(row == n // 8, lse, jnp.where(row == 2 + n // 8, dlt, 0.0))
        o_ref[h, 64:72] = stats.astype(BF)


def join_kernel(rows_ref, g_ref, o_ref):
    o_ref[:, 48:64, :] = g_ref[...]


def pick_grad(offsets, grad):
    return pl.pallas_call(
        pick_grad_kernel,
        in_specs=[SM, VM],
        out_specs=VM,
        out_shape=jax.ShapeDtypeStruct((HEADS, PICK, HD), BF),
        compiler_params=small(),
        name="pick_grad",
    )(offsets, grad)


def pick_rest(offsets, pos, query, key, value, lse, delta):
    return pl.pallas_call(
        pick_kernel,
        in_specs=[SM, SM] + [VM] * 5,
        out_specs=VM,
        out_shape=jax.ShapeDtypeStruct((HEADS, ROWS, HD), BF),
        compiler_params=small(),
        name="pick_rest",
    )(offsets, pos, query, key, value, lse, delta)


def join(rows, grad):
    return pl.pallas_call(
        join_kernel,
        in_specs=[VM, VM],
        out_specs=VM,
        out_shape=jax.ShapeDtypeStruct((HEADS, ROWS, HD), BF),
        input_output_aliases={0: 0},
        compiler_params=small(),
        name="join",
    )(rows, grad)


def local_kernel(q_ref, k_ref, v_ref, g_ref, l_ref, d_ref, dq_ref, dk_ref, dv_ref, st_ref):
    step = pl.program_id(0)

    @pl.when(step == 0)
    def _():
        st_ref[0] = l_ref[0].astype(F32)
        st_ref[1] = d_ref[0].astype(F32)

    base = pl.multiple_of(step * 4, 4)
    lses = st_ref[0, pl.ds(base, 4), :]
    dlts = st_ref[1, pl.ds(base, 4), :]
    for i in range(4):
        cols = slice(i * HD, (i + 1) * HD)
        q, k, v, g = q_ref[0, :, cols], k_ref[0, :, cols], v_ref[0, :, cols], g_ref[0, :, cols]
        p = jnp.exp(dot_t(k, q) * SCALE - lses[i:i + 1])
        ds = (p * (dot_t(v, g) - dlts[i:i + 1])).astype(BF)
        dv_ref[:, cols] = dot(p.astype(BF), g).astype(BF)
        dk_ref[:, cols] = (dot(ds, q) * SCALE).astype(BF)
        dq_ref[:, cols] = (dot_l(ds, k) * SCALE).astype(BF)


def local_grads(query, key, value, grad, lse, delta):
    wide = pl.BlockSpec((1, TOK, 4 * HD), lambda i: (0, 0, i))
    out = pl.BlockSpec((TOK, 4 * HD), lambda i: (0, i))
    stat = pl.BlockSpec((1, HEADS, TOK), lambda i: (0, 0, 0))
    shape = jax.ShapeDtypeStruct((TOK, HEADS * HD), BF)
    return pl.pallas_call(
        local_kernel,
        grid=(4,),
        in_specs=[wide, wide, wide, wide, stat, stat],
        out_specs=[out, out, out],
        out_shape=[shape, shape, shape],
        scratch_shapes=[pltpu.VMEM((2, HEADS, TOK), F32)],
        compiler_params=small(),
        cost_estimate=pl.CostEstimate(flops=16 * 5 * 2 * 128 ** 3 * 4, bytes_accessed=3670016, transcendentals=262144),
        name="local_grads",
    )(query, key, value, grad, lse, delta)


def rows_of(ref, part):
    count = ref.shape[0]
    return ref[:, part * PICK:(part + 1) * PICK, :].reshape(count * PICK, HD)


def both_halves(a, b, part):
    return jnp.concatenate([rows_of(a, part), rows_of(b, part)], axis=0)


def stats_of(ref):
    return jnp.sum(ref[:, 64:72, :].astype(F32), axis=0)


def query_side(q, g, k, v, lse, dlt):
    p = jnp.exp(dot_t(q, k) * SCALE - lse)
    ds = (p * (dot_t(g, v) - dlt)).astype(BF)
    return dot(ds, k)


def key_side(k, v, q, g, stats):
    lse = jnp.concatenate([stats[0:1], stats[1:2]], axis=1)
    dlt = jnp.concatenate([stats[2:3], stats[3:4]], axis=1)
    p = jnp.exp(dot_t(k, q) * SCALE - lse)
    ds = (p * (dot_t(v, g) - dlt)).astype(BF)
    return dot(ds, q), dot(p.astype(BF), g)


def columns(stats):
    turned = jnp.transpose(jnp.concatenate([stats, jnp.zeros((HD - 8, HD), F32)], axis=0))
    lse = jnp.concatenate([turned[:, 0:1], turned[:, 1:2]], axis=0)
    dlt = jnp.concatenate([turned[:, 2:3], turned[:, 3:4]], axis=0)
    return lse, dlt


def near_kernel(own_ref, left_ref, right_ref, dq_ref, dk_ref, dv_ref):
    q, k, v, g = (rows_of(own_ref, part) for part in range(4))
    stats = stats_of(own_ref)
    lse, dlt = columns(stats)
    dq = query_side(q, g, k, v, lse, dlt)
    dk, dv = key_side(k, v, q, g, stats)
    for ref in (left_ref, right_ref):
        qx, kx, vx, gx = (rows_of(ref, part) for part in range(4))
        dq = dq + query_side(q, g, kx, vx, lse, dlt)
        more_k, more_v = key_side(k, v, qx, gx, stats_of(ref))
        dk, dv = dk + more_k, dv + more_v
    dq_ref[...] = dq
    dk_ref[...] = dk
    dv_ref[...] = dv


def near_grads(*args):
    part = jax.ShapeDtypeStruct((GROUP * PICK, HD), F32)
    return pl.pallas_call(
        near_kernel,
        in_specs=[VM] * 3,
        out_specs=[VM] * 3,
        out_shape=[part] * 3,
        compiler_params=small(),
        cost_estimate=pl.CostEstimate(flops=21 * 2 * 256 * 256 * 128 * 2, bytes_accessed=1572864, transcendentals=524288),
        name="near_grads",
    )(*args)


def far_kernel(own_ref, a_ref, b_ref, dq_ref, dk_ref, dv_ref, o_ref):
    q, k, v, g = (rows_of(own_ref, part) for part in range(4))
    lse, dlt = columns(stats_of(own_ref))
    qx, kx, vx, gx = (both_halves(a_ref, b_ref, part) for part in range(4))
    dq = query_side(q, g, kx, vx, lse, dlt)
    dk, dv = key_side(k, v, qx, gx, stats_of(a_ref) + stats_of(b_ref))
    o_ref[:, 0:16, :] = ((dq_ref[...] + dq) * SCALE).astype(BF).reshape(GROUP, PICK, HD)
    o_ref[:, 16:32, :] = ((dk_ref[...] + dk) * SCALE).astype(BF).reshape(GROUP, PICK, HD)
    o_ref[:, 32:48, :] = (dv_ref[...] + dv).astype(BF).reshape(GROUP, PICK, HD)


def far_grads(*args):
    return pl.pallas_call(
        far_kernel,
        in_specs=[VM] * 6,
        out_specs=VM,
        out_shape=jax.ShapeDtypeStruct((GROUP, 3 * PICK, HD), BF),
        compiler_params=small(),
        name="far_grads",
    )(*args)


def combine_kernel(off_ref, w_ref, *refs):
    row = lax.broadcasted_iota(jnp.int32, (PICK, RATE, HD), 1)
    for h in range(HEADS):
        hit = row == off_ref[0, h]
        for part in range(3):
            w = w_ref[h, part * PICK:(part + 1) * PICK, :].astype(F32)
            local = refs[part][:, h * HD:(h + 1) * HD].astype(F32).reshape(PICK, RATE, HD)
            total = local + jnp.where(hit, w[:, None, :], 0.0)
            refs[3 + part][0, :, h * HD:(h + 1) * HD] = total.reshape(TOK, HD).astype(BF)


def combine(offsets, wide, local):
    shape = jax.ShapeDtypeStruct((1, TOK, HEADS * HD), BF)
    return pl.pallas_call(
        combine_kernel,
        in_specs=[SM] + [VM] * 4,
        out_specs=[VM] * 3,
        out_shape=[shape, shape, shape],
        compiler_params=small(),
        name="combine",
    )(offsets, wide, *local)


def place_of(z, x, c):
    return (z * NX + x) * NC + c


GROUPS = [[place_of(z, x, c) for z in range(NZ) for c in range(NC)] for x in range(NX)]


def shift_x(value, steps):
    pairs = [
        (place_of(z, x, c), place_of(z, (x + steps) % NX, c))
        for z in range(NZ) for x in range(NX) for c in range(NC)
    ]
    return lax.ppermute(value, "seq", pairs)


def from_next(value):
    count = lax.axis_size("section")
    return lax.ppermute(value, "section", [((s + 1) % count, s) for s in range(count)])


def swap(value):
    return lax.all_to_all(value, "seq", 0, 0, axis_index_groups=GROUPS, tiled=True)


def body(queries, key_rows, value_rows, grad_out, log_sums, deltas, offsets):
    seat = lax.axis_index("seq")
    pos = ((seat // (NX * NC)) * NC + seat % NC).astype(jnp.int32).reshape(1)
    grad_rows = pick_grad(offsets, grad_out)
    picked_grad = from_next(grad_rows)
    grad = from_next(grad_out)
    rows = pick_rest(offsets, pos, queries, key_rows, value_rows, log_sums, deltas)
    own = swap(join(rows, picked_grad))
    half = GROUP // 2
    left, right = shift_x(own, 1), shift_x(own, -1)
    far = (shift_x(left[:half], 1), shift_x(right[half:], -1))
    local = local_grads(queries, key_rows, value_rows, grad, log_sums, deltas)
    dq, dk, dv = near_grads(own, left, right)
    back = swap(far_grads(own, *far, dq, dk, dv))
    return tuple(combine(offsets, back, local))


def solution(mesh):
    rows = P("section", "seq", None)
    stats = P("section", None, "seq")
    return jax.shard_map(
        body,
        mesh=mesh,
        in_specs=(rows, rows, rows, rows, stats, stats, P("seq", None)),
        out_specs=(rows, rows, rows),
        check_vma=False,
    )
```

```python
import jax
import jax.numpy as jnp
from jax import lax
from jax.experimental import pallas as pl
from jax.experimental.pallas import tpu as pltpu
from jax.sharding import PartitionSpec as P


HEADS = 16
HD = 128
PICK = 16
RATE = 8
TOK = 128
NZ, NX, NC = 8, 4, 2
ROWS = 72
MAIN = 56
GROUP = NZ * NC
SCALE = HD ** (-0.5)
BF = jnp.bfloat16
F32 = jnp.float32

VM = pl.BlockSpec(memory_space=pltpu.VMEM)
SM = pl.BlockSpec(memory_space=pltpu.SMEM)


def dot(a, b):
    return lax.dot_general(a, b, (((1,), (0,)), ((), ())), preferred_element_type=F32)


def dot_t(a, b):
    return lax.dot_general(a, b, (((1,), (1,)), ((), ())), preferred_element_type=F32)


def dot_l(a, b):
    return lax.dot_general(a, b, (((0,), (0,)), ((), ())), preferred_element_type=F32)


def pick(x, off):
    t = x.astype(F32).reshape(PICK, RATE, HD)
    row = lax.broadcasted_iota(jnp.int32, (PICK, RATE, HD), 1)
    return jnp.sum(jnp.where(row == off, t, 0.0), axis=1).astype(BF)


def small(mib=12):
    return pltpu.CompilerParams(vmem_limit_bytes=mib << 20)


def pick_kernel(pos_ref, off_hbm, l_hbm, d_hbm, q_hbm, k_hbm, v_hbm, g_hbm, o_ref, off_ref, l_ref, d_ref, x_ref, sems):
    loads = [
        pltpu.make_async_copy(src, dst, sems.at[i])
        for i, (src, dst) in enumerate(
            (
                (off_hbm, off_ref),
                (q_hbm.at[0], x_ref.at[0]),
                (k_hbm.at[0], x_ref.at[1]),
                (v_hbm.at[0], x_ref.at[2]),
                (g_hbm.at[0], x_ref.at[3]),
                (l_hbm.at[0], l_ref),
                (d_hbm.at[0], d_ref),
            )
        )
    ]
    for load in loads:
        load.start()
    n = pos_ref[0]
    src = lax.broadcasted_iota(jnp.int32, (TOK, TOK), 0)
    dst = lax.broadcasted_iota(jnp.int32, (TOK, TOK), 1)
    place = jnp.where(dst == (n % 8) * PICK + src // RATE, 1.0, 0.0).astype(BF)
    loads[0].wait()
    for part, first in ((0, 0), (1, 16), (2, 32), (3, MAIN)):
        loads[1 + part].wait()
        for h in range(HEADS):
            o_ref[h, first:first + 16] = pick(x_ref[part, :, h * HD:(h + 1) * HD], off_ref[0, h])
    loads[5].wait()
    loads[6].wait()
    head = lax.broadcasted_iota(jnp.int32, (HEADS, TOK), 0)
    lane = lax.broadcasted_iota(jnp.int32, (HEADS, TOK), 1)
    off = jnp.zeros((HEADS, TOK), jnp.int32)
    for h in range(HEADS):
        off = jnp.where(head == h, off_ref[0, h], off)
    hit = (lane % RATE) == off
    lses = dot(jnp.where(hit, l_ref[...].astype(F32), 0.0).astype(BF), place)
    dlts = dot(jnp.where(hit, d_ref[...].astype(F32), 0.0).astype(BF), place)
    row = lax.broadcasted_iota(jnp.int32, (8, HD), 0)
    for h in range(HEADS):
        lse = jnp.broadcast_to(lses[h:h + 1], (8, HD))
        dlt = jnp.broadcast_to(dlts[h:h + 1], (8, HD))
        stats = jnp.where(row == n // 8, lse, jnp.where(row == 2 + n // 8, dlt, 0.0))
        o_ref[h, 48:MAIN] = stats.astype(BF)


def pick_all(pos, offsets, lse, delta, query, key, value, grad):
    raw = pl.BlockSpec(memory_space=pltpu.HBM)
    return pl.pallas_call(
        pick_kernel,
        in_specs=[SM] + [raw] * 7,
        out_specs=VM,
        out_shape=jax.ShapeDtypeStruct((HEADS, ROWS, HD), BF),
        scratch_shapes=[
            pltpu.SMEM((1, HEADS), jnp.int32),
            pltpu.VMEM((HEADS, TOK), BF),
            pltpu.VMEM((HEADS, TOK), BF),
            pltpu.VMEM((4, TOK, HEADS * HD), BF),
            pltpu.SemaphoreType.DMA((7,)),
        ],
        name="pick_all",
    )(pos, offsets, lse, delta, query, key, value, grad)


def local_kernel(q_ref, k_ref, v_ref, g_ref, l_ref, d_ref, dq_ref, dk_ref, dv_ref, st_ref):
    step = pl.program_id(0)

    @pl.when(step == 0)
    def _():
        st_ref[0] = l_ref[0].astype(F32)
        st_ref[1] = d_ref[0].astype(F32)

    base = pl.multiple_of(step * 4, 4)
    lses = st_ref[0, pl.ds(base, 4), :]
    dlts = st_ref[1, pl.ds(base, 4), :]
    for i in range(4):
        cols = slice(i * HD, (i + 1) * HD)
        q, k, v, g = q_ref[0, :, cols], k_ref[0, :, cols], v_ref[0, :, cols], g_ref[0, :, cols]
        p = jnp.exp(dot_t(k, q) * SCALE - lses[i:i + 1])
        ds = (p * (dot_t(v, g) - dlts[i:i + 1])).astype(BF)
        dv_ref[:, cols] = dot(p.astype(BF), g).astype(BF)
        dk_ref[:, cols] = (dot(ds, q) * SCALE).astype(BF)
        dq_ref[:, cols] = (dot_l(ds, k) * SCALE).astype(BF)


def local_grads(query, key, value, grad, lse, delta):
    wide = pl.BlockSpec((1, TOK, 4 * HD), lambda i: (0, 0, i))
    out = pl.BlockSpec((TOK, 4 * HD), lambda i: (0, i))
    stat = pl.BlockSpec((1, HEADS, TOK), lambda i: (0, 0, 0))
    shape = jax.ShapeDtypeStruct((TOK, HEADS * HD), BF)
    return pl.pallas_call(
        local_kernel,
        grid=(4,),
        in_specs=[wide, wide, wide, wide, stat, stat],
        out_specs=[out, out, out],
        out_shape=[shape, shape, shape],
        scratch_shapes=[pltpu.VMEM((2, HEADS, TOK), F32)],
        compiler_params=small(),
        cost_estimate=pl.CostEstimate(flops=16 * 5 * 2 * 128 ** 3 * 4, bytes_accessed=3670016, transcendentals=262144),
        name="local_grads",
    )(query, key, value, grad, lse, delta)


def rows_of(ref, part):
    count = ref.shape[0]
    return ref[:, part * PICK:(part + 1) * PICK, :].reshape(count * PICK, HD)


def stats_of(ref):
    return jnp.sum(ref[:, 48:MAIN, :].astype(F32), axis=0)


def query_side(q, g, k, v, lse, dlt):
    p = jnp.exp(dot_t(q, k) * SCALE - lse)
    ds = (p * (dot_t(g, v) - dlt)).astype(BF)
    return dot(ds, k)


def key_side(k, v, q, g, stats):
    lse = jnp.concatenate([stats[0:1], stats[1:2]], axis=1)
    dlt = jnp.concatenate([stats[2:3], stats[3:4]], axis=1)
    p = jnp.exp(dot_t(k, q) * SCALE - lse)
    ds = (p * (dot_t(v, g) - dlt)).astype(BF)
    return dot(ds, q), dot(p.astype(BF), g)


def columns(stats):
    turned = jnp.transpose(jnp.concatenate([stats, jnp.zeros((HD - 8, HD), F32)], axis=0))
    lse = jnp.concatenate([turned[:, 0:1], turned[:, 1:2]], axis=0)
    dlt = jnp.concatenate([turned[:, 2:3], turned[:, 3:4]], axis=0)
    return lse, dlt


def block_of(ref, g_ref):
    return rows_of(ref, 0), rows_of(ref, 1), rows_of(ref, 2), g_ref[...].reshape(GROUP * PICK, HD)


def near_kernel(own_ref, og_ref, left_ref, lg_ref, right_ref, rg_ref, dq_ref, dk_ref, dv_ref):
    q, k, v, g = block_of(own_ref, og_ref)
    stats = stats_of(own_ref)
    lse, dlt = columns(stats)
    dq = query_side(q, g, k, v, lse, dlt)
    dk, dv = key_side(k, v, q, g, stats)
    for ref, g_ref in ((left_ref, lg_ref), (right_ref, rg_ref)):
        qx, kx, vx, gx = block_of(ref, g_ref)
        dq = dq + query_side(q, g, kx, vx, lse, dlt)
        more_k, more_v = key_side(k, v, qx, gx, stats_of(ref))
        dk, dv = dk + more_k, dv + more_v
    dq_ref[...] = dq
    dk_ref[...] = dk
    dv_ref[...] = dv


def near_grads(*args):
    part = jax.ShapeDtypeStruct((GROUP * PICK, HD), F32)
    return pl.pallas_call(
        near_kernel,
        in_specs=[VM] * 6,
        out_specs=[VM] * 3,
        out_shape=[part] * 3,
        compiler_params=small(),
        cost_estimate=pl.CostEstimate(flops=21 * 2 * 256 * 256 * 128 * 2, bytes_accessed=1572864, transcendentals=524288),
        name="near_grads",
    )(*args)


def far_kernel(own_ref, og_ref, far_ref, fg_ref, dq_ref, dk_ref, dv_ref, o_ref):
    q, k, v, g = block_of(own_ref, og_ref)
    lse, dlt = columns(stats_of(own_ref))
    qx, kx, vx, gx = block_of(far_ref, fg_ref)
    dq = query_side(q, g, kx, vx, lse, dlt)
    dk, dv = key_side(k, v, qx, gx, stats_of(far_ref))
    o_ref[:, 0:16, :] = ((dq_ref[...] + dq) * SCALE).astype(BF).reshape(GROUP, PICK, HD)
    o_ref[:, 16:32, :] = ((dk_ref[...] + dk) * SCALE).astype(BF).reshape(GROUP, PICK, HD)
    o_ref[:, 32:48, :] = (dv_ref[...] + dv).astype(BF).reshape(GROUP, PICK, HD)


def far_grads(*args):
    return pl.pallas_call(
        far_kernel,
        in_specs=[VM] * 7,
        out_specs=VM,
        out_shape=jax.ShapeDtypeStruct((GROUP, 3 * PICK, HD), BF),
        compiler_params=small(),
        name="far_grads",
    )(*args)


def combine_kernel(off_ref, w_ref, *refs):
    row = lax.broadcasted_iota(jnp.int32, (PICK, RATE, HD), 1)
    for h in range(HEADS):
        hit = row == off_ref[0, h]
        for part in range(3):
            w = w_ref[h, part * PICK:(part + 1) * PICK, :].astype(F32)
            local = refs[part][:, h * HD:(h + 1) * HD].astype(F32).reshape(PICK, RATE, HD)
            total = local + jnp.where(hit, w[:, None, :], 0.0)
            refs[3 + part][0, :, h * HD:(h + 1) * HD] = total.reshape(TOK, HD).astype(BF)


def combine(offsets, wide, local):
    shape = jax.ShapeDtypeStruct((1, TOK, HEADS * HD), BF)
    return pl.pallas_call(
        combine_kernel,
        in_specs=[SM] + [VM] * 4,
        out_specs=[VM] * 3,
        out_shape=[shape, shape, shape],
        compiler_params=small(),
        name="combine",
    )(offsets, wide, *local)


def place_of(z, x, c):
    return (z * NX + x) * NC + c


GROUPS = [[place_of(z, x, c) for z in range(NZ) for c in range(NC)] for x in range(NX)]


def shift_x(value, steps):
    pairs = [
        (place_of(z, x, c), place_of(z, (x + steps) % NX, c))
        for z in range(NZ) for x in range(NX) for c in range(NC)
    ]
    return lax.ppermute(value, "seq", pairs)


def from_next(value):
    count = lax.axis_size("section")
    return lax.ppermute(value, "section", [((s + 1) % count, s) for s in range(count)])


def from_next_x(value, steps):
    count, seats = lax.axis_size("section"), lax.axis_size("seq")
    pairs = [
        (((s + 1) % count) * seats + place_of(z, x, c), s * seats + place_of(z, (x + steps) % NX, c))
        for s in range(count) for z in range(NZ) for x in range(NX) for c in range(NC)
    ]
    return lax.ppermute(value, ("section", "seq"), pairs)


def swap(value):
    return lax.all_to_all(value, "seq", 0, 0, axis_index_groups=GROUPS, tiled=True)


def body(queries, key_rows, value_rows, grad_out, log_sums, deltas, offsets):
    seat = lax.axis_index("seq")
    pos = ((seat // (NX * NC)) * NC + seat % NC).astype(jnp.int32).reshape(1)
    picked = pick_all(pos, offsets, log_sums, deltas, queries, key_rows, value_rows, grad_out)
    mine = swap(picked)
    own, grad_row = mine[:, :MAIN], mine[:, MAIN:]
    far = shift_x(own, 2)
    left = shift_x(own, 1)
    right = shift_x(own, -1)
    far_g = from_next_x(grad_row, 2)
    left_g = from_next_x(grad_row, 1)
    right_g = from_next_x(grad_row, -1)
    own_g = from_next_x(grad_row, 0)
    grad = from_next(grad_out)
    local = local_grads(queries, key_rows, value_rows, grad, log_sums, deltas)
    part = near_grads(own, own_g, left, left_g, right, right_g)
    back = swap(far_grads(own, own_g, far, far_g, *part))
    return tuple(combine(offsets, back, local))


def solution(mesh):
    rows = P("section", "seq", None)
    stats = P("section", None, "seq")
    return jax.shard_map(
        body,
        mesh=mesh,
        in_specs=(rows, rows, rows, rows, stats, stats, P("seq", None)),
        out_specs=(rows, rows, rows),
        check_vma=False,
    )
```

```python
import jax
import jax.numpy as jnp
from jax import lax
from jax.experimental import pallas as pl
from jax.experimental.pallas import tpu as pltpu
from jax.sharding import PartitionSpec as P


HEADS = 16
HD = 128
PICK = 16
RATE = 8
TOK = 128
NZ, NX, NC = 8, 4, 2
ROWS = 40
MAIN = 24
GROUP = 32
HALF = GROUP * PICK // 2
SCALE = HD ** (-0.5)
BF = jnp.bfloat16
F32 = jnp.float32

VM = pl.BlockSpec(memory_space=pltpu.VMEM)
SM = pl.BlockSpec(memory_space=pltpu.SMEM)


def dot(a, b):
    return lax.dot_general(a, b, (((1,), (0,)), ((), ())), preferred_element_type=F32)


def dot_t(a, b):
    return lax.dot_general(a, b, (((1,), (1,)), ((), ())), preferred_element_type=F32)


def dot_l(a, b):
    return lax.dot_general(a, b, (((0,), (0,)), ((), ())), preferred_element_type=F32)


def pick(x, off):
    t = x.astype(F32).reshape(PICK, RATE, HD)
    row = lax.broadcasted_iota(jnp.int32, (PICK, RATE, HD), 1)
    return jnp.sum(jnp.where(row == off, t, 0.0), axis=1).astype(BF)


def small(mib=12):
    return pltpu.CompilerParams(vmem_limit_bytes=mib << 20)


def pick_kernel(pos_ref, off_hbm, l_hbm, d_hbm, q_hbm, k_hbm, v_hbm, g_hbm, o_ref, off_ref, l_ref, d_ref, x_ref, sems):
    loads = [
        pltpu.make_async_copy(src, dst, sems.at[i])
        for i, (src, dst) in enumerate(
            (
                (off_hbm, off_ref),
                (q_hbm.at[0], x_ref.at[0]),
                (k_hbm.at[0], x_ref.at[1]),
                (v_hbm.at[0], x_ref.at[2]),
                (g_hbm.at[0], x_ref.at[3]),
                (l_hbm.at[0], l_ref),
                (d_hbm.at[0], d_ref),
            )
        )
    ]
    for load in loads:
        load.start()
    n = pos_ref[0]
    src = lax.broadcasted_iota(jnp.int32, (TOK, TOK), 0)
    dst = lax.broadcasted_iota(jnp.int32, (TOK, TOK), 1)
    place = jnp.where(dst == (n % 8) * PICK + src // RATE, 1.0, 0.0).astype(BF)
    loads[0].wait()
    for part, core, first in ((0, 0, 0), (1, 0, MAIN), (2, 1, 0), (3, 1, MAIN)):
        loads[1 + part].wait()
        for h in range(HEADS):
            rows = pick(x_ref[part, :, h * HD:(h + 1) * HD], off_ref[0, h])
            o_ref[2 * h + core, first:first + 16] = rows
    loads[5].wait()
    loads[6].wait()
    head = lax.broadcasted_iota(jnp.int32, (HEADS, TOK), 0)
    lane = lax.broadcasted_iota(jnp.int32, (HEADS, TOK), 1)
    off = jnp.zeros((HEADS, TOK), jnp.int32)
    for h in range(HEADS):
        off = jnp.where(head == h, off_ref[0, h], off)
    hit = (lane % RATE) == off
    lses = dot(jnp.where(hit, l_ref[...].astype(F32), 0.0).astype(BF), place)
    dlts = dot(jnp.where(hit, d_ref[...].astype(F32), 0.0).astype(BF), place)
    row = lax.broadcasted_iota(jnp.int32, (8, HD), 0)
    for h in range(HEADS):
        lse = jnp.broadcast_to(lses[h:h + 1], (8, HD))
        dlt = jnp.broadcast_to(dlts[h:h + 1], (8, HD))
        stats = jnp.where(row == n // 8, lse, jnp.where(row == 4 + n // 8, dlt, 0.0))
        o_ref[2 * h, 16:MAIN] = stats.astype(BF)
        o_ref[2 * h + 1, 16:MAIN] = jnp.zeros((8, HD), BF)


def pick_all(pos, offsets, lse, delta, query, key, value, grad):
    raw = pl.BlockSpec(memory_space=pltpu.HBM)
    return pl.pallas_call(
        pick_kernel,
        in_specs=[SM] + [raw] * 7,
        out_specs=VM,
        out_shape=jax.ShapeDtypeStruct((GROUP, ROWS, HD), BF),
        scratch_shapes=[
            pltpu.SMEM((1, HEADS), jnp.int32),
            pltpu.VMEM((HEADS, TOK), BF),
            pltpu.VMEM((HEADS, TOK), BF),
            pltpu.VMEM((4, TOK, HEADS * HD), BF),
            pltpu.SemaphoreType.DMA((7,)),
        ],
        name="pick_all",
    )(pos, offsets, lse, delta, query, key, value, grad)


def local_kernel(off_ref, q_ref, k_ref, v_ref, g_ref, l_ref, d_ref, dq_ref, dk_ref, dv_ref, offs_ref, st_ref):
    step = pl.program_id(0)

    @pl.when(step == 0)
    def _():
        st_ref[0] = l_ref[0].astype(F32)
        st_ref[1] = d_ref[0].astype(F32)
        for h in range(HEADS):
            offs_ref[h:h + 1, :] = jnp.full((1, TOK), off_ref[0, h], jnp.int32)

    base = pl.multiple_of(step * 4, 4)
    lses = st_ref[0, pl.ds(base, 4), :]
    dlts = st_ref[1, pl.ds(base, 4), :]
    for i in range(4):
        cols = slice(i * HD, (i + 1) * HD)
        q, k, v, g = q_ref[0, :, cols], k_ref[0, :, cols], v_ref[0, :, cols], g_ref[0, :, cols]
        p = jnp.exp(dot_t(k, q) * SCALE - lses[i:i + 1])
        ds = (p * (dot_t(v, g) - dlts[i:i + 1])).astype(BF)
        dv_ref[:, cols] = dot(p.astype(BF), g).astype(BF)
        dk_ref[:, cols] = (dot(ds, q) * SCALE).astype(BF)
        dq_ref[:, cols] = (dot_l(ds, k) * SCALE).astype(BF)


def local_grads(offsets, query, key, value, grad, lse, delta):
    wide = pl.BlockSpec((1, TOK, 4 * HD), lambda i: (0, 0, i))
    out = pl.BlockSpec((TOK, 4 * HD), lambda i: (0, i))
    stat = pl.BlockSpec((1, HEADS, TOK), lambda i: (0, 0, 0))
    shape = jax.ShapeDtypeStruct((TOK, HEADS * HD), BF)
    return pl.pallas_call(
        local_kernel,
        grid=(4,),
        in_specs=[SM, wide, wide, wide, wide, stat, stat],
        out_specs=[out, out, out, pl.BlockSpec((HEADS, TOK), lambda i: (0, 0))],
        out_shape=[shape, shape, shape, jax.ShapeDtypeStruct((HEADS, TOK), jnp.int32)],
        scratch_shapes=[pltpu.VMEM((2, HEADS, TOK), F32)],
        compiler_params=small(),
        cost_estimate=pl.CostEstimate(flops=16 * 5 * 2 * 128 ** 3 * 4, bytes_accessed=3670016, transcendentals=262144),
        name="local_grads",
    )(offsets, query, key, value, grad, lse, delta)


def query_side(q, g, k, v, lse, dlt):
    p = jnp.exp(dot_t(q, k) * SCALE - lse)
    ds = (p * (dot_t(g, v) - dlt)).astype(BF)
    return dot(ds, k)


def key_side(k, v, q, g, stats):
    lse = jnp.concatenate([stats[i:i + 1] for i in range(4)], axis=1)
    dlt = jnp.concatenate([stats[i:i + 1] for i in range(4, 8)], axis=1)
    p = jnp.exp(dot_t(k, q) * SCALE - lse)
    ds = (p * (dot_t(v, g) - dlt)).astype(BF)
    return dot(ds, q), dot(p.astype(BF), g)


def flat(rows):
    return rows.reshape(GROUP * PICK, HD)


def whole(core, mine_a, mine_b, other_a, other_b):
    zero = core == 0
    q = jnp.where(zero, mine_a[:, 0:16], other_a[:, 0:16])
    v = jnp.where(zero, other_a[:, 0:16], mine_a[:, 0:16])
    st = jnp.sum(jnp.where(zero, mine_a[:, 16:MAIN], other_a[:, 16:MAIN]).astype(F32), axis=0)
    k = jnp.where(zero, mine_b[...], other_b[...])
    g = jnp.where(zero, other_b[...], mine_b[...])
    return flat(q), flat(k), flat(v), flat(g), st


def share(core, rows):
    width = rows.shape[-1]
    t = rows.astype(F32).reshape(GROUP, 2, 8, width)
    return jnp.where(core == 0, t[:, 0], t[:, 1]).reshape(HALF, width)


def near_kernel(core_ref, a_ref, b_ref, oa_ref, hop_ref, cross_ref, sub_ref, col_ref, dq_ref, dk_ref, dv_ref):
    core = core_ref[0]
    mine_b = jnp.where(core == 0, b_ref[...], hop_ref[...])
    q, k, v, g, stats = whole(core, a_ref, mine_b, oa_ref, cross_ref)
    turned = jnp.transpose(jnp.concatenate([stats, jnp.zeros((HD - 8, HD), F32)], axis=0))
    lse = share(core, jnp.concatenate([turned[:, i:i + 1] for i in range(4)], axis=0))
    dlt = share(core, jnp.concatenate([turned[:, i:i + 1] for i in range(4, 8)], axis=0))
    sq, sk, sv, sg = (share(core, rows).astype(BF) for rows in (q, k, v, g))
    for i, rows in enumerate((sq, sk, sv, sg)):
        sub_ref[i] = rows
    lane = lax.broadcasted_iota(jnp.int32, (HALF, HD), 1)
    col_ref[...] = jnp.where(lane == 0, lse, dlt)
    dq_ref[...] = query_side(sq, sg, k, v, lse, dlt)
    dk_ref[...], dv_ref[...] = key_side(sk, sv, q, g, stats)


def near_grads(*args):
    part = jax.ShapeDtypeStruct((HALF, HD), F32)
    return pl.pallas_call(
        near_kernel,
        in_specs=[SM] + [VM] * 5,
        out_specs=[VM] * 5,
        out_shape=[jax.ShapeDtypeStruct((4, HALF, HD), BF)] + [part] * 4,
        compiler_params=small(),
        cost_estimate=pl.CostEstimate(flops=14 * 2 * 256 * 256 * 128 * 2, bytes_accessed=1572864, transcendentals=262144),
        name="near_grads",
    )(*args)


def far_kernel(core_ref, a_ref, b_ref, oa_ref, ob_ref, sub_ref, col_ref, dq_ref, dk_ref, dv_ref, o_ref):
    core = core_ref[0]
    q, k, v, g, stats = whole(core, a_ref, b_ref, oa_ref, ob_ref)
    lse, dlt = col_ref[:, 0:1], col_ref[:, 1:2]
    dq = dq_ref[...] + query_side(sub_ref[0], sub_ref[3], k, v, lse, dlt)
    dk, dv = key_side(sub_ref[1], sub_ref[2], q, g, stats)
    o_ref[:, 0:8, :] = (dq * SCALE).reshape(GROUP, 8, HD).astype(BF)
    o_ref[:, 8:16, :] = ((dk_ref[...] + dk) * SCALE).reshape(GROUP, 8, HD).astype(BF)
    o_ref[:, 16:24, :] = (dv_ref[...] + dv).reshape(GROUP, 8, HD).astype(BF)


def far_grads(*args):
    return pl.pallas_call(
        far_kernel,
        in_specs=[SM] + [VM] * 9,
        out_specs=VM,
        out_shape=jax.ShapeDtypeStruct((GROUP, 24, HD), BF),
        compiler_params=small(),
        name="far_grads",
    )(*args)


def combine_kernel(w_ref, dq_ref, dk_ref, dv_ref, off_ref, oq_ref, ok_ref, ov_ref):
    row = lax.broadcasted_iota(jnp.int32, (PICK, RATE, HD), 1)
    for h in range(HEADS):
        hit = row == off_ref[h:h + 1, :].reshape(1, 1, TOK)
        for part, (src, out) in enumerate(((dq_ref, oq_ref), (dk_ref, ok_ref), (dv_ref, ov_ref))):
            rows = slice(part * 8, (part + 1) * 8)
            w = jnp.concatenate([w_ref[2 * h, rows, :].astype(F32), w_ref[2 * h + 1, rows, :].astype(F32)], axis=0)
            local = src[:, h * HD:(h + 1) * HD].astype(F32).reshape(PICK, RATE, HD)
            total = local + jnp.where(hit, w[:, None, :], 0.0)
            out[0, :, h * HD:(h + 1) * HD] = total.reshape(TOK, HD).astype(BF)


def combine(wide, local):
    shape = jax.ShapeDtypeStruct((1, TOK, HEADS * HD), BF)
    return pl.pallas_call(
        combine_kernel,
        in_specs=[VM] * 5,
        out_specs=[VM] * 3,
        out_shape=[shape, shape, shape],
        compiler_params=small(),
        name="combine",
    )(wide, *local)


def place_of(z, x, c):
    return (z * NX + x) * NC + c


def column(half, place):
    return place if half == 0 else NX - 1 - place


GROUPS = [
    [place_of(z, column(half, p), c) for z in range(NZ) for p in range(2) for c in range(NC)]
    for half in range(2)
]


def move(value, route):
    count, seats = lax.axis_size("section"), lax.axis_size("seq")
    pairs = []
    for s in range(count):
        for z in range(NZ):
            for x in range(NX):
                for c in range(NC):
                    target = route(s, x, c)
                    if target is not None:
                        ts, tx, tc = target
                        pairs.append((s * seats + place_of(z, x, c), (ts % count) * seats + place_of(z, tx, tc)))
    return lax.ppermute(value, ("section", "seq"), pairs)


def swap(value):
    return lax.all_to_all(value, "seq", 0, 0, axis_index_groups=GROUPS, tiled=True)


def body(queries, key_rows, value_rows, grad_out, log_sums, deltas, offsets):
    seat = lax.axis_index("seq").astype(jnp.int32)
    x = seat // NC % NX
    core = (seat % NC).reshape(1)
    pos = (seat // (NX * NC) * 4 + jnp.where(x < 2, x, NX - 1 - x) * 2 + seat % NC).reshape(1)
    grad = move(grad_out, lambda s, x, c: (s - 1, x, c))
    picked = pick_all(pos, offsets, log_sums, deltas, queries, key_rows, value_rows, grad_out)
    mine = swap(picked)
    a, b = mine[:, :MAIN], mine[:, MAIN:]
    far_a = move(a, lambda s, x, c: (s, 3 - x, c))
    far_b = move(b, lambda s, x, c: (s - c, 3 - x, c))
    hop = move(b, lambda s, x, c: (s - 1, x, 1) if c == 1 else None)
    cross = move(b, lambda s, x, c: (s - c, x, 1 - c))
    other_a = move(a, lambda s, x, c: (s, x, 1 - c))
    other_far_a = move(far_a, lambda s, x, c: (s, x, 1 - c))
    other_far_b = move(far_b, lambda s, x, c: (s, x, 1 - c))
    local = local_grads(offsets, queries, key_rows, value_rows, grad, log_sums, deltas)
    part = near_grads(core, a, b, other_a, hop, cross)
    back = swap(far_grads(core, far_a, far_b, other_far_a, other_far_b, *part))
    return tuple(combine(back, local))


def solution(mesh):
    rows = P("section", "seq", None)
    stats = P("section", None, "seq")
    return jax.shard_map(
        body,
        mesh=mesh,
        in_specs=(rows, rows, rows, rows, stats, stats, P("seq", None)),
        out_specs=(rows, rows, rows),
        check_vma=False,
    )
```

```python
import jax
import jax.numpy as jnp
from jax import lax
from jax.experimental import pallas as pl
from jax.experimental.pallas import tpu as pltpu
from jax.sharding import PartitionSpec as P


HEADS = 16
HD = 128
PICK = 16
RATE = 8
TOK = 128
NZ, NX, NC = 8, 4, 2
ROWS = 40
MAIN = 24
GROUP = 32
HALF = GROUP * PICK // 2
SCALE = HD ** (-0.5)
BF = jnp.bfloat16
F32 = jnp.float32

VM = pl.BlockSpec(memory_space=pltpu.VMEM)
SM = pl.BlockSpec(memory_space=pltpu.SMEM)


def dot(a, b):
    return lax.dot_general(a, b, (((1,), (0,)), ((), ())), preferred_element_type=F32)


def dot_t(a, b):
    return lax.dot_general(a, b, (((1,), (1,)), ((), ())), preferred_element_type=F32)


def dot_l(a, b):
    return lax.dot_general(a, b, (((0,), (0,)), ((), ())), preferred_element_type=F32)


def chooser(off):
    row = lax.broadcasted_iota(jnp.int32, (PICK, TOK), 0)
    tok = lax.broadcasted_iota(jnp.int32, (PICK, TOK), 1)
    return jnp.where(tok == row * RATE + off, 1.0, 0.0).astype(BF)


def small(mib=12):
    return pltpu.CompilerParams(vmem_limit_bytes=mib << 20)


def pick_kernel(pos_ref, off_hbm, l_hbm, d_hbm, q_hbm, k_hbm, v_hbm, g_hbm, o_ref, off_ref, l_ref, d_ref, x_ref, sems):
    loads = [
        pltpu.make_async_copy(src, dst, sems.at[i])
        for i, (src, dst) in enumerate(
            (
                (off_hbm, off_ref),
                (q_hbm.at[0], x_ref.at[0]),
                (k_hbm.at[0], x_ref.at[1]),
                (v_hbm.at[0], x_ref.at[2]),
                (g_hbm.at[0], x_ref.at[3]),
                (l_hbm.at[0], l_ref),
                (d_hbm.at[0], d_ref),
            )
        )
    ]
    for load in loads:
        load.start()
    n = pos_ref[0]
    src = lax.broadcasted_iota(jnp.int32, (TOK, TOK), 0)
    dst = lax.broadcasted_iota(jnp.int32, (TOK, TOK), 1)
    place = jnp.where(dst == (n % 8) * PICK + src // RATE, 1.0, 0.0).astype(BF)
    loads[0].wait()
    choose = [chooser(off_ref[0, h]) for h in range(HEADS)]
    for part, core, first in ((0, 0, 0), (1, 0, MAIN), (2, 1, 0), (3, 1, MAIN)):
        loads[1 + part].wait()
        for h in range(HEADS):
            rows = dot(choose[h], x_ref[part, :, h * HD:(h + 1) * HD])
            o_ref[2 * h + core, first:first + 16] = rows.astype(BF)
    loads[5].wait()
    loads[6].wait()
    head = lax.broadcasted_iota(jnp.int32, (HEADS, TOK), 0)
    lane = lax.broadcasted_iota(jnp.int32, (HEADS, TOK), 1)
    off = jnp.zeros((HEADS, TOK), jnp.int32)
    for h in range(HEADS):
        off = jnp.where(head == h, off_ref[0, h], off)
    hit = (lane % RATE) == off
    lses = dot(jnp.where(hit, l_ref[...].astype(F32), 0.0).astype(BF), place)
    dlts = dot(jnp.where(hit, d_ref[...].astype(F32), 0.0).astype(BF), place)
    row = lax.broadcasted_iota(jnp.int32, (8, HD), 0)
    for h in range(HEADS):
        lse = jnp.broadcast_to(lses[h:h + 1], (8, HD))
        dlt = jnp.broadcast_to(dlts[h:h + 1], (8, HD))
        stats = jnp.where(row == n // 8, lse, jnp.where(row == 4 + n // 8, dlt, 0.0))
        o_ref[2 * h, 16:MAIN] = stats.astype(BF)
        o_ref[2 * h + 1, 16:MAIN] = jnp.zeros((8, HD), BF)


def pick_all(pos, offsets, lse, delta, query, key, value, grad):
    raw = pl.BlockSpec(memory_space=pltpu.HBM)
    return pl.pallas_call(
        pick_kernel,
        in_specs=[SM] + [raw] * 7,
        out_specs=VM,
        out_shape=jax.ShapeDtypeStruct((GROUP, ROWS, HD), BF),
        scratch_shapes=[
            pltpu.SMEM((1, HEADS), jnp.int32),
            pltpu.VMEM((HEADS, TOK), BF),
            pltpu.VMEM((HEADS, TOK), BF),
            pltpu.VMEM((4, TOK, HEADS * HD), BF),
            pltpu.SemaphoreType.DMA((7,)),
        ],
        name="pick_all",
    )(pos, offsets, lse, delta, query, key, value, grad)


def local_kernel(off_ref, q_ref, k_ref, v_ref, g_ref, l_ref, d_ref, dq_ref, dk_ref, dv_ref, offs_ref, st_ref):
    step = pl.program_id(0)

    @pl.when(step == 0)
    def _():
        st_ref[0] = l_ref[0].astype(F32)
        st_ref[1] = d_ref[0].astype(F32)
        for h in range(HEADS):
            offs_ref[h:h + 1, :] = jnp.full((1, TOK), off_ref[0, h], jnp.int32)

    base = pl.multiple_of(step * 4, 4)
    lses = st_ref[0, pl.ds(base, 4), :]
    dlts = st_ref[1, pl.ds(base, 4), :]
    for i in range(4):
        cols = slice(i * HD, (i + 1) * HD)
        q, k, v, g = q_ref[0, :, cols], k_ref[0, :, cols], v_ref[0, :, cols], g_ref[0, :, cols]
        p = jnp.exp(dot_t(k, q) * SCALE - lses[i:i + 1])
        ds = (p * (dot_t(v, g) - dlts[i:i + 1])).astype(BF)
        dv_ref[:, cols] = dot(p.astype(BF), g).astype(BF)
        dk_ref[:, cols] = (dot(ds, q) * SCALE).astype(BF)
        dq_ref[:, cols] = (dot_l(ds, k) * SCALE).astype(BF)


def local_grads(offsets, query, key, value, grad, lse, delta):
    wide = pl.BlockSpec((1, TOK, 4 * HD), lambda i: (0, 0, i))
    out = pl.BlockSpec((TOK, 4 * HD), lambda i: (0, i))
    stat = pl.BlockSpec((1, HEADS, TOK), lambda i: (0, 0, 0))
    shape = jax.ShapeDtypeStruct((TOK, HEADS * HD), BF)
    return pl.pallas_call(
        local_kernel,
        grid=(4,),
        in_specs=[SM, wide, wide, wide, wide, stat, stat],
        out_specs=[out, out, out, pl.BlockSpec((HEADS, TOK), lambda i: (0, 0))],
        out_shape=[shape, shape, shape, jax.ShapeDtypeStruct((HEADS, TOK), jnp.int32)],
        scratch_shapes=[pltpu.VMEM((2, HEADS, TOK), F32)],
        compiler_params=small(),
        cost_estimate=pl.CostEstimate(flops=16 * 5 * 2 * 128 ** 3 * 4, bytes_accessed=3670016, transcendentals=262144),
        name="local_grads",
    )(offsets, query, key, value, grad, lse, delta)


def query_side(q, g, k, v, lse, dlt):
    p = jnp.exp(dot_t(q, k) * SCALE - lse)
    ds = (p * (dot_t(g, v) - dlt)).astype(BF)
    return dot(ds, k)


def key_side(k, v, q, g, stats):
    lse = jnp.concatenate([stats[i:i + 1] for i in range(4)], axis=1)
    dlt = jnp.concatenate([stats[i:i + 1] for i in range(4, 8)], axis=1)
    p = jnp.exp(dot_t(k, q) * SCALE - lse)
    ds = (p * (dot_t(v, g) - dlt)).astype(BF)
    return dot(ds, q), dot(p.astype(BF), g)


def flat(rows):
    return rows.reshape(GROUP * PICK, HD)


def whole(core, mine_a, mine_b, other_a, other_b):
    zero = core == 0
    q = jnp.where(zero, mine_a, other_a)
    v = jnp.where(zero, other_a, mine_a)
    k = jnp.where(zero, mine_b, other_b)
    g = jnp.where(zero, other_b, mine_b)
    return flat(q), flat(k), flat(v), flat(g)


def share(core, rows):
    width = rows.shape[-1]
    t = rows.astype(F32).reshape(GROUP, 2, 8, width)
    return jnp.where(core == 0, t[:, 0], t[:, 1]).reshape(HALF, width)


def near_kernel(core_ref, a_ref, b_ref, st_ref, oa_ref, ost_ref, hop_ref, cross_ref, sub_ref, col_ref, dq_ref, dk_ref, dv_ref):
    core = core_ref[0]
    mine_b = jnp.where(core == 0, b_ref[...], hop_ref[...])
    q, k, v, g = whole(core, a_ref[...], mine_b, oa_ref[...], cross_ref[...])
    stats = jnp.where(core == 0, st_ref[...], ost_ref[...]).astype(F32)
    turned = jnp.transpose(jnp.concatenate([stats, jnp.zeros((HD - 8, HD), F32)], axis=0))
    lse = share(core, jnp.concatenate([turned[:, i:i + 1] for i in range(4)], axis=0))
    dlt = share(core, jnp.concatenate([turned[:, i:i + 1] for i in range(4, 8)], axis=0))
    sq, sk, sv, sg = (share(core, rows).astype(BF) for rows in (q, k, v, g))
    for i, rows in enumerate((sq, sk, sv, sg)):
        sub_ref[i] = rows
    lane = lax.broadcasted_iota(jnp.int32, (HALF, HD), 1)
    col_ref[...] = jnp.where(lane == 0, lse, dlt)
    dq_ref[...] = query_side(sq, sg, k, v, lse, dlt)
    dk_ref[...], dv_ref[...] = key_side(sk, sv, q, g, stats)


def stats_kernel(m_ref, o_ref):
    o_ref[...] = jnp.sum(m_ref[:, 16:MAIN, :].astype(F32), axis=0).astype(BF)


def gather_stats(rows):
    return pl.pallas_call(
        stats_kernel,
        in_specs=[VM],
        out_specs=VM,
        out_shape=jax.ShapeDtypeStruct((8, HD), BF),
        compiler_params=small(),
        name="gather_stats",
    )(rows)


def near_grads(*args):
    part = jax.ShapeDtypeStruct((HALF, HD), F32)
    return pl.pallas_call(
        near_kernel,
        in_specs=[SM] + [VM] * 7,
        out_specs=[VM] * 5,
        out_shape=[jax.ShapeDtypeStruct((4, HALF, HD), BF)] + [part] * 4,
        compiler_params=small(),
        cost_estimate=pl.CostEstimate(flops=14 * 2 * 256 * 256 * 128 * 2, bytes_accessed=1572864, transcendentals=262144),
        name="near_grads",
    )(*args)


def far_kernel(core_ref, a_ref, b_ref, st_ref, oa_ref, ob_ref, ost_ref, sub_ref, col_ref, dq_ref, dk_ref, dv_ref, o_ref):
    core = core_ref[0]
    q, k, v, g = whole(core, a_ref[...], b_ref[...], oa_ref[...], ob_ref[...])
    stats = jnp.where(core == 0, st_ref[...], ost_ref[...]).astype(F32)
    lse, dlt = col_ref[:, 0:1], col_ref[:, 1:2]
    dq = dq_ref[...] + query_side(sub_ref[0], sub_ref[3], k, v, lse, dlt)
    dk, dv = key_side(sub_ref[1], sub_ref[2], q, g, stats)
    o_ref[:, 0:8, :] = (dq * SCALE).reshape(GROUP, 8, HD).astype(BF)
    o_ref[:, 8:16, :] = ((dk_ref[...] + dk) * SCALE).reshape(GROUP, 8, HD).astype(BF)
    o_ref[:, 16:24, :] = (dv_ref[...] + dv).reshape(GROUP, 8, HD).astype(BF)


def far_grads(*args):
    return pl.pallas_call(
        far_kernel,
        in_specs=[SM] + [VM] * 11,
        out_specs=VM,
        out_shape=jax.ShapeDtypeStruct((GROUP, 24, HD), BF),
        compiler_params=small(),
        name="far_grads",
    )(*args)


def combine_kernel(w_ref, dq_ref, dk_ref, dv_ref, off_ref, oq_ref, ok_ref, ov_ref):
    row = lax.broadcasted_iota(jnp.int32, (PICK, RATE, HD), 1)
    for h in range(HEADS):
        hit = row == off_ref[h:h + 1, :].reshape(1, 1, TOK)
        for part, (src, out) in enumerate(((dq_ref, oq_ref), (dk_ref, ok_ref), (dv_ref, ov_ref))):
            rows = slice(part * 8, (part + 1) * 8)
            w = jnp.concatenate([w_ref[2 * h, rows, :].astype(F32), w_ref[2 * h + 1, rows, :].astype(F32)], axis=0)
            local = src[:, h * HD:(h + 1) * HD].astype(F32).reshape(PICK, RATE, HD)
            total = local + jnp.where(hit, w[:, None, :], 0.0)
            out[0, :, h * HD:(h + 1) * HD] = total.reshape(TOK, HD).astype(BF)


def combine(wide, local):
    shape = jax.ShapeDtypeStruct((1, TOK, HEADS * HD), BF)
    return pl.pallas_call(
        combine_kernel,
        in_specs=[VM] * 5,
        out_specs=[VM] * 3,
        out_shape=[shape, shape, shape],
        compiler_params=small(),
        name="combine",
    )(wide, *local)


def place_of(z, x, c):
    return (z * NX + x) * NC + c


def column(half, place):
    return place if half == 0 else NX - 1 - place


GROUPS = [
    [place_of(z, column(half, p), c) for z in reversed(range(NZ)) for p in range(2) for c in range(NC)]
    for half in range(2)
]


def move(value, route):
    count, seats = lax.axis_size("section"), lax.axis_size("seq")
    pairs = []
    for s in range(count):
        for z in range(NZ):
            for x in range(NX):
                for c in range(NC):
                    target = route(s, x, c)
                    if target is not None:
                        ts, tx, tc = target
                        pairs.append((s * seats + place_of(z, x, c), (ts % count) * seats + place_of(z, tx, tc)))
    return lax.ppermute(value, ("section", "seq"), pairs)


def swap(value):
    return lax.all_to_all(value, "seq", 0, 0, axis_index_groups=GROUPS, tiled=True)


def body(queries, key_rows, value_rows, grad_out, log_sums, deltas, offsets):
    seat = lax.axis_index("seq").astype(jnp.int32)
    x = seat // NC % NX
    core = (seat % NC).reshape(1)
    pos = ((NZ - 1 - seat // (NX * NC)) * 4 + jnp.where(x < 2, x, NX - 1 - x) * 2 + seat % NC).reshape(1)
    picked = pick_all(pos, offsets, log_sums, deltas, queries, key_rows, value_rows, grad_out)
    mine = swap(picked)
    a, b = mine[:, :16], mine[:, MAIN:]
    far_a = move(a, lambda s, x, c: (s, 3 - x, c))
    far_b = move(b, lambda s, x, c: (s - c, 3 - x, c))
    hop = move(b, lambda s, x, c: (s - 1, x, 1) if c == 1 else None)
    cross = move(b, lambda s, x, c: (s - c, x, 1 - c))
    st = gather_stats(mine)
    far_st = move(st, lambda s, x, c: (s, 3 - x, c))
    other_a = move(a, lambda s, x, c: (s, x, 1 - c))
    other_st = move(st, lambda s, x, c: (s, x, 1 - c))
    grad = move(grad_out, lambda s, x, c: (s - 1, x, c))
    other_far_st = move(far_st, lambda s, x, c: (s, x, 1 - c))
    other_far_a = move(far_a, lambda s, x, c: (s, x, 1 - c))
    other_far_b = move(far_b, lambda s, x, c: (s, x, 1 - c))
    local = local_grads(offsets, queries, key_rows, value_rows, grad, log_sums, deltas)
    part = near_grads(core, a, b, st, other_a, other_st, hop, cross)
    back = swap(far_grads(core, far_a, far_b, far_st, other_far_a, other_far_b, other_far_st, *part))
    return tuple(combine(back, local))


def solution(mesh):
    rows = P("section", "seq", None)
    stats = P("section", None, "seq")
    return jax.shard_map(
        body,
        mesh=mesh,
        in_specs=(rows, rows, rows, rows, stats, stats, P("seq", None)),
        out_specs=(rows, rows, rows),
        check_vma=False,
    )
```

```python
import jax
import jax.numpy as jnp
from jax import lax
from jax.experimental import pallas as pl
from jax.experimental.pallas import tpu as pltpu
from jax.sharding import PartitionSpec as P


HEADS = 16
HD = 128
PICK = 16
RATE = 8
TOK = 128
NZ, NX, NC = 8, 4, 2
ROWS = 40
MAIN = 24
GROUP = 32
HALF = GROUP * PICK // 2
SCALE = HD ** (-0.5)
BF = jnp.bfloat16
F32 = jnp.float32

VM = pl.BlockSpec(memory_space=pltpu.VMEM)
SM = pl.BlockSpec(memory_space=pltpu.SMEM)


def dot(a, b):
    return lax.dot_general(a, b, (((1,), (0,)), ((), ())), preferred_element_type=F32)


def dot_t(a, b):
    return lax.dot_general(a, b, (((1,), (1,)), ((), ())), preferred_element_type=F32)


def dot_l(a, b):
    return lax.dot_general(a, b, (((0,), (0,)), ((), ())), preferred_element_type=F32)


def chooser(off):
    row = lax.broadcasted_iota(jnp.int32, (PICK, TOK), 0)
    tok = lax.broadcasted_iota(jnp.int32, (PICK, TOK), 1)
    return jnp.where(tok == row * RATE + off, 1.0, 0.0).astype(BF)


def small(mib=12):
    return pltpu.CompilerParams(vmem_limit_bytes=mib << 20)


def pick_kernel(pos_ref, off_hbm, l_hbm, d_hbm, q_hbm, k_hbm, v_hbm, g_hbm, o_ref, off_ref, l_ref, d_ref, x_ref, sems):
    loads = [
        pltpu.make_async_copy(src, dst, sems.at[i])
        for i, (src, dst) in enumerate(
            (
                (off_hbm, off_ref),
                (q_hbm.at[0], x_ref.at[0]),
                (k_hbm.at[0], x_ref.at[1]),
                (v_hbm.at[0], x_ref.at[2]),
                (g_hbm.at[0], x_ref.at[3]),
                (l_hbm.at[0], l_ref),
                (d_hbm.at[0], d_ref),
            )
        )
    ]
    for load in loads:
        load.start()
    n = pos_ref[0]
    src = lax.broadcasted_iota(jnp.int32, (TOK, TOK), 0)
    dst = lax.broadcasted_iota(jnp.int32, (TOK, TOK), 1)
    place = jnp.where(dst == (n % 8) * PICK + src // RATE, 1.0, 0.0).astype(BF)
    loads[0].wait()
    choose = [chooser(off_ref[0, h]) for h in range(HEADS)]
    for part, core, first in ((0, 0, 0), (1, 0, MAIN), (2, 1, 0), (3, 1, MAIN)):
        loads[1 + part].wait()
        for h in range(HEADS):
            rows = dot(choose[h], x_ref[part, :, h * HD:(h + 1) * HD])
            o_ref[2 * h + core, first:first + 16] = rows.astype(BF)
    loads[5].wait()
    loads[6].wait()
    head = lax.broadcasted_iota(jnp.int32, (HEADS, TOK), 0)
    lane = lax.broadcasted_iota(jnp.int32, (HEADS, TOK), 1)
    off = jnp.zeros((HEADS, TOK), jnp.int32)
    for h in range(HEADS):
        off = jnp.where(head == h, off_ref[0, h], off)
    hit = (lane % RATE) == off
    lses = dot(jnp.where(hit, l_ref[...].astype(F32), 0.0).astype(BF), place)
    dlts = dot(jnp.where(hit, d_ref[...].astype(F32), 0.0).astype(BF), place)
    row = lax.broadcasted_iota(jnp.int32, (8, HD), 0)
    for h in range(HEADS):
        lse = jnp.broadcast_to(lses[h:h + 1], (8, HD))
        dlt = jnp.broadcast_to(dlts[h:h + 1], (8, HD))
        stats = jnp.where(row == n // 8, lse, jnp.where(row == 4 + n // 8, dlt, 0.0))
        o_ref[2 * h, 16:MAIN] = stats.astype(BF)
        o_ref[2 * h + 1, 16:MAIN] = jnp.zeros((8, HD), BF)


def pick_all(pos, offsets, lse, delta, query, key, value, grad):
    raw = pl.BlockSpec(memory_space=pltpu.HBM)
    return pl.pallas_call(
        pick_kernel,
        in_specs=[SM] + [raw] * 7,
        out_specs=VM,
        out_shape=jax.ShapeDtypeStruct((GROUP, ROWS, HD), BF),
        scratch_shapes=[
            pltpu.SMEM((1, HEADS), jnp.int32),
            pltpu.VMEM((HEADS, TOK), BF),
            pltpu.VMEM((HEADS, TOK), BF),
            pltpu.VMEM((4, TOK, HEADS * HD), BF),
            pltpu.SemaphoreType.DMA((7,)),
        ],
        name="pick_all",
    )(pos, offsets, lse, delta, query, key, value, grad)


def score_kernel(off_ref, q_ref, k_ref, l_ref, p_ref, offs_ref, st_ref):
    step = pl.program_id(0)

    @pl.when(step == 0)
    def _():
        st_ref[...] = l_ref[0].astype(F32)
        for h in range(HEADS):
            offs_ref[h:h + 1, :] = jnp.full((1, TOK), off_ref[0, h], jnp.int32)

    lses = st_ref[pl.ds(pl.multiple_of(step * 4, 4), 4), :]
    for i in range(4):
        cols = slice(i * HD, (i + 1) * HD)
        p_ref[i] = jnp.exp(dot_t(k_ref[0, :, cols], q_ref[0, :, cols]) * SCALE - lses[i:i + 1])


def local_scores(offsets, query, key, lse):
    wide = pl.BlockSpec((1, TOK, 4 * HD), lambda i: (0, 0, i))
    stat = pl.BlockSpec((1, HEADS, TOK), lambda i: (0, 0, 0))
    return pl.pallas_call(
        score_kernel,
        grid=(4,),
        in_specs=[SM, wide, wide, stat],
        out_specs=[pl.BlockSpec((4, TOK, TOK), lambda i: (i, 0, 0)), pl.BlockSpec((HEADS, TOK), lambda i: (0, 0))],
        out_shape=[jax.ShapeDtypeStruct((HEADS, TOK, TOK), F32), jax.ShapeDtypeStruct((HEADS, TOK), jnp.int32)],
        scratch_shapes=[pltpu.VMEM((HEADS, TOK), F32)],
        compiler_params=small(),
        cost_estimate=pl.CostEstimate(flops=16 * 2 * 128 ** 3 * 4, bytes_accessed=2097152, transcendentals=262144),
        name="local_scores",
    )(offsets, query, key, lse)


def local_kernel(p_ref, q_ref, k_ref, v_ref, g_ref, d_ref, dq_ref, dk_ref, dv_ref, st_ref):
    step = pl.program_id(0)

    @pl.when(step == 0)
    def _():
        st_ref[...] = d_ref[0].astype(F32)

    dlts = st_ref[pl.ds(pl.multiple_of(step * 4, 4), 4), :]
    for i in range(4):
        cols = slice(i * HD, (i + 1) * HD)
        q, k, v, g = q_ref[0, :, cols], k_ref[0, :, cols], v_ref[0, :, cols], g_ref[0, :, cols]
        p = p_ref[i]
        ds = (p * (dot_t(v, g) - dlts[i:i + 1])).astype(BF)
        dv_ref[:, cols] = dot(p.astype(BF), g).astype(BF)
        dk_ref[:, cols] = (dot(ds, q) * SCALE).astype(BF)
        dq_ref[:, cols] = (dot_l(ds, k) * SCALE).astype(BF)


def local_grads(probs, query, key, value, grad, delta):
    wide = pl.BlockSpec((1, TOK, 4 * HD), lambda i: (0, 0, i))
    out = pl.BlockSpec((TOK, 4 * HD), lambda i: (0, i))
    stat = pl.BlockSpec((1, HEADS, TOK), lambda i: (0, 0, 0))
    shape = jax.ShapeDtypeStruct((TOK, HEADS * HD), BF)
    return pl.pallas_call(
        local_kernel,
        grid=(4,),
        in_specs=[pl.BlockSpec((4, TOK, TOK), lambda i: (i, 0, 0)), wide, wide, wide, wide, stat],
        out_specs=[out, out, out],
        out_shape=[shape, shape, shape],
        scratch_shapes=[pltpu.VMEM((HEADS, TOK), F32)],
        compiler_params=small(),
        cost_estimate=pl.CostEstimate(flops=16 * 4 * 2 * 128 ** 3 * 4, bytes_accessed=4718592, transcendentals=0),
        name="local_grads",
    )(probs, query, key, value, grad, delta)


def query_side(q, g, k, v, lse, dlt):
    p = jnp.exp(dot_t(q, k) * SCALE - lse)
    ds = (p * (dot_t(g, v) - dlt)).astype(BF)
    return dot(ds, k)


def key_side(k, v, q, g, stats):
    lse = jnp.concatenate([stats[i:i + 1] for i in range(4)], axis=1)
    dlt = jnp.concatenate([stats[i:i + 1] for i in range(4, 8)], axis=1)
    p = jnp.exp(dot_t(k, q) * SCALE - lse)
    ds = (p * (dot_t(v, g) - dlt)).astype(BF)
    return dot(ds, q), dot(p.astype(BF), g)


def flat(rows):
    return rows.reshape(GROUP * PICK, HD)


def whole(core, mine_a, mine_b, other_a, other_b):
    zero = core == 0
    q = jnp.where(zero, mine_a, other_a)
    v = jnp.where(zero, other_a, mine_a)
    k = jnp.where(zero, mine_b, other_b)
    g = jnp.where(zero, other_b, mine_b)
    return flat(q), flat(k), flat(v), flat(g)


def stats_of(core, mine_a, other_a):
    return jnp.sum(jnp.where(core == 0, mine_a[:, 16:MAIN], other_a[:, 16:MAIN]).astype(F32), axis=0)


def share(core, rows):
    width = rows.shape[-1]
    t = rows.astype(F32).reshape(GROUP, 2, 8, width)
    return jnp.where(core == 0, t[:, 0], t[:, 1]).reshape(HALF, width)


def near_kernel(core_ref, a_ref, b_ref, oa_ref, hop_ref, cross_ref, sub_ref, col_ref, dq_ref, dk_ref, dv_ref):
    core = core_ref[0]
    mine_b = jnp.where(core == 0, b_ref[...], hop_ref[...])
    q, k, v, g = whole(core, a_ref[:, 0:16], mine_b, oa_ref[:, 0:16], cross_ref[...])
    stats = stats_of(core, a_ref, oa_ref)
    turned = jnp.transpose(jnp.concatenate([stats, jnp.zeros((HD - 8, HD), F32)], axis=0))
    lse = share(core, jnp.concatenate([turned[:, i:i + 1] for i in range(4)], axis=0))
    dlt = share(core, jnp.concatenate([turned[:, i:i + 1] for i in range(4, 8)], axis=0))
    sq, sk, sv, sg = (share(core, rows).astype(BF) for rows in (q, k, v, g))
    for i, rows in enumerate((sq, sk, sv, sg)):
        sub_ref[i] = rows
    lane = lax.broadcasted_iota(jnp.int32, (HALF, HD), 1)
    col_ref[...] = jnp.where(lane == 0, lse, dlt)
    dq_ref[...] = query_side(sq, sg, k, v, lse, dlt)
    dk_ref[...], dv_ref[...] = key_side(sk, sv, q, g, stats)


def near_grads(*args):
    part = jax.ShapeDtypeStruct((HALF, HD), F32)
    return pl.pallas_call(
        near_kernel,
        in_specs=[SM] + [VM] * 5,
        out_specs=[VM] * 5,
        out_shape=[jax.ShapeDtypeStruct((4, HALF, HD), BF)] + [part] * 4,
        compiler_params=small(),
        cost_estimate=pl.CostEstimate(flops=14 * 2 * 256 * 256 * 128 * 2, bytes_accessed=1572864, transcendentals=262144),
        name="near_grads",
    )(*args)


def far_kernel(core_ref, a_ref, b_ref, oa_ref, ob_ref, sub_ref, col_ref, dq_ref, dk_ref, dv_ref, o_ref):
    core = core_ref[0]
    q, k, v, g = whole(core, a_ref[:, 0:16], b_ref[...], oa_ref[:, 0:16], ob_ref[...])
    stats = stats_of(core, a_ref, oa_ref)
    lse, dlt = col_ref[:, 0:1], col_ref[:, 1:2]
    dq = dq_ref[...] + query_side(sub_ref[0], sub_ref[3], k, v, lse, dlt)
    dk, dv = key_side(sub_ref[1], sub_ref[2], q, g, stats)
    o_ref[:, 0:8, :] = (dq * SCALE).reshape(GROUP, 8, HD).astype(BF)
    o_ref[:, 8:16, :] = ((dk_ref[...] + dk) * SCALE).reshape(GROUP, 8, HD).astype(BF)
    o_ref[:, 16:24, :] = (dv_ref[...] + dv).reshape(GROUP, 8, HD).astype(BF)


def far_grads(*args):
    return pl.pallas_call(
        far_kernel,
        in_specs=[SM] + [VM] * 9,
        out_specs=VM,
        out_shape=jax.ShapeDtypeStruct((GROUP, 24, HD), BF),
        compiler_params=small(),
        name="far_grads",
    )(*args)


def combine_kernel(w_ref, dq_ref, dk_ref, dv_ref, off_ref, oq_ref, ok_ref, ov_ref):
    row = lax.broadcasted_iota(jnp.int32, (PICK, RATE, HD), 1)
    for h in range(HEADS):
        hit = row == off_ref[h:h + 1, :].reshape(1, 1, TOK)
        for part, (src, out) in enumerate(((dq_ref, oq_ref), (dk_ref, ok_ref), (dv_ref, ov_ref))):
            rows = slice(part * 8, (part + 1) * 8)
            w = jnp.concatenate([w_ref[2 * h, rows, :].astype(F32), w_ref[2 * h + 1, rows, :].astype(F32)], axis=0)
            local = src[:, h * HD:(h + 1) * HD].astype(F32).reshape(PICK, RATE, HD)
            total = local + jnp.where(hit, w[:, None, :], 0.0)
            out[0, :, h * HD:(h + 1) * HD] = total.reshape(TOK, HD).astype(BF)


def combine(wide, local):
    shape = jax.ShapeDtypeStruct((1, TOK, HEADS * HD), BF)
    return pl.pallas_call(
        combine_kernel,
        in_specs=[VM] * 5,
        out_specs=[VM] * 3,
        out_shape=[shape, shape, shape],
        compiler_params=small(),
        name="combine",
    )(wide, *local)


def place_of(z, x, c):
    return (z * NX + x) * NC + c


def column(half, place):
    return place if half == 0 else NX - 1 - place


GROUPS = [
    [place_of(z, column(half, p), c) for z in reversed(range(NZ)) for p in range(2) for c in range(NC)]
    for half in range(2)
]


def move(value, route):
    count, seats = lax.axis_size("section"), lax.axis_size("seq")
    pairs = []
    for s in range(count):
        for z in range(NZ):
            for x in range(NX):
                for c in range(NC):
                    target = route(s, x, c)
                    if target is not None:
                        ts, tx, tc = target
                        pairs.append((s * seats + place_of(z, x, c), (ts % count) * seats + place_of(z, tx, tc)))
    return lax.ppermute(value, ("section", "seq"), pairs)


def swap(value):
    return lax.all_to_all(value, "seq", 0, 0, axis_index_groups=GROUPS, tiled=True)


def body(queries, key_rows, value_rows, grad_out, log_sums, deltas, offsets):
    seat = lax.axis_index("seq").astype(jnp.int32)
    x = seat // NC % NX
    core = (seat % NC).reshape(1)
    pos = ((NZ - 1 - seat // (NX * NC)) * 4 + jnp.where(x < 2, x, NX - 1 - x) * 2 + seat % NC).reshape(1)
    picked = pick_all(pos, offsets, log_sums, deltas, queries, key_rows, value_rows, grad_out)
    mine = swap(picked)
    grad = move(grad_out, lambda s, x, c: (s - 1, x, c))
    probs, offs = local_scores(offsets, queries, key_rows, log_sums)
    a, b = mine[:, :MAIN], mine[:, MAIN:]
    far_a = move(a, lambda s, x, c: (s, 3 - x, c))
    far_b = move(b, lambda s, x, c: (s - c, 3 - x, c))
    other_a = move(a, lambda s, x, c: (s, x, 1 - c))
    hop = move(b, lambda s, x, c: (s - 1, x, 1) if c == 1 else None)
    cross = move(b, lambda s, x, c: (s - c, x, 1 - c))
    other_far_a = move(far_a, lambda s, x, c: (s, x, 1 - c))
    other_far_b = move(far_b, lambda s, x, c: (s, x, 1 - c))
    local = local_grads(probs, queries, key_rows, value_rows, grad, deltas)
    part = near_grads(core, a, b, other_a, hop, cross)
    back = swap(far_grads(core, far_a, far_b, other_far_a, other_far_b, *part))
    return tuple(combine(back, (*local, offs)))


def solution(mesh):
    rows = P("section", "seq", None)
    stats = P("section", None, "seq")
    return jax.shard_map(
        body,
        mesh=mesh,
        in_specs=(rows, rows, rows, rows, stats, stats, P("seq", None)),
        out_specs=(rows, rows, rows),
        check_vma=False,
    )
```

```python
import jax
import jax.numpy as jnp
from jax import lax
from jax.experimental import pallas as pl
from jax.experimental.pallas import tpu as pltpu
from jax.sharding import PartitionSpec as P


HEADS = 16
HD = 128
PICK = 16
RATE = 8
TOK = 128
NZ, NX, NC = 8, 4, 2
ROWS = 40
MAIN = 24
GROUP = 32
HALF = GROUP * PICK // 2
SCALE = HD ** (-0.5)
BF = jnp.bfloat16
F32 = jnp.float32

VM = pl.BlockSpec(memory_space=pltpu.VMEM)
SM = pl.BlockSpec(memory_space=pltpu.SMEM)


def dot(a, b):
    return lax.dot_general(a, b, (((1,), (0,)), ((), ())), preferred_element_type=F32)


def dot_t(a, b):
    return lax.dot_general(a, b, (((1,), (1,)), ((), ())), preferred_element_type=F32)


def dot_l(a, b):
    return lax.dot_general(a, b, (((0,), (0,)), ((), ())), preferred_element_type=F32)


def chooser(off):
    row = lax.broadcasted_iota(jnp.int32, (PICK, TOK), 0)
    tok = lax.broadcasted_iota(jnp.int32, (PICK, TOK), 1)
    return jnp.where(tok == row * RATE + off, 1.0, 0.0).astype(BF)


def small(mib=12):
    return pltpu.CompilerParams(vmem_limit_bytes=mib << 20)


def pick_kernel(pos_ref, off_hbm, l_hbm, d_hbm, q_hbm, k_hbm, v_hbm, g_hbm, o_hbm, off_ref, l_ref, d_ref, x_ref, o_ref, sems, load_sems, store_sems):
    small_loads = [
        pltpu.make_async_copy(src, dst, sems.at[i])
        for i, (src, dst) in enumerate(((off_hbm, off_ref), (l_hbm.at[0], l_ref), (d_hbm.at[0], d_ref)))
    ]
    for load in small_loads:
        load.start()
    loads = []
    for group in range(4):
        cols = pl.ds(group * 4 * HD, 4 * HD)
        for part, src in enumerate((q_hbm, k_hbm, v_hbm, g_hbm)):
            load = pltpu.make_async_copy(src.at[0, :, cols], x_ref.at[part, :, cols], load_sems.at[group, part])
            load.start()
            loads.append(load)
    n = pos_ref[0]
    src = lax.broadcasted_iota(jnp.int32, (TOK, TOK), 0)
    dst = lax.broadcasted_iota(jnp.int32, (TOK, TOK), 1)
    place = jnp.where(dst == (n % 8) * PICK + src // RATE, 1.0, 0.0).astype(BF)
    for load in small_loads:
        load.wait()
    head = lax.broadcasted_iota(jnp.int32, (HEADS, TOK), 0)
    lane = lax.broadcasted_iota(jnp.int32, (HEADS, TOK), 1)
    off = jnp.zeros((HEADS, TOK), jnp.int32)
    for h in range(HEADS):
        off = jnp.where(head == h, off_ref[0, h], off)
    hit = (lane % RATE) == off
    lses = dot(jnp.where(hit, l_ref[...].astype(F32), 0.0).astype(BF), place)
    dlts = dot(jnp.where(hit, d_ref[...].astype(F32), 0.0).astype(BF), place)
    row = lax.broadcasted_iota(jnp.int32, (8, HD), 0)
    stores = []
    for group in range(4):
        for load in loads[4 * group:4 * group + 4]:
            load.wait()
        for h in range(4 * group, 4 * group + 4):
            choose = chooser(off_ref[0, h])
            for part, core, first in ((0, 0, 0), (1, 0, MAIN), (2, 1, 0), (3, 1, MAIN)):
                rows = dot(choose, x_ref[part, :, h * HD:(h + 1) * HD])
                o_ref[2 * h + core, first:first + 16] = rows.astype(BF)
            lse = jnp.broadcast_to(lses[h:h + 1], (8, HD))
            dlt = jnp.broadcast_to(dlts[h:h + 1], (8, HD))
            stats = jnp.where(row == n // 8, lse, jnp.where(row == 4 + n // 8, dlt, 0.0))
            o_ref[2 * h, 16:MAIN] = stats.astype(BF)
            o_ref[2 * h + 1, 16:MAIN] = jnp.zeros((8, HD), BF)
        out = pl.ds(8 * group, 8)
        store = pltpu.make_async_copy(o_ref.at[out], o_hbm.at[out], store_sems.at[group])
        store.start()
        stores.append(store)
    for store in stores:
        store.wait()


def pick_all(pos, offsets, lse, delta, query, key, value, grad):
    raw = pl.BlockSpec(memory_space=pltpu.HBM)
    return pl.pallas_call(
        pick_kernel,
        in_specs=[SM] + [raw] * 7,
        out_specs=raw,
        out_shape=jax.ShapeDtypeStruct((GROUP, ROWS, HD), BF),
        scratch_shapes=[
            pltpu.SMEM((1, HEADS), jnp.int32),
            pltpu.VMEM((HEADS, TOK), BF),
            pltpu.VMEM((HEADS, TOK), BF),
            pltpu.VMEM((4, TOK, HEADS * HD), BF),
            pltpu.VMEM((GROUP, ROWS, HD), BF),
            pltpu.SemaphoreType.DMA((3,)),
            pltpu.SemaphoreType.DMA((4, 4)),
            pltpu.SemaphoreType.DMA((4,)),
        ],
        name="pick_all",
    )(pos, offsets, lse, delta, query, key, value, grad)


def score_kernel(off_ref, q_ref, k_ref, l_ref, p_ref, offs_ref, st_ref):
    step = pl.program_id(0)

    @pl.when(step == 0)
    def _():
        st_ref[...] = l_ref[0].astype(F32)
        for h in range(HEADS):
            offs_ref[h:h + 1, :] = jnp.full((1, TOK), off_ref[0, h], jnp.int32)

    lses = st_ref[pl.ds(pl.multiple_of(step * 4, 4), 4), :]
    for i in range(4):
        cols = slice(i * HD, (i + 1) * HD)
        p_ref[i] = jnp.exp(dot_t(k_ref[0, :, cols], q_ref[0, :, cols]) * SCALE - lses[i:i + 1])


def local_scores(offsets, query, key, lse):
    wide = pl.BlockSpec((1, TOK, 4 * HD), lambda i: (0, 0, i))
    stat = pl.BlockSpec((1, HEADS, TOK), lambda i: (0, 0, 0))
    return pl.pallas_call(
        score_kernel,
        grid=(4,),
        in_specs=[SM, wide, wide, stat],
        out_specs=[pl.BlockSpec((4, TOK, TOK), lambda i: (i, 0, 0)), pl.BlockSpec((HEADS, TOK), lambda i: (0, 0))],
        out_shape=[jax.ShapeDtypeStruct((HEADS, TOK, TOK), F32), jax.ShapeDtypeStruct((HEADS, TOK), jnp.int32)],
        scratch_shapes=[pltpu.VMEM((HEADS, TOK), F32)],
        compiler_params=small(),
        cost_estimate=pl.CostEstimate(flops=16 * 2 * 128 ** 3 * 4, bytes_accessed=2097152, transcendentals=262144),
        name="local_scores",
    )(offsets, query, key, lse)


def local_kernel(p_ref, q_ref, k_ref, v_ref, g_ref, d_ref, dq_ref, dk_ref, dv_ref, st_ref):
    step = pl.program_id(0)

    @pl.when(step == 0)
    def _():
        st_ref[...] = d_ref[0].astype(F32)

    dlts = st_ref[pl.ds(pl.multiple_of(step * 4, 4), 4), :]
    for i in range(4):
        cols = slice(i * HD, (i + 1) * HD)
        q, k, v, g = q_ref[0, :, cols], k_ref[0, :, cols], v_ref[0, :, cols], g_ref[0, :, cols]
        p = p_ref[i]
        ds = (p * (dot_t(v, g) - dlts[i:i + 1])).astype(BF)
        dv_ref[:, cols] = dot(p.astype(BF), g).astype(BF)
        dk_ref[:, cols] = (dot(ds, q) * SCALE).astype(BF)
        dq_ref[:, cols] = (dot_l(ds, k) * SCALE).astype(BF)


def local_grads(probs, query, key, value, grad, delta):
    wide = pl.BlockSpec((1, TOK, 4 * HD), lambda i: (0, 0, i))
    out = pl.BlockSpec((TOK, 4 * HD), lambda i: (0, i))
    stat = pl.BlockSpec((1, HEADS, TOK), lambda i: (0, 0, 0))
    shape = jax.ShapeDtypeStruct((TOK, HEADS * HD), BF)
    return pl.pallas_call(
        local_kernel,
        grid=(4,),
        in_specs=[pl.BlockSpec((4, TOK, TOK), lambda i: (i, 0, 0)), wide, wide, wide, wide, stat],
        out_specs=[out, out, out],
        out_shape=[shape, shape, shape],
        scratch_shapes=[pltpu.VMEM((HEADS, TOK), F32)],
        compiler_params=small(),
        cost_estimate=pl.CostEstimate(flops=16 * 4 * 2 * 128 ** 3 * 4, bytes_accessed=4718592, transcendentals=0),
        name="local_grads",
    )(probs, query, key, value, grad, delta)


def query_side(q, g, k, v, lse, dlt):
    p = jnp.exp(dot_t(q, k) * SCALE - lse)
    ds = (p * (dot_t(g, v) - dlt)).astype(BF)
    return dot(ds, k)


def key_side(k, v, q, g, stats):
    lse = jnp.concatenate([stats[i:i + 1] for i in range(4)], axis=1)
    dlt = jnp.concatenate([stats[i:i + 1] for i in range(4, 8)], axis=1)
    p = jnp.exp(dot_t(k, q) * SCALE - lse)
    ds = (p * (dot_t(v, g) - dlt)).astype(BF)
    return dot(ds, q), dot(p.astype(BF), g)


def flat(rows):
    return rows.reshape(GROUP * PICK, HD)


def whole(core, mine_a, mine_b, other_a, other_b):
    zero = core == 0
    q = jnp.where(zero, mine_a, other_a)
    v = jnp.where(zero, other_a, mine_a)
    k = jnp.where(zero, mine_b, other_b)
    g = jnp.where(zero, other_b, mine_b)
    return flat(q), flat(k), flat(v), flat(g)


def stats_of(core, mine_a, other_a):
    return jnp.sum(jnp.where(core == 0, mine_a[:, 16:MAIN], other_a[:, 16:MAIN]).astype(F32), axis=0)


def share(core, rows):
    width = rows.shape[-1]
    t = rows.astype(F32).reshape(GROUP, 2, 8, width)
    return jnp.where(core == 0, t[:, 0], t[:, 1]).reshape(HALF, width)


def near_kernel(core_ref, a_ref, b_ref, oa_ref, hop_ref, cross_ref, sub_ref, col_ref, dq_ref, dk_ref, dv_ref):
    core = core_ref[0]
    mine_b = jnp.where(core == 0, b_ref[...], hop_ref[...])
    q, k, v, g = whole(core, a_ref[:, 0:16], mine_b, oa_ref[:, 0:16], cross_ref[...])
    stats = stats_of(core, a_ref, oa_ref)
    turned = jnp.transpose(jnp.concatenate([stats, jnp.zeros((HD - 8, HD), F32)], axis=0))
    lse = share(core, jnp.concatenate([turned[:, i:i + 1] for i in range(4)], axis=0))
    dlt = share(core, jnp.concatenate([turned[:, i:i + 1] for i in range(4, 8)], axis=0))
    sq, sk, sv, sg = (share(core, rows).astype(BF) for rows in (q, k, v, g))
    for i, rows in enumerate((sq, sk, sv, sg)):
        sub_ref[i] = rows
    lane = lax.broadcasted_iota(jnp.int32, (HALF, HD), 1)
    col_ref[...] = jnp.where(lane == 0, lse, dlt)
    dq_ref[...] = query_side(sq, sg, k, v, lse, dlt)
    dk_ref[...], dv_ref[...] = key_side(sk, sv, q, g, stats)


def near_grads(*args):
    part = jax.ShapeDtypeStruct((HALF, HD), F32)
    return pl.pallas_call(
        near_kernel,
        in_specs=[SM] + [VM] * 5,
        out_specs=[VM] * 5,
        out_shape=[jax.ShapeDtypeStruct((4, HALF, HD), BF)] + [part] * 4,
        compiler_params=small(),
        cost_estimate=pl.CostEstimate(flops=14 * 2 * 256 * 256 * 128 * 2, bytes_accessed=1572864, transcendentals=262144),
        name="near_grads",
    )(*args)


def far_kernel(core_ref, a_ref, b_ref, oa_ref, ob_ref, sub_ref, col_ref, dq_ref, dk_ref, dv_ref, o_ref):
    core = core_ref[0]
    q, k, v, g = whole(core, a_ref[:, 0:16], b_ref[...], oa_ref[:, 0:16], ob_ref[...])
    stats = stats_of(core, a_ref, oa_ref)
    lse, dlt = col_ref[:, 0:1], col_ref[:, 1:2]
    dq = dq_ref[...] + query_side(sub_ref[0], sub_ref[3], k, v, lse, dlt)
    dk, dv = key_side(sub_ref[1], sub_ref[2], q, g, stats)
    parts = (dq * SCALE, (dk_ref[...] + dk) * SCALE, dv_ref[...] + dv)
    for i, part in enumerate(parts):
        rows = part.reshape(GROUP, 8, HD).astype(BF)
        for to, z in enumerate(OUT_ORDER):
            at = IN_ORDER.index(z) * 4
            o_ref[4 * to:4 * to + 4, 8 * i:8 * i + 8, :] = rows[at:at + 4]


def far_grads(*args):
    return pl.pallas_call(
        far_kernel,
        in_specs=[SM] + [VM] * 9,
        out_specs=VM,
        out_shape=jax.ShapeDtypeStruct((GROUP, 24, HD), BF),
        compiler_params=small(),
        name="far_grads",
    )(*args)


def combine_kernel(w_ref, dq_ref, dk_ref, dv_ref, off_ref, oq_hbm, ok_hbm, ov_hbm, out_ref, sems):
    row = lax.broadcasted_iota(jnp.int32, (PICK, RATE, HD), 1)
    stores = []
    for group in range(4):
        for h in range(4 * group, 4 * group + 4):
            hit = row == off_ref[h:h + 1, :].reshape(1, 1, TOK)
            first = OUT_ORDER.index(IN_ORDER[h // 2]) * 4 + h % 2 * 2
            for part, src in enumerate((dq_ref, dk_ref, dv_ref)):
                rows = slice(part * 8, (part + 1) * 8)
                w = jnp.concatenate([w_ref[first, rows, :].astype(F32), w_ref[first + 1, rows, :].astype(F32)], axis=0)
                local = src[:, h * HD:(h + 1) * HD].astype(F32).reshape(PICK, RATE, HD)
                total = local + jnp.where(hit, w[:, None, :], 0.0)
                out_ref[part, :, h * HD:(h + 1) * HD] = total.reshape(TOK, HD).astype(BF)
        cols = pl.ds(group * 4 * HD, 4 * HD)
        for part, dst in enumerate((oq_hbm, ok_hbm, ov_hbm)):
            store = pltpu.make_async_copy(out_ref.at[part, :, cols], dst.at[0, :, cols], sems.at[group, part])
            store.start()
            stores.append(store)
    for store in stores:
        store.wait()


def combine(wide, local):
    shape = jax.ShapeDtypeStruct((1, TOK, HEADS * HD), BF)
    return pl.pallas_call(
        combine_kernel,
        in_specs=[VM] * 5,
        out_specs=[pl.BlockSpec(memory_space=pltpu.HBM)] * 3,
        out_shape=[shape, shape, shape],
        scratch_shapes=[pltpu.VMEM((3, TOK, HEADS * HD), BF), pltpu.SemaphoreType.DMA((4, 3))],
        compiler_params=small(),
        name="combine",
    )(wide, *local)


def place_of(z, x, c):
    return (z * NX + x) * NC + c


def column(half, place):
    return place if half == 0 else NX - 1 - place


def groups_of(order):
    return [[place_of(z, column(half, p), c) for z in order for p in range(2) for c in range(NC)] for half in range(2)]


IN_ORDER = (7, 6, 5, 4, 3, 2, 1, 0)
OUT_ORDER = (7, 6, 5, 4, 0, 1, 2, 3)


def move(value, route):
    count, seats = lax.axis_size("section"), lax.axis_size("seq")
    pairs = []
    for s in range(count):
        for z in range(NZ):
            for x in range(NX):
                for c in range(NC):
                    target = route(s, x, c)
                    if target is not None:
                        ts, tx, tc = target
                        pairs.append((s * seats + place_of(z, x, c), (ts % count) * seats + place_of(z, tx, tc)))
    return lax.ppermute(value, ("section", "seq"), pairs)


def swap(value, order):
    return lax.all_to_all(value, "seq", 0, 0, axis_index_groups=groups_of(order), tiled=True)


def body(queries, key_rows, value_rows, grad_out, log_sums, deltas, offsets):
    seat = lax.axis_index("seq").astype(jnp.int32)
    x = seat // NC % NX
    core = (seat % NC).reshape(1)
    pos = ((NZ - 1 - seat // (NX * NC)) * 4 + jnp.where(x < 2, x, NX - 1 - x) * 2 + seat % NC).reshape(1)
    picked = pick_all(pos, offsets, log_sums, deltas, queries, key_rows, value_rows, grad_out)
    mine = swap(picked, IN_ORDER)
    grad = move(grad_out, lambda s, x, c: (s - 1, x, c))
    probs, offs = local_scores(offsets, queries, key_rows, log_sums)
    a, b = mine[:, :MAIN], mine[:, MAIN:]
    far_a = move(a, lambda s, x, c: (s, 3 - x, c))
    far_b = move(b, lambda s, x, c: (s - c, 3 - x, c))
    other_a = move(a, lambda s, x, c: (s, x, 1 - c))
    hop = move(b, lambda s, x, c: (s - 1, x, 1) if c == 1 else None)
    cross = move(b, lambda s, x, c: (s - c, x, 1 - c))
    other_far_a = move(far_a, lambda s, x, c: (s, x, 1 - c))
    other_far_b = move(far_b, lambda s, x, c: (s, x, 1 - c))
    local = local_grads(probs, queries, key_rows, value_rows, grad, deltas)
    part = near_grads(core, a, b, other_a, hop, cross)
    back = swap(far_grads(core, far_a, far_b, other_far_a, other_far_b, *part), OUT_ORDER)
    return tuple(combine(back, (*local, offs)))


def solution(mesh):
    rows = P("section", "seq", None)
    stats = P("section", None, "seq")
    return jax.shard_map(
        body,
        mesh=mesh,
        in_specs=(rows, rows, rows, rows, stats, stats, P("seq", None)),
        out_specs=(rows, rows, rows),
        check_vma=False,
    )
```

```python
import jax
import jax.numpy as jnp
from jax import lax
from jax.experimental import pallas as pl
from jax.experimental.pallas import tpu as pltpu
from jax.sharding import PartitionSpec as P


HEADS = 16
HD = 128
PICK = 16
RATE = 8
TOK = 128
NZ, NX, NC = 8, 4, 2
ROWS = 40
MAIN = 24
GROUP = 32
HALF = GROUP * PICK // 2
SCALE = HD ** (-0.5)
BF = jnp.bfloat16
F32 = jnp.float32

VM = pl.BlockSpec(memory_space=pltpu.VMEM)
SM = pl.BlockSpec(memory_space=pltpu.SMEM)


def dot(a, b):
    return lax.dot_general(a, b, (((1,), (0,)), ((), ())), preferred_element_type=F32)


def dot_t(a, b):
    return lax.dot_general(a, b, (((1,), (1,)), ((), ())), preferred_element_type=F32)


def dot_l(a, b):
    return lax.dot_general(a, b, (((0,), (0,)), ((), ())), preferred_element_type=F32)


def chooser(off):
    row = lax.broadcasted_iota(jnp.int32, (PICK, TOK), 0)
    tok = lax.broadcasted_iota(jnp.int32, (PICK, TOK), 1)
    return jnp.where(tok == row * RATE + off, 1.0, 0.0).astype(BF)


def small(mib=12):
    return pltpu.CompilerParams(vmem_limit_bytes=mib << 20)


def pick_kernel(pos_ref, off_hbm, l_hbm, d_hbm, q_hbm, k_hbm, v_hbm, g_hbm, o_ref, off_ref, l_ref, d_ref, x_ref, sems):
    loads = [
        pltpu.make_async_copy(src, dst, sems.at[i])
        for i, (src, dst) in enumerate(
            (
                (off_hbm, off_ref),
                (q_hbm.at[0], x_ref.at[0]),
                (k_hbm.at[0], x_ref.at[1]),
                (v_hbm.at[0], x_ref.at[2]),
                (g_hbm.at[0], x_ref.at[3]),
                (l_hbm.at[0], l_ref),
                (d_hbm.at[0], d_ref),
            )
        )
    ]
    for load in loads:
        load.start()
    n = pos_ref[0]
    src = lax.broadcasted_iota(jnp.int32, (TOK, TOK), 0)
    dst = lax.broadcasted_iota(jnp.int32, (TOK, TOK), 1)
    place = jnp.where(dst == (n % 8) * PICK + src // RATE, 1.0, 0.0).astype(BF)
    loads[0].wait()
    choose = [chooser(off_ref[0, h]) for h in range(HEADS)]
    for part, core, first in ((0, 0, 0), (1, 0, MAIN), (2, 1, 0), (3, 1, MAIN)):
        loads[1 + part].wait()
        for h in range(HEADS):
            rows = dot(choose[h], x_ref[part, :, h * HD:(h + 1) * HD])
            o_ref[2 * h + core, first:first + 16] = rows.astype(BF)
    loads[5].wait()
    loads[6].wait()
    head = lax.broadcasted_iota(jnp.int32, (HEADS, TOK), 0)
    lane = lax.broadcasted_iota(jnp.int32, (HEADS, TOK), 1)
    off = jnp.zeros((HEADS, TOK), jnp.int32)
    for h in range(HEADS):
        off = jnp.where(head == h, off_ref[0, h], off)
    hit = (lane % RATE) == off
    lses = dot(jnp.where(hit, l_ref[...].astype(F32), 0.0).astype(BF), place)
    dlts = dot(jnp.where(hit, d_ref[...].astype(F32), 0.0).astype(BF), place)
    row = lax.broadcasted_iota(jnp.int32, (8, HD), 0)
    for h in range(HEADS):
        lse = jnp.broadcast_to(lses[h:h + 1], (8, HD))
        dlt = jnp.broadcast_to(dlts[h:h + 1], (8, HD))
        stats = jnp.where(row == n // 8, lse, jnp.where(row == 4 + n // 8, dlt, 0.0))
        o_ref[2 * h, 16:MAIN] = stats.astype(BF)
        o_ref[2 * h + 1, 16:MAIN] = jnp.zeros((8, HD), BF)


def pick_all(pos, offsets, lse, delta, query, key, value, grad):
    raw = pl.BlockSpec(memory_space=pltpu.HBM)
    return pl.pallas_call(
        pick_kernel,
        in_specs=[SM] + [raw] * 7,
        out_specs=VM,
        out_shape=jax.ShapeDtypeStruct((GROUP, ROWS, HD), BF),
        scratch_shapes=[
            pltpu.SMEM((1, HEADS), jnp.int32),
            pltpu.VMEM((HEADS, TOK), BF),
            pltpu.VMEM((HEADS, TOK), BF),
            pltpu.VMEM((4, TOK, HEADS * HD), BF),
            pltpu.SemaphoreType.DMA((7,)),
        ],
        name="pick_all",
    )(pos, offsets, lse, delta, query, key, value, grad)


def score_kernel(off_ref, q_ref, k_ref, l_ref, p_ref, offs_ref, st_ref):
    step = pl.program_id(0)

    @pl.when(step == 0)
    def _():
        st_ref[...] = l_ref[0].astype(F32)
        for h in range(HEADS):
            offs_ref[h:h + 1, :] = jnp.full((1, TOK), off_ref[0, h], jnp.int32)

    lses = st_ref[pl.ds(pl.multiple_of(step * 4, 4), 4), :]
    for i in range(4):
        cols = slice(i * HD, (i + 1) * HD)
        p_ref[i] = jnp.exp(dot_t(k_ref[0, :, cols], q_ref[0, :, cols]) * SCALE - lses[i:i + 1])


def local_scores(offsets, query, key, lse):
    wide = pl.BlockSpec((1, TOK, 4 * HD), lambda i: (0, 0, i))
    stat = pl.BlockSpec((1, HEADS, TOK), lambda i: (0, 0, 0))
    return pl.pallas_call(
        score_kernel,
        grid=(4,),
        in_specs=[SM, wide, wide, stat],
        out_specs=[pl.BlockSpec((4, TOK, TOK), lambda i: (i, 0, 0)), pl.BlockSpec((HEADS, TOK), lambda i: (0, 0))],
        out_shape=[jax.ShapeDtypeStruct((HEADS, TOK, TOK), F32), jax.ShapeDtypeStruct((HEADS, TOK), jnp.int32)],
        scratch_shapes=[pltpu.VMEM((HEADS, TOK), F32)],
        compiler_params=small(),
        cost_estimate=pl.CostEstimate(flops=16 * 2 * 128 ** 3 * 4, bytes_accessed=2097152, transcendentals=262144),
        name="local_scores",
    )(offsets, query, key, lse)


def local_kernel(p_ref, q_ref, k_ref, v_ref, g_ref, d_ref, dq_ref, dk_ref, dv_ref, st_ref):
    step = pl.program_id(0)

    @pl.when(step == 0)
    def _():
        st_ref[...] = d_ref[0].astype(F32)

    dlts = st_ref[pl.ds(pl.multiple_of(step * 4, 4), 4), :]
    for i in range(4):
        cols = slice(i * HD, (i + 1) * HD)
        q, k, v, g = q_ref[0, :, cols], k_ref[0, :, cols], v_ref[0, :, cols], g_ref[0, :, cols]
        p = p_ref[i]
        ds = (p * (dot_t(v, g) - dlts[i:i + 1])).astype(BF)
        dv_ref[:, cols] = dot(p.astype(BF), g).astype(BF)
        dk_ref[:, cols] = (dot(ds, q) * SCALE).astype(BF)
        dq_ref[:, cols] = (dot_l(ds, k) * SCALE).astype(BF)


def local_grads(probs, query, key, value, grad, delta):
    wide = pl.BlockSpec((1, TOK, 4 * HD), lambda i: (0, 0, i))
    out = pl.BlockSpec((TOK, 4 * HD), lambda i: (0, i))
    stat = pl.BlockSpec((1, HEADS, TOK), lambda i: (0, 0, 0))
    shape = jax.ShapeDtypeStruct((TOK, HEADS * HD), BF)
    return pl.pallas_call(
        local_kernel,
        grid=(4,),
        in_specs=[pl.BlockSpec((4, TOK, TOK), lambda i: (i, 0, 0)), wide, wide, wide, wide, stat],
        out_specs=[out, out, out],
        out_shape=[shape, shape, shape],
        scratch_shapes=[pltpu.VMEM((HEADS, TOK), F32)],
        compiler_params=small(),
        cost_estimate=pl.CostEstimate(flops=16 * 4 * 2 * 128 ** 3 * 4, bytes_accessed=4718592, transcendentals=0),
        name="local_grads",
    )(probs, query, key, value, grad, delta)


def query_side(q, g, k, v, lse, dlt):
    p = jnp.exp(dot_t(q, k) * SCALE - lse)
    ds = (p * (dot_t(g, v) - dlt)).astype(BF)
    return dot(ds, k)


def key_side(k, v, q, g, stats):
    lse = jnp.concatenate([stats[i:i + 1] for i in range(4)], axis=1)
    dlt = jnp.concatenate([stats[i:i + 1] for i in range(4, 8)], axis=1)
    p = jnp.exp(dot_t(k, q) * SCALE - lse)
    ds = (p * (dot_t(v, g) - dlt)).astype(BF)
    return dot(ds, q), dot(p.astype(BF), g)


def flat(rows):
    return rows.reshape(GROUP * PICK, HD)


def whole(core, mine_a, mine_b, other_a, other_b):
    zero = core == 0
    q = jnp.where(zero, mine_a, other_a)
    v = jnp.where(zero, other_a, mine_a)
    k = jnp.where(zero, mine_b, other_b)
    g = jnp.where(zero, other_b, mine_b)
    return flat(q), flat(k), flat(v), flat(g)


def stats_of(core, mine_a, other_a):
    return jnp.sum(jnp.where(core == 0, mine_a[:, 16:MAIN], other_a[:, 16:MAIN]).astype(F32), axis=0)


def share(core, rows):
    width = rows.shape[-1]
    t = rows.astype(F32).reshape(GROUP, 2, 8, width)
    return jnp.where(core == 0, t[:, 0], t[:, 1]).reshape(HALF, width)


def near_kernel(core_ref, a_ref, b_ref, oa_ref, ob_ref, sub_ref, col_ref, dq_ref, dk_ref, dv_ref):
    core = core_ref[0]
    q, k, v, g = whole(core, a_ref[:, 0:16], b_ref[...], oa_ref[:, 0:16], ob_ref[...])
    stats = stats_of(core, a_ref, oa_ref)
    turned = jnp.transpose(jnp.concatenate([stats, jnp.zeros((HD - 8, HD), F32)], axis=0))
    lse = share(core, jnp.concatenate([turned[:, i:i + 1] for i in range(4)], axis=0))
    dlt = share(core, jnp.concatenate([turned[:, i:i + 1] for i in range(4, 8)], axis=0))
    sq, sk, sv, sg = (share(core, rows).astype(BF) for rows in (q, k, v, g))
    for i, rows in enumerate((sq, sk, sv, sg)):
        sub_ref[i] = rows
    lane = lax.broadcasted_iota(jnp.int32, (HALF, HD), 1)
    col_ref[...] = jnp.where(lane == 0, lse, dlt)
    dq_ref[...] = query_side(sq, sg, k, v, lse, dlt)
    dk_ref[...], dv_ref[...] = key_side(sk, sv, q, g, stats)


def near_grads(*args):
    part = jax.ShapeDtypeStruct((HALF, HD), F32)
    return pl.pallas_call(
        near_kernel,
        in_specs=[SM] + [VM] * 4,
        out_specs=[VM] * 5,
        out_shape=[jax.ShapeDtypeStruct((4, HALF, HD), BF)] + [part] * 4,
        compiler_params=small(),
        cost_estimate=pl.CostEstimate(flops=14 * 2 * 256 * 256 * 128 * 2, bytes_accessed=1572864, transcendentals=262144),
        name="near_grads",
    )(*args)


def far_kernel(core_ref, a_ref, b_ref, oa_ref, ob_ref, sub_ref, col_ref, dq_ref, dk_ref, dv_ref, o_ref):
    core = core_ref[0]
    q, k, v, g = whole(core, a_ref[:, 0:16], b_ref[...], oa_ref[:, 0:16], ob_ref[...])
    stats = stats_of(core, a_ref, oa_ref)
    lse, dlt = col_ref[:, 0:1], col_ref[:, 1:2]
    dq = dq_ref[...] + query_side(sub_ref[0], sub_ref[3], k, v, lse, dlt)
    dk, dv = key_side(sub_ref[1], sub_ref[2], q, g, stats)
    parts = (dq * SCALE, (dk_ref[...] + dk) * SCALE, dv_ref[...] + dv)
    for i, part in enumerate(parts):
        rows = part.reshape(GROUP, 8, HD).astype(BF)
        for to, z in enumerate(OUT_ORDER):
            at = IN_ORDER.index(z) * 4
            o_ref[4 * to:4 * to + 4, 8 * i:8 * i + 8, :] = rows[at:at + 4]


def far_grads(*args):
    return pl.pallas_call(
        far_kernel,
        in_specs=[SM] + [VM] * 9,
        out_specs=VM,
        out_shape=jax.ShapeDtypeStruct((GROUP, 24, HD), BF),
        compiler_params=small(),
        name="far_grads",
    )(*args)


def combine_kernel(w_ref, dq_ref, dk_ref, dv_ref, off_ref, oq_hbm, ok_hbm, ov_hbm, out_ref, sems):
    row = lax.broadcasted_iota(jnp.int32, (PICK, RATE, HD), 1)
    stores = []
    for group in range(4):
        for h in range(4 * group, 4 * group + 4):
            hit = row == off_ref[h:h + 1, :].reshape(1, 1, TOK)
            first = OUT_ORDER.index(IN_ORDER[h // 2]) * 4 + h % 2 * 2
            for part, src in enumerate((dq_ref, dk_ref, dv_ref)):
                rows = slice(part * 8, (part + 1) * 8)
                w = jnp.concatenate([w_ref[first, rows, :].astype(F32), w_ref[first + 1, rows, :].astype(F32)], axis=0)
                local = src[:, h * HD:(h + 1) * HD].astype(F32).reshape(PICK, RATE, HD)
                total = local + jnp.where(hit, w[:, None, :], 0.0)
                out_ref[part, :, h * HD:(h + 1) * HD] = total.reshape(TOK, HD).astype(BF)
        cols = pl.ds(group * 4 * HD, 4 * HD)
        for part, dst in enumerate((oq_hbm, ok_hbm, ov_hbm)):
            store = pltpu.make_async_copy(out_ref.at[part, :, cols], dst.at[0, :, cols], sems.at[group, part])
            store.start()
            stores.append(store)
    for store in stores:
        store.wait()


def combine(wide, local):
    shape = jax.ShapeDtypeStruct((1, TOK, HEADS * HD), BF)
    return pl.pallas_call(
        combine_kernel,
        in_specs=[VM] * 5,
        out_specs=[pl.BlockSpec(memory_space=pltpu.HBM)] * 3,
        out_shape=[shape, shape, shape],
        scratch_shapes=[pltpu.VMEM((3, TOK, HEADS * HD), BF), pltpu.SemaphoreType.DMA((4, 3))],
        compiler_params=small(),
        name="combine",
    )(wide, *local)


def place_of(z, x, c):
    return (z * NX + x) * NC + c


def column(half, place):
    return place if half == 0 else NX - 1 - place


def groups_of(order):
    return [[place_of(z, column(half, p), c) for z in order for p in range(2) for c in range(NC)] for half in range(2)]


IN_ORDER = (5, 4, 3, 2, 1, 0, 7, 6)
OUT_ORDER = IN_ORDER


def move(value, route):
    count, seats = lax.axis_size("section"), lax.axis_size("seq")
    pairs = []
    for s in range(count):
        for z in range(NZ):
            for x in range(NX):
                for c in range(NC):
                    target = route(s, x, c)
                    if target is not None:
                        ts, tx, tc = target
                        pairs.append((s * seats + place_of(z, x, c), (ts % count) * seats + place_of(z, tx, tc)))
    return lax.ppermute(value, ("section", "seq"), pairs)


def swap(value, order):
    return lax.all_to_all(value, "seq", 0, 0, axis_index_groups=groups_of(order), tiled=True)


def body(queries, key_rows, value_rows, grad_out, log_sums, deltas, offsets):
    seat = lax.axis_index("seq").astype(jnp.int32)
    x = seat // NC % NX
    core = (seat % NC).reshape(1)
    z = seat // (NX * NC)
    turn = sum(jnp.where(z == at, i, 0) for i, at in enumerate(IN_ORDER))
    pos = (turn * 4 + jnp.where(x < 2, x, NX - 1 - x) * 2 + seat % NC).reshape(1)
    picked = pick_all(pos, offsets, log_sums, deltas, queries, key_rows, value_rows, grad_out)
    mine = swap(picked, IN_ORDER)
    grad = move(grad_out, lambda s, x, c: (s - 1, x, c))
    probs, offs = local_scores(offsets, queries, key_rows, log_sums)
    a, b = mine[:, :MAIN], mine[:, MAIN:]
    far_a = move(a, lambda s, x, c: (s, 3 - x, c))
    far_b = move(b, lambda s, x, c: (s - c, 3 - x, c))
    other_a = move(a, lambda s, x, c: (s, x, 1 - c))
    own_b = move(b, lambda s, x, c: (s - c, x, c))
    other_b = move(own_b, lambda s, x, c: (s, x, 1 - c))
    other_far_a = move(far_a, lambda s, x, c: (s, x, 1 - c))
    other_far_b = move(far_b, lambda s, x, c: (s, x, 1 - c))
    local = local_grads(probs, queries, key_rows, value_rows, grad, deltas)
    part = near_grads(core, a, own_b, other_a, other_b)
    back = swap(far_grads(core, far_a, far_b, other_far_a, other_far_b, *part), OUT_ORDER)
    return tuple(combine(back, (*local, offs)))


def solution(mesh):
    rows = P("section", "seq", None)
    stats = P("section", None, "seq")
    return jax.shard_map(
        body,
        mesh=mesh,
        in_specs=(rows, rows, rows, rows, stats, stats, P("seq", None)),
        out_specs=(rows, rows, rows),
        check_vma=False,
    )
```

```python
import jax
import jax.numpy as jnp
from jax import lax
from jax.experimental import pallas as pl
from jax.experimental.pallas import tpu as pltpu
from jax.sharding import PartitionSpec as P


HEADS = 16
HD = 128
PICK = 16
RATE = 8
TOK = 128
NZ, NX, NC = 8, 4, 2
ROWS = 40
MAIN = 24
GROUP = 32
HALF = GROUP * PICK // 2
SCALE = HD ** (-0.5)
BF = jnp.bfloat16
F32 = jnp.float32

VM = pl.BlockSpec(memory_space=pltpu.VMEM)
SM = pl.BlockSpec(memory_space=pltpu.SMEM)


def dot(a, b):
    return lax.dot_general(a, b, (((1,), (0,)), ((), ())), preferred_element_type=F32)


def dot_t(a, b):
    return lax.dot_general(a, b, (((1,), (1,)), ((), ())), preferred_element_type=F32)


def dot_l(a, b):
    return lax.dot_general(a, b, (((0,), (0,)), ((), ())), preferred_element_type=F32)


def chooser(off):
    row = lax.broadcasted_iota(jnp.int32, (PICK, TOK), 0)
    tok = lax.broadcasted_iota(jnp.int32, (PICK, TOK), 1)
    return jnp.where(tok == row * RATE + off, 1.0, 0.0).astype(BF)


def small(mib=12):
    return pltpu.CompilerParams(vmem_limit_bytes=mib << 20)


def pick_kernel(pos_ref, off_hbm, l_hbm, d_hbm, q_hbm, k_hbm, v_hbm, g_hbm, o_hbm, off_ref, l_ref, d_ref, x_ref, o_ref, sems, out_sems):
    loads = [
        pltpu.make_async_copy(src, dst, sems.at[i])
        for i, (src, dst) in enumerate(
            (
                (off_hbm, off_ref),
                (l_hbm.at[0], l_ref),
                (d_hbm.at[0], d_ref),
                (q_hbm.at[0], x_ref.at[0]),
                (k_hbm.at[0], x_ref.at[1]),
                (v_hbm.at[0], x_ref.at[2]),
                (g_hbm.at[0], x_ref.at[3]),
            )
        )
    ]
    for load in loads:
        load.start()
    n = pos_ref[0]
    src = lax.broadcasted_iota(jnp.int32, (TOK, TOK), 0)
    dst = lax.broadcasted_iota(jnp.int32, (TOK, TOK), 1)
    place = jnp.where(dst == (n % 8) * PICK + src // RATE, 1.0, 0.0).astype(BF)
    for load in loads[:3]:
        load.wait()
    head = lax.broadcasted_iota(jnp.int32, (HEADS, TOK), 0)
    lane = lax.broadcasted_iota(jnp.int32, (HEADS, TOK), 1)
    off = jnp.zeros((HEADS, TOK), jnp.int32)
    for h in range(HEADS):
        off = jnp.where(head == h, off_ref[0, h], off)
    hit = (lane % RATE) == off
    lses = dot(jnp.where(hit, l_ref[...].astype(F32), 0.0).astype(BF), place)
    dlts = dot(jnp.where(hit, d_ref[...].astype(F32), 0.0).astype(BF), place)
    row = lax.broadcasted_iota(jnp.int32, (8, HD), 0)
    for h in range(HEADS):
        lse = jnp.broadcast_to(lses[h:h + 1], (8, HD))
        dlt = jnp.broadcast_to(dlts[h:h + 1], (8, HD))
        stats = jnp.where(row == n // 8, lse, jnp.where(row == 4 + n // 8, dlt, 0.0))
        o_ref[h, 0, 16:MAIN] = stats.astype(BF)
        o_ref[h, 1, 16:MAIN] = jnp.zeros((8, HD), BF)
    choose = [chooser(off_ref[0, h]) for h in range(HEADS)]
    stores = []
    for core in range(2):
        for part, first in ((2 * core, 0), (2 * core + 1, MAIN)):
            loads[3 + part].wait()
            for h in range(HEADS):
                rows = dot(choose[h], x_ref[part, :, h * HD:(h + 1) * HD])
                o_ref[h, core, first:first + 16] = rows.astype(BF)
        store = pltpu.make_async_copy(o_ref.at[:, core], o_hbm.at[:, core], out_sems.at[core])
        store.start()
        stores.append(store)
    for store in stores:
        store.wait()


def pick_all(pos, offsets, lse, delta, query, key, value, grad):
    raw = pl.BlockSpec(memory_space=pltpu.HBM)
    return pl.pallas_call(
        pick_kernel,
        in_specs=[SM] + [raw] * 7,
        out_specs=raw,
        out_shape=jax.ShapeDtypeStruct((HEADS, 2, ROWS, HD), BF),
        scratch_shapes=[
            pltpu.SMEM((1, HEADS), jnp.int32),
            pltpu.VMEM((HEADS, TOK), BF),
            pltpu.VMEM((HEADS, TOK), BF),
            pltpu.VMEM((4, TOK, HEADS * HD), BF),
            pltpu.VMEM((HEADS, 2, ROWS, HD), BF),
            pltpu.SemaphoreType.DMA((7,)),
            pltpu.SemaphoreType.DMA((2,)),
        ],
        name="pick_all",
    )(pos, offsets, lse, delta, query, key, value, grad).reshape(GROUP, ROWS, HD)


def score_kernel(off_ref, q_ref, k_ref, l_ref, p_ref, offs_ref, st_ref):
    step = pl.program_id(0)

    @pl.when(step == 0)
    def _():
        st_ref[...] = l_ref[0].astype(F32)
        for h in range(HEADS):
            offs_ref[h:h + 1, :] = jnp.full((1, TOK), off_ref[0, h], jnp.int32)

    lses = st_ref[pl.ds(pl.multiple_of(step * 4, 4), 4), :]
    for i in range(4):
        cols = slice(i * HD, (i + 1) * HD)
        p_ref[i] = jnp.exp(dot_t(k_ref[0, :, cols], q_ref[0, :, cols]) * SCALE - lses[i:i + 1])


def local_scores(offsets, query, key, lse):
    wide = pl.BlockSpec((1, TOK, 4 * HD), lambda i: (0, 0, i))
    stat = pl.BlockSpec((1, HEADS, TOK), lambda i: (0, 0, 0))
    return pl.pallas_call(
        score_kernel,
        grid=(4,),
        in_specs=[SM, wide, wide, stat],
        out_specs=[pl.BlockSpec((4, TOK, TOK), lambda i: (i, 0, 0)), pl.BlockSpec((HEADS, TOK), lambda i: (0, 0))],
        out_shape=[jax.ShapeDtypeStruct((HEADS, TOK, TOK), F32), jax.ShapeDtypeStruct((HEADS, TOK), jnp.int32)],
        scratch_shapes=[pltpu.VMEM((HEADS, TOK), F32)],
        compiler_params=small(),
        cost_estimate=pl.CostEstimate(flops=16 * 2 * 128 ** 3 * 4, bytes_accessed=2097152, transcendentals=262144),
        name="local_scores",
    )(offsets, query, key, lse)


def local_kernel(p_ref, q_ref, k_ref, v_ref, g0_ref, g1_ref, d_ref, dq_ref, dk_ref, dv_ref, st_ref):
    step = pl.program_id(0)

    @pl.when(step == 0)
    def _():
        st_ref[...] = d_ref[0].astype(F32)

    dlts = st_ref[pl.ds(pl.multiple_of(step * 4, 4), 4), :]
    for i in range(4):
        cols = slice(i * HD, (i + 1) * HD)
        q, k, v = q_ref[0, :, cols], k_ref[0, :, cols], v_ref[0, :, cols]
        g = jnp.concatenate([g0_ref[0, :, cols], g1_ref[0, :, cols]], axis=0)
        p = p_ref[i]
        ds = (p * (dot_t(v, g) - dlts[i:i + 1])).astype(BF)
        dv_ref[:, cols] = dot(p.astype(BF), g).astype(BF)
        dk_ref[:, cols] = (dot(ds, q) * SCALE).astype(BF)
        dq_ref[:, cols] = (dot_l(ds, k) * SCALE).astype(BF)


def local_grads(probs, query, key, value, grad0, grad1, delta):
    wide = pl.BlockSpec((1, TOK, 4 * HD), lambda i: (0, 0, i))
    half = pl.BlockSpec((1, TOK // 2, 4 * HD), lambda i: (0, 0, i))
    out = pl.BlockSpec((TOK, 4 * HD), lambda i: (0, i))
    stat = pl.BlockSpec((1, HEADS, TOK), lambda i: (0, 0, 0))
    shape = jax.ShapeDtypeStruct((TOK, HEADS * HD), BF)
    return pl.pallas_call(
        local_kernel,
        grid=(4,),
        in_specs=[pl.BlockSpec((4, TOK, TOK), lambda i: (i, 0, 0)), wide, wide, wide, half, half, stat],
        out_specs=[out, out, out],
        out_shape=[shape, shape, shape],
        scratch_shapes=[pltpu.VMEM((HEADS, TOK), F32)],
        compiler_params=small(),
        cost_estimate=pl.CostEstimate(flops=16 * 4 * 2 * 128 ** 3 * 4, bytes_accessed=4718592, transcendentals=0),
        name="local_grads",
    )(probs, query, key, value, grad0, grad1, delta)


def query_side(q, g, k, v, lse, dlt):
    p = jnp.exp(dot_t(q, k) * SCALE - lse)
    ds = (p * (dot_t(g, v) - dlt)).astype(BF)
    return dot(ds, k)


def key_side(k, v, q, g, stats):
    lse = jnp.concatenate([stats[i:i + 1] for i in range(4)], axis=1)
    dlt = jnp.concatenate([stats[i:i + 1] for i in range(4, 8)], axis=1)
    p = jnp.exp(dot_t(k, q) * SCALE - lse)
    ds = (p * (dot_t(v, g) - dlt)).astype(BF)
    return dot(ds, q), dot(p.astype(BF), g)


def flat(rows):
    return rows.reshape(GROUP * PICK, HD)


def whole(core, mine_a, mine_b, other_a, other_b):
    zero = core == 0
    q = jnp.where(zero, mine_a, other_a)
    v = jnp.where(zero, other_a, mine_a)
    k = jnp.where(zero, mine_b, other_b)
    g = jnp.where(zero, other_b, mine_b)
    return flat(q), flat(k), flat(v), flat(g)


def stats_of(core, mine_a, other_a):
    return jnp.sum(jnp.where(core == 0, mine_a[:, 16:MAIN], other_a[:, 16:MAIN]).astype(F32), axis=0)


def share(core, rows):
    width = rows.shape[-1]
    t = rows.astype(F32).reshape(GROUP, 2, 8, width)
    return jnp.where(core == 0, t[:, 0], t[:, 1]).reshape(HALF, width)


def near_kernel(core_ref, a_ref, b_ref, oa_ref, ob_ref, sub_ref, col_ref, dq_ref, dk_ref, dv_ref):
    core = core_ref[0]
    q, k, v, g = whole(core, a_ref[:, 0:16], b_ref[...], oa_ref[:, 0:16], ob_ref[...])
    stats = stats_of(core, a_ref, oa_ref)
    turned = jnp.transpose(jnp.concatenate([stats, jnp.zeros((HD - 8, HD), F32)], axis=0))
    lse = share(core, jnp.concatenate([turned[:, i:i + 1] for i in range(4)], axis=0))
    dlt = share(core, jnp.concatenate([turned[:, i:i + 1] for i in range(4, 8)], axis=0))
    sq, sk, sv, sg = (share(core, rows).astype(BF) for rows in (q, k, v, g))
    for i, rows in enumerate((sq, sk, sv, sg)):
        sub_ref[i] = rows
    lane = lax.broadcasted_iota(jnp.int32, (HALF, HD), 1)
    col_ref[...] = jnp.where(lane == 0, lse, dlt)
    dq_ref[...] = query_side(sq, sg, k, v, lse, dlt)
    dk_ref[...], dv_ref[...] = key_side(sk, sv, q, g, stats)


def near_grads(*args):
    part = jax.ShapeDtypeStruct((HALF, HD), F32)
    return pl.pallas_call(
        near_kernel,
        in_specs=[SM] + [VM] * 4,
        out_specs=[VM] * 5,
        out_shape=[jax.ShapeDtypeStruct((4, HALF, HD), BF)] + [part] * 4,
        compiler_params=small(),
        cost_estimate=pl.CostEstimate(flops=14 * 2 * 256 * 256 * 128 * 2, bytes_accessed=1572864, transcendentals=262144),
        name="near_grads",
    )(*args)


def far_kernel(core_ref, a_ref, b_ref, oa_ref, ob_ref, sub_ref, col_ref, dq_ref, dk_ref, dv_ref, o_ref):
    core = core_ref[0]
    q, k, v, g = whole(core, a_ref[:, 0:16], b_ref[...], oa_ref[:, 0:16], ob_ref[...])
    stats = stats_of(core, a_ref, oa_ref)
    lse, dlt = col_ref[:, 0:1], col_ref[:, 1:2]
    dq = dq_ref[...] + query_side(sub_ref[0], sub_ref[3], k, v, lse, dlt)
    dk, dv = key_side(sub_ref[1], sub_ref[2], q, g, stats)
    parts = (dq * SCALE, (dk_ref[...] + dk) * SCALE, dv_ref[...] + dv)
    for i, part in enumerate(parts):
        rows = part.reshape(GROUP, 8, HD).astype(BF)
        for to, z in enumerate(OUT_ORDER):
            at = IN_ORDER.index(z) * 4
            o_ref[4 * to:4 * to + 4, 8 * i:8 * i + 8, :] = rows[at:at + 4]


def far_grads(*args):
    return pl.pallas_call(
        far_kernel,
        in_specs=[SM] + [VM] * 9,
        out_specs=VM,
        out_shape=jax.ShapeDtypeStruct((GROUP, 24, HD), BF),
        compiler_params=small(),
        name="far_grads",
    )(*args)


def combine_kernel(w_ref, dq_ref, dk_ref, dv_ref, off_ref, oq_hbm, ok_hbm, ov_hbm, out_ref, sems):
    row = lax.broadcasted_iota(jnp.int32, (PICK, RATE, HD), 1)
    stores = []
    for group in range(4):
        for h in range(4 * group, 4 * group + 4):
            hit = row == off_ref[h:h + 1, :].reshape(1, 1, TOK)
            first = OUT_ORDER.index(IN_ORDER[h // 2]) * 4 + h % 2 * 2
            for part, src in enumerate((dq_ref, dk_ref, dv_ref)):
                rows = slice(part * 8, (part + 1) * 8)
                w = jnp.concatenate([w_ref[first, rows, :].astype(F32), w_ref[first + 1, rows, :].astype(F32)], axis=0)
                local = src[:, h * HD:(h + 1) * HD].astype(F32).reshape(PICK, RATE, HD)
                total = local + jnp.where(hit, w[:, None, :], 0.0)
                out_ref[part, :, h * HD:(h + 1) * HD] = total.reshape(TOK, HD).astype(BF)
        cols = pl.ds(group * 4 * HD, 4 * HD)
        for part, dst in enumerate((oq_hbm, ok_hbm, ov_hbm)):
            store = pltpu.make_async_copy(out_ref.at[part, :, cols], dst.at[0, :, cols], sems.at[group, part])
            store.start()
            stores.append(store)
    for store in stores:
        store.wait()


def combine(wide, local):
    shape = jax.ShapeDtypeStruct((1, TOK, HEADS * HD), BF)
    return pl.pallas_call(
        combine_kernel,
        in_specs=[VM] * 5,
        out_specs=[pl.BlockSpec(memory_space=pltpu.HBM)] * 3,
        out_shape=[shape, shape, shape],
        scratch_shapes=[pltpu.VMEM((3, TOK, HEADS * HD), BF), pltpu.SemaphoreType.DMA((4, 3))],
        compiler_params=small(),
        name="combine",
    )(wide, *local)


def place_of(z, x, c):
    return (z * NX + x) * NC + c


def column(half, place):
    return place if half == 0 else NX - 1 - place


def groups_of(order):
    return [[place_of(z, column(half, p), c) for z in order for p in range(2) for c in range(NC)] for half in range(2)]


IN_ORDER = (5, 4, 3, 2, 1, 0, 7, 6)
OUT_ORDER = IN_ORDER


def move(value, route):
    count, seats = lax.axis_size("section"), lax.axis_size("seq")
    pairs = []
    for s in range(count):
        for z in range(NZ):
            for x in range(NX):
                for c in range(NC):
                    target = route(s, x, c)
                    if target is not None:
                        ts, tx, tc = target
                        pairs.append((s * seats + place_of(z, x, c), (ts % count) * seats + place_of(z, tx, tc)))
    return lax.ppermute(value, ("section", "seq"), pairs)


def swap(value, order):
    return lax.all_to_all(value, "seq", 0, 0, axis_index_groups=groups_of(order), tiled=True)


def body(queries, key_rows, value_rows, grad_out, log_sums, deltas, offsets):
    seat = lax.axis_index("seq").astype(jnp.int32)
    x = seat // NC % NX
    core = (seat % NC).reshape(1)
    z = seat // (NX * NC)
    turn = sum(jnp.where(z == at, i, 0) for i, at in enumerate(IN_ORDER))
    pos = (turn * 4 + jnp.where(x < 2, x, NX - 1 - x) * 2 + seat % NC).reshape(1)
    picked = pick_all(pos, offsets, log_sums, deltas, queries, key_rows, value_rows, grad_out)
    mine = swap(picked, IN_ORDER)
    grad0 = move(grad_out[:, :TOK // 2], lambda s, x, c: (s - 1, x, c))
    grad1 = move(grad_out[:, TOK // 2:], lambda s, x, c: (s - 1, x, c))
    probs, offs = local_scores(offsets, queries, key_rows, log_sums)
    a, b = mine[:, :MAIN], mine[:, MAIN:]
    far_a = move(a, lambda s, x, c: (s, 3 - x, c))
    far_b = move(b, lambda s, x, c: (s - c, 3 - x, c))
    other_a = move(a, lambda s, x, c: (s, x, 1 - c))
    own_b = move(b, lambda s, x, c: (s - c, x, c))
    other_b = move(own_b, lambda s, x, c: (s, x, 1 - c))
    other_far_a = move(far_a, lambda s, x, c: (s, x, 1 - c))
    other_far_b = move(far_b, lambda s, x, c: (s, x, 1 - c))
    local = local_grads(probs, queries, key_rows, value_rows, grad0, grad1, deltas)
    part = near_grads(core, a, own_b, other_a, other_b)
    back = swap(far_grads(core, far_a, far_b, other_far_a, other_far_b, *part), OUT_ORDER)
    return tuple(combine(back, (*local, offs)))


def solution(mesh):
    rows = P("section", "seq", None)
    stats = P("section", None, "seq")
    return jax.shard_map(
        body,
        mesh=mesh,
        in_specs=(rows, rows, rows, rows, stats, stats, P("seq", None)),
        out_specs=(rows, rows, rows),
        check_vma=False,
    )
```

```python
import jax
import jax.numpy as jnp
from jax import lax
from jax.experimental import pallas as pl
from jax.experimental.pallas import tpu as pltpu
from jax.sharding import PartitionSpec as P


HEADS = 16
HD = 128
PICK = 16
RATE = 8
TOK = 128
NZ, NX, NC = 8, 4, 2
ROWS = 40
MAIN = 24
GROUP = 32
HALF = GROUP * PICK // 2
SCALE = HD ** (-0.5)
BF = jnp.bfloat16
F32 = jnp.float32

VM = pl.BlockSpec(memory_space=pltpu.VMEM)
SM = pl.BlockSpec(memory_space=pltpu.SMEM)


def dot(a, b):
    return lax.dot_general(a, b, (((1,), (0,)), ((), ())), preferred_element_type=F32)


def dot_t(a, b):
    return lax.dot_general(a, b, (((1,), (1,)), ((), ())), preferred_element_type=F32)


def dot_l(a, b):
    return lax.dot_general(a, b, (((0,), (0,)), ((), ())), preferred_element_type=F32)


def chooser(off):
    row = lax.broadcasted_iota(jnp.int32, (PICK, TOK), 0)
    tok = lax.broadcasted_iota(jnp.int32, (PICK, TOK), 1)
    return jnp.where(tok == row * RATE + off, 1.0, 0.0).astype(BF)


def small(mib=12):
    return pltpu.CompilerParams(vmem_limit_bytes=mib << 20)


def pick_kernel(pos_ref, off_hbm, l_hbm, d_hbm, q_hbm, k_hbm, v_hbm, g_hbm, o_hbm, off_ref, l_ref, d_ref, x_ref, o_ref, sems, out_sems):
    loads = [
        pltpu.make_async_copy(src, dst, sems.at[i])
        for i, (src, dst) in enumerate(
            (
                (off_hbm, off_ref),
                (l_hbm.at[0], l_ref),
                (d_hbm.at[0], d_ref),
                (q_hbm.at[0], x_ref.at[0]),
                (k_hbm.at[0], x_ref.at[1]),
                (v_hbm.at[0], x_ref.at[2]),
                (g_hbm.at[0], x_ref.at[3]),
            )
        )
    ]
    for load in loads:
        load.start()
    n = pos_ref[0]
    src = lax.broadcasted_iota(jnp.int32, (TOK, TOK), 0)
    dst = lax.broadcasted_iota(jnp.int32, (TOK, TOK), 1)
    place = jnp.where(dst == (n % 8) * PICK + src // RATE, 1.0, 0.0).astype(BF)
    for load in loads[:3]:
        load.wait()
    head = lax.broadcasted_iota(jnp.int32, (HEADS, TOK), 0)
    lane = lax.broadcasted_iota(jnp.int32, (HEADS, TOK), 1)
    off = jnp.zeros((HEADS, TOK), jnp.int32)
    for h in range(HEADS):
        off = jnp.where(head == h, off_ref[0, h], off)
    hit = (lane % RATE) == off
    lses = dot(jnp.where(hit, l_ref[...].astype(F32), 0.0).astype(BF), place)
    dlts = dot(jnp.where(hit, d_ref[...].astype(F32), 0.0).astype(BF), place)
    row = lax.broadcasted_iota(jnp.int32, (8, HD), 0)
    for h in range(HEADS):
        lse = jnp.broadcast_to(lses[h:h + 1], (8, HD))
        dlt = jnp.broadcast_to(dlts[h:h + 1], (8, HD))
        stats = jnp.where(row == n // 8, lse, jnp.where(row == 4 + n // 8, dlt, 0.0))
        o_ref[h, 0, 16:MAIN] = stats.astype(BF)
        o_ref[h, 1, 16:MAIN] = jnp.zeros((8, HD), BF)
    choose = [chooser(off_ref[0, h]) for h in range(HEADS)]
    stores = []
    for core in range(2):
        for part, first in ((2 * core, 0), (2 * core + 1, MAIN)):
            loads[3 + part].wait()
            for h in range(HEADS):
                rows = dot(choose[h], x_ref[part, :, h * HD:(h + 1) * HD])
                o_ref[h, core, first:first + 16] = rows.astype(BF)
        store = pltpu.make_async_copy(o_ref.at[:, core], o_hbm.at[:, core], out_sems.at[core])
        store.start()
        stores.append(store)
    for store in stores:
        store.wait()


def pick_all(pos, offsets, lse, delta, query, key, value, grad):
    raw = pl.BlockSpec(memory_space=pltpu.HBM)
    return pl.pallas_call(
        pick_kernel,
        in_specs=[SM] + [raw] * 7,
        out_specs=raw,
        out_shape=jax.ShapeDtypeStruct((HEADS, 2, ROWS, HD), BF),
        scratch_shapes=[
            pltpu.SMEM((1, HEADS), jnp.int32),
            pltpu.VMEM((HEADS, TOK), BF),
            pltpu.VMEM((HEADS, TOK), BF),
            pltpu.VMEM((4, TOK, HEADS * HD), BF),
            pltpu.VMEM((HEADS, 2, ROWS, HD), BF),
            pltpu.SemaphoreType.DMA((7,)),
            pltpu.SemaphoreType.DMA((2,)),
        ],
        name="pick_all",
    )(pos, offsets, lse, delta, query, key, value, grad).reshape(GROUP, ROWS, HD)


def offsets_kernel(off_ref, o_ref):
    for h in range(HEADS):
        o_ref[h:h + 1, :] = jnp.full((1, TOK), off_ref[0, h], jnp.int32)


def spread_offsets(offsets):
    return pl.pallas_call(
        offsets_kernel,
        in_specs=[SM],
        out_specs=VM,
        out_shape=jax.ShapeDtypeStruct((HEADS, TOK), jnp.int32),
        compiler_params=small(),
        name="spread_offsets",
    )(offsets)


def local_kernel(q_ref, k_ref, v_ref, g_ref, l_ref, d_ref, dq_ref, dk_ref, dv_ref, st_ref):
    step = pl.program_id(0)

    @pl.when(step == 0)
    def _():
        st_ref[0] = l_ref[0].astype(F32)
        st_ref[1] = d_ref[0].astype(F32)

    base = pl.multiple_of(step * 4, 4)
    lses = st_ref[0, pl.ds(base, 4), :]
    dlts = st_ref[1, pl.ds(base, 4), :]
    for i in range(4):
        cols = slice(i * HD, (i + 1) * HD)
        q, k, v, g = q_ref[0, :, cols], k_ref[0, :, cols], v_ref[0, :, cols], g_ref[0, :, cols]
        p = jnp.exp(dot_t(k, q) * SCALE - lses[i:i + 1])
        ds = (p * (dot_t(v, g) - dlts[i:i + 1])).astype(BF)
        dv_ref[:, cols] = dot(p.astype(BF), g).astype(BF)
        dk_ref[:, cols] = (dot(ds, q) * SCALE).astype(BF)
        dq_ref[:, cols] = (dot_l(ds, k) * SCALE).astype(BF)


def local_grads(query, key, value, grad, lse, delta):
    wide = pl.BlockSpec((1, TOK, 4 * HD), lambda i: (0, 0, i))
    out = pl.BlockSpec((TOK, 4 * HD), lambda i: (0, i))
    stat = pl.BlockSpec((1, HEADS, TOK), lambda i: (0, 0, 0))
    shape = jax.ShapeDtypeStruct((TOK, HEADS * HD), BF)
    return pl.pallas_call(
        local_kernel,
        grid=(4,),
        in_specs=[wide, wide, wide, wide, stat, stat],
        out_specs=[out, out, out],
        out_shape=[shape, shape, shape],
        scratch_shapes=[pltpu.VMEM((2, HEADS, TOK), F32)],
        compiler_params=small(),
        cost_estimate=pl.CostEstimate(flops=16 * 5 * 2 * 128 ** 3 * 4, bytes_accessed=3670016, transcendentals=262144),
        name="local_grads",
    )(query, key, value, grad, lse, delta)


def query_side(q, g, k, v, lse, dlt):
    p = jnp.exp(dot_t(q, k) * SCALE - lse)
    ds = (p * (dot_t(g, v) - dlt)).astype(BF)
    return dot(ds, k)


def key_side(k, v, q, g, stats):
    lse = jnp.concatenate([stats[i:i + 1] for i in range(4)], axis=1)
    dlt = jnp.concatenate([stats[i:i + 1] for i in range(4, 8)], axis=1)
    p = jnp.exp(dot_t(k, q) * SCALE - lse)
    ds = (p * (dot_t(v, g) - dlt)).astype(BF)
    return dot(ds, q), dot(p.astype(BF), g)


def flat(rows):
    return rows.reshape(GROUP * PICK, HD)


def whole(core, mine_a, mine_b, other_a, other_b):
    zero = core == 0
    q = jnp.where(zero, mine_a, other_a)
    v = jnp.where(zero, other_a, mine_a)
    k = jnp.where(zero, mine_b, other_b)
    g = jnp.where(zero, other_b, mine_b)
    return flat(q), flat(k), flat(v), flat(g)


def stats_of(core, mine_a, other_a):
    return jnp.sum(jnp.where(core == 0, mine_a[:, 16:MAIN], other_a[:, 16:MAIN]).astype(F32), axis=0)


def share(core, rows):
    width = rows.shape[-1]
    t = rows.astype(F32).reshape(GROUP, 2, 8, width)
    return jnp.where(core == 0, t[:, 0], t[:, 1]).reshape(HALF, width)


def near_kernel(core_ref, a_ref, b_ref, oa_ref, hop_ref, ob_ref, sub_ref, col_ref, dq_ref, dk_ref, dv_ref):
    core = core_ref[0]
    mine_b = jnp.where(core == 0, b_ref[...], hop_ref[...])
    q, k, v, g = whole(core, a_ref[:, 0:16], mine_b, oa_ref[:, 0:16], ob_ref[...])
    stats = stats_of(core, a_ref, oa_ref)
    turned = jnp.transpose(jnp.concatenate([stats, jnp.zeros((HD - 8, HD), F32)], axis=0))
    lse = share(core, jnp.concatenate([turned[:, i:i + 1] for i in range(4)], axis=0))
    dlt = share(core, jnp.concatenate([turned[:, i:i + 1] for i in range(4, 8)], axis=0))
    sq, sk, sv, sg = (share(core, rows).astype(BF) for rows in (q, k, v, g))
    for i, rows in enumerate((sq, sk, sv, sg)):
        sub_ref[i] = rows
    lane = lax.broadcasted_iota(jnp.int32, (HALF, HD), 1)
    col_ref[...] = jnp.where(lane == 0, lse, dlt)
    dq_ref[...] = query_side(sq, sg, k, v, lse, dlt)
    dk_ref[...], dv_ref[...] = key_side(sk, sv, q, g, stats)


def near_grads(*args):
    part = jax.ShapeDtypeStruct((HALF, HD), F32)
    return pl.pallas_call(
        near_kernel,
        in_specs=[SM] + [VM] * 5,
        out_specs=[VM] * 5,
        out_shape=[jax.ShapeDtypeStruct((4, HALF, HD), BF)] + [part] * 4,
        compiler_params=small(),
        cost_estimate=pl.CostEstimate(flops=14 * 2 * 256 * 256 * 128 * 2, bytes_accessed=1572864, transcendentals=262144),
        name="near_grads",
    )(*args)


def far_kernel(core_ref, a_ref, b_ref, oa_ref, ob_ref, sub_ref, col_ref, dq_ref, dk_ref, dv_ref, o_ref):
    core = core_ref[0]
    q, k, v, g = whole(core, a_ref[:, 0:16], b_ref[...], oa_ref[:, 0:16], ob_ref[...])
    stats = stats_of(core, a_ref, oa_ref)
    lse, dlt = col_ref[:, 0:1], col_ref[:, 1:2]
    dq = dq_ref[...] + query_side(sub_ref[0], sub_ref[3], k, v, lse, dlt)
    dk, dv = key_side(sub_ref[1], sub_ref[2], q, g, stats)
    parts = (dq * SCALE, (dk_ref[...] + dk) * SCALE, dv_ref[...] + dv)
    for i, part in enumerate(parts):
        rows = part.reshape(GROUP, 8, HD).astype(BF)
        for to, z in enumerate(OUT_ORDER):
            at = IN_ORDER.index(z) * 4
            o_ref[4 * to:4 * to + 4, 8 * i:8 * i + 8, :] = rows[at:at + 4]


def far_grads(*args):
    return pl.pallas_call(
        far_kernel,
        in_specs=[SM] + [VM] * 9,
        out_specs=VM,
        out_shape=jax.ShapeDtypeStruct((GROUP, 24, HD), BF),
        compiler_params=small(),
        name="far_grads",
    )(*args)


def combine_kernel(w_ref, dq_ref, dk_ref, dv_ref, off_ref, oq_hbm, ok_hbm, ov_hbm, out_ref, sems):
    row = lax.broadcasted_iota(jnp.int32, (PICK, RATE, HD), 1)
    stores = []
    for group in range(4):
        for h in range(4 * group, 4 * group + 4):
            hit = row == off_ref[h:h + 1, :].reshape(1, 1, TOK)
            first = OUT_ORDER.index(IN_ORDER[h // 2]) * 4 + h % 2 * 2
            for part, src in enumerate((dq_ref, dk_ref, dv_ref)):
                rows = slice(part * 8, (part + 1) * 8)
                w = jnp.concatenate([w_ref[first, rows, :].astype(F32), w_ref[first + 1, rows, :].astype(F32)], axis=0)
                local = src[:, h * HD:(h + 1) * HD].astype(F32).reshape(PICK, RATE, HD)
                total = local + jnp.where(hit, w[:, None, :], 0.0)
                out_ref[part, :, h * HD:(h + 1) * HD] = total.reshape(TOK, HD).astype(BF)
        cols = pl.ds(group * 4 * HD, 4 * HD)
        for part, dst in enumerate((oq_hbm, ok_hbm, ov_hbm)):
            store = pltpu.make_async_copy(out_ref.at[part, :, cols], dst.at[0, :, cols], sems.at[group, part])
            store.start()
            stores.append(store)
    for store in stores:
        store.wait()


def combine(wide, local):
    shape = jax.ShapeDtypeStruct((1, TOK, HEADS * HD), BF)
    return pl.pallas_call(
        combine_kernel,
        in_specs=[VM] * 5,
        out_specs=[pl.BlockSpec(memory_space=pltpu.HBM)] * 3,
        out_shape=[shape, shape, shape],
        scratch_shapes=[pltpu.VMEM((3, TOK, HEADS * HD), BF), pltpu.SemaphoreType.DMA((4, 3))],
        compiler_params=small(),
        name="combine",
    )(wide, *local)


def place_of(z, x, c):
    return (z * NX + x) * NC + c


def column(half, place):
    return place if half == 0 else NX - 1 - place


def groups_of(order):
    return [[place_of(z, column(half, p), c) for z in order for p in range(2) for c in range(NC)] for half in range(2)]


IN_ORDER = (5, 4, 3, 2, 1, 0, 7, 6)
OUT_ORDER = IN_ORDER


def move(value, route):
    count, seats = lax.axis_size("section"), lax.axis_size("seq")
    pairs = []
    for s in range(count):
        for z in range(NZ):
            for x in range(NX):
                for c in range(NC):
                    target = route(s, x, c)
                    if target is not None:
                        ts, tx, tc = target
                        pairs.append((s * seats + place_of(z, x, c), (ts % count) * seats + place_of(z, tx, tc)))
    return lax.ppermute(value, ("section", "seq"), pairs)


def swap(value, order):
    return lax.all_to_all(value, "seq", 0, 0, axis_index_groups=groups_of(order), tiled=True)


def body(queries, key_rows, value_rows, grad_out, log_sums, deltas, offsets):
    seat = lax.axis_index("seq").astype(jnp.int32)
    x = seat // NC % NX
    core = (seat % NC).reshape(1)
    z = seat // (NX * NC)
    turn = sum(jnp.where(z == at, i, 0) for i, at in enumerate(IN_ORDER))
    pos = (turn * 4 + jnp.where(x < 2, x, NX - 1 - x) * 2 + seat % NC).reshape(1)
    picked = pick_all(pos, offsets, log_sums, deltas, queries, key_rows, value_rows, grad_out)
    mine = swap(picked, IN_ORDER)
    offs = spread_offsets(offsets)
    a, b = mine[:, :MAIN], mine[:, MAIN:]
    far_a = move(a, lambda s, x, c: (s, 3 - x, c))
    far_b = move(b, lambda s, x, c: (s - c, 3 - x, c))
    hop = move(b, lambda s, x, c: (s - 1, x, 1) if c == 1 else None)
    other_b = move(b, lambda s, x, c: (s - c, x, 1 - c))
    other_a = move(a, lambda s, x, c: (s, x, 1 - c))
    grad = move(grad_out, lambda s, x, c: (s - 1, x, c))
    other_far_a = move(far_a, lambda s, x, c: (s, x, 1 - c))
    other_far_b = move(far_b, lambda s, x, c: (s, x, 1 - c))
    local = local_grads(queries, key_rows, value_rows, grad, log_sums, deltas)
    part = near_grads(core, a, b, other_a, hop, other_b)
    back = swap(far_grads(core, far_a, far_b, other_far_a, other_far_b, *part), OUT_ORDER)
    return tuple(combine(back, (*local, offs)))


def solution(mesh):
    rows = P("section", "seq", None)
    stats = P("section", None, "seq")
    return jax.shard_map(
        body,
        mesh=mesh,
        in_specs=(rows, rows, rows, rows, stats, stats, P("seq", None)),
        out_specs=(rows, rows, rows),
        check_vma=False,
    )
```

```python
import jax
import jax.numpy as jnp
from jax import lax
from jax.experimental import pallas as pl
from jax.experimental.pallas import tpu as pltpu
from jax.sharding import PartitionSpec as P


HEADS = 16
HD = 128
PICK = 16
RATE = 8
TOK = 128
NZ, NX, NC = 8, 4, 2
ROWS = 40
MAIN = 24
GROUP = 32
HALF = GROUP * PICK // 2
SCALE = HD ** (-0.5)
BF = jnp.bfloat16
F32 = jnp.float32

VM = pl.BlockSpec(memory_space=pltpu.VMEM)
SM = pl.BlockSpec(memory_space=pltpu.SMEM)


def dot(a, b):
    return lax.dot_general(a, b, (((1,), (0,)), ((), ())), preferred_element_type=F32)


def dot_t(a, b):
    return lax.dot_general(a, b, (((1,), (1,)), ((), ())), preferred_element_type=F32)


def dot_l(a, b):
    return lax.dot_general(a, b, (((0,), (0,)), ((), ())), preferred_element_type=F32)


def chooser(off):
    row = lax.broadcasted_iota(jnp.int32, (PICK, TOK), 0)
    tok = lax.broadcasted_iota(jnp.int32, (PICK, TOK), 1)
    return jnp.where(tok == row * RATE + off, 1.0, 0.0).astype(BF)


def small(mib=12):
    return pltpu.CompilerParams(vmem_limit_bytes=mib << 20)


def pick_kernel(pos_ref, off_hbm, l_hbm, d_hbm, q_hbm, k_hbm, v_hbm, g_hbm, o_hbm, off_ref, l_ref, d_ref, x_ref, o_ref, sems, out_sems):
    loads = [
        pltpu.make_async_copy(src, dst, sems.at[i])
        for i, (src, dst) in enumerate(
            (
                (off_hbm, off_ref),
                (l_hbm.at[0], l_ref),
                (d_hbm.at[0], d_ref),
                (q_hbm.at[0], x_ref.at[0]),
                (k_hbm.at[0], x_ref.at[1]),
                (v_hbm.at[0], x_ref.at[2]),
                (g_hbm.at[0], x_ref.at[3]),
            )
        )
    ]
    for load in loads:
        load.start()
    n = pos_ref[0]
    src = lax.broadcasted_iota(jnp.int32, (TOK, TOK), 0)
    dst = lax.broadcasted_iota(jnp.int32, (TOK, TOK), 1)
    place = jnp.where(dst == (n % 8) * PICK + src // RATE, 1.0, 0.0).astype(BF)
    for load in loads[:3]:
        load.wait()
    head = lax.broadcasted_iota(jnp.int32, (HEADS, TOK), 0)
    lane = lax.broadcasted_iota(jnp.int32, (HEADS, TOK), 1)
    off = jnp.zeros((HEADS, TOK), jnp.int32)
    for h in range(HEADS):
        off = jnp.where(head == h, off_ref[0, h], off)
    hit = (lane % RATE) == off
    lses = dot(jnp.where(hit, l_ref[...].astype(F32), 0.0).astype(BF), place)
    dlts = dot(jnp.where(hit, d_ref[...].astype(F32), 0.0).astype(BF), place)
    row = lax.broadcasted_iota(jnp.int32, (8, HD), 0)
    for h in range(HEADS):
        lse = jnp.broadcast_to(lses[h:h + 1], (8, HD))
        dlt = jnp.broadcast_to(dlts[h:h + 1], (8, HD))
        stats = jnp.where(row == n // 8, lse, jnp.where(row == 4 + n // 8, dlt, 0.0))
        o_ref[h, 0, 16:MAIN] = stats.astype(BF)
        o_ref[h, 1, 16:MAIN] = jnp.zeros((8, HD), BF)
    choose = [chooser(off_ref[0, h]) for h in range(HEADS)]
    stores = []
    for core in range(2):
        for part, first in ((2 * core, 0), (2 * core + 1, MAIN)):
            loads[3 + part].wait()
            for h in range(HEADS):
                rows = dot(choose[h], x_ref[part, :, h * HD:(h + 1) * HD])
                o_ref[h, core, first:first + 16] = rows.astype(BF)
        store = pltpu.make_async_copy(o_ref.at[:, core], o_hbm.at[:, core], out_sems.at[core])
        store.start()
        stores.append(store)
    for store in stores:
        store.wait()


def pick_all(pos, offsets, lse, delta, query, key, value, grad):
    raw = pl.BlockSpec(memory_space=pltpu.HBM)
    return pl.pallas_call(
        pick_kernel,
        in_specs=[SM] + [raw] * 7,
        out_specs=raw,
        out_shape=jax.ShapeDtypeStruct((HEADS, 2, ROWS, HD), BF),
        scratch_shapes=[
            pltpu.SMEM((1, HEADS), jnp.int32),
            pltpu.VMEM((HEADS, TOK), BF),
            pltpu.VMEM((HEADS, TOK), BF),
            pltpu.VMEM((4, TOK, HEADS * HD), BF),
            pltpu.VMEM((HEADS, 2, ROWS, HD), BF),
            pltpu.SemaphoreType.DMA((7,)),
            pltpu.SemaphoreType.DMA((2,)),
        ],
        name="pick_all",
    )(pos, offsets, lse, delta, query, key, value, grad).reshape(GROUP, ROWS, HD)


def offsets_kernel(off_ref, o_ref):
    for h in range(HEADS):
        o_ref[h:h + 1, :] = jnp.full((1, TOK), off_ref[0, h], jnp.int32)


def spread_offsets(offsets):
    return pl.pallas_call(
        offsets_kernel,
        in_specs=[SM],
        out_specs=VM,
        out_shape=jax.ShapeDtypeStruct((HEADS, TOK), jnp.int32),
        compiler_params=small(),
        name="spread_offsets",
    )(offsets)


def local_kernel(q_ref, k_ref, v_ref, g_ref, l_ref, d_ref, dq_ref, dk_ref, dv_ref, st_ref):
    step = pl.program_id(0)

    @pl.when(step == 0)
    def _():
        st_ref[0] = l_ref[0].astype(F32)
        st_ref[1] = d_ref[0].astype(F32)

    base = pl.multiple_of(step * 4, 4)
    lses = st_ref[0, pl.ds(base, 4), :]
    dlts = st_ref[1, pl.ds(base, 4), :]
    for i in range(4):
        cols = slice(i * HD, (i + 1) * HD)
        q, k, v, g = q_ref[0, :, cols], k_ref[0, :, cols], v_ref[0, :, cols], g_ref[0, :, cols]
        p = jnp.exp(dot_t(k, q) * SCALE - lses[i:i + 1])
        ds = (p * (dot_t(v, g) - dlts[i:i + 1])).astype(BF)
        dv_ref[:, cols] = dot(p.astype(BF), g).astype(BF)
        dk_ref[:, cols] = (dot(ds, q) * SCALE).astype(BF)
        dq_ref[:, cols] = (dot_l(ds, k) * SCALE).astype(BF)


def local_grads(query, key, value, grad, lse, delta):
    wide = pl.BlockSpec((1, TOK, 4 * HD), lambda i: (0, 0, i))
    out = pl.BlockSpec((TOK, 4 * HD), lambda i: (0, i))
    stat = pl.BlockSpec((1, HEADS, TOK), lambda i: (0, 0, 0))
    shape = jax.ShapeDtypeStruct((TOK, HEADS * HD), BF)
    return pl.pallas_call(
        local_kernel,
        grid=(4,),
        in_specs=[wide, wide, wide, wide, stat, stat],
        out_specs=[out, out, out],
        out_shape=[shape, shape, shape],
        scratch_shapes=[pltpu.VMEM((2, HEADS, TOK), F32)],
        compiler_params=small(),
        cost_estimate=pl.CostEstimate(flops=16 * 5 * 2 * 128 ** 3 * 4, bytes_accessed=3670016, transcendentals=262144),
        name="local_grads",
    )(query, key, value, grad, lse, delta)


def query_side(q, g, k, v, lse, dlt):
    p = jnp.exp(dot_t(q, k) * SCALE - lse)
    ds = (p * (dot_t(g, v) - dlt)).astype(BF)
    return dot(ds, k)


def key_side(k, v, q, g, stats):
    lse = jnp.concatenate([stats[i:i + 1] for i in range(4)], axis=1)
    dlt = jnp.concatenate([stats[i:i + 1] for i in range(4, 8)], axis=1)
    p = jnp.exp(dot_t(k, q) * SCALE - lse)
    ds = (p * (dot_t(v, g) - dlt)).astype(BF)
    return dot(ds, q), dot(p.astype(BF), g)


def flat(rows):
    return rows.reshape(GROUP * PICK, HD)


def whole(core, mine_a, mine_b, other_a, other_b):
    zero = core == 0
    q = jnp.where(zero, mine_a, other_a)
    v = jnp.where(zero, other_a, mine_a)
    k = jnp.where(zero, mine_b, other_b)
    g = jnp.where(zero, other_b, mine_b)
    return flat(q), flat(k), flat(v), flat(g)


def stats_of(core, mine_a, other_a):
    return jnp.sum(jnp.where(core == 0, mine_a[:, 16:MAIN], other_a[:, 16:MAIN]).astype(F32), axis=0)


def share(core, rows):
    width = rows.shape[-1]
    t = rows.astype(F32).reshape(GROUP, 2, 8, width)
    return jnp.where(core == 0, t[:, 0], t[:, 1]).reshape(HALF, width)


def near_kernel(core_ref, a_ref, b_ref, oa_ref, ob_ref, sub_ref, col_ref, dq_ref, dk_ref, dv_ref):
    core = core_ref[0]
    q, k, v, g = whole(core, a_ref[:, 0:16], b_ref[...], oa_ref[:, 0:16], ob_ref[...])
    stats = stats_of(core, a_ref, oa_ref)
    turned = jnp.transpose(jnp.concatenate([stats, jnp.zeros((HD - 8, HD), F32)], axis=0))
    lse = share(core, jnp.concatenate([turned[:, i:i + 1] for i in range(4)], axis=0))
    dlt = share(core, jnp.concatenate([turned[:, i:i + 1] for i in range(4, 8)], axis=0))
    sq, sk, sv, sg = (share(core, rows).astype(BF) for rows in (q, k, v, g))
    for i, rows in enumerate((sq, sk, sv, sg)):
        sub_ref[i] = rows
    lane = lax.broadcasted_iota(jnp.int32, (HALF, HD), 1)
    col_ref[...] = jnp.where(lane == 0, lse, dlt)
    dq_ref[...] = query_side(sq, sg, k, v, lse, dlt)
    dk_ref[...], dv_ref[...] = key_side(sk, sv, q, g, stats)


def near_grads(*args):
    part = jax.ShapeDtypeStruct((HALF, HD), F32)
    return pl.pallas_call(
        near_kernel,
        in_specs=[SM] + [VM] * 4,
        out_specs=[VM] * 5,
        out_shape=[jax.ShapeDtypeStruct((4, HALF, HD), BF)] + [part] * 4,
        compiler_params=small(),
        cost_estimate=pl.CostEstimate(flops=14 * 2 * 256 * 256 * 128 * 2, bytes_accessed=1572864, transcendentals=262144),
        name="near_grads",
    )(*args)


def far_kernel(core_ref, a_ref, b_ref, oa_ref, ob_ref, sub_ref, col_ref, dq_ref, dk_ref, dv_ref, o_ref):
    core = core_ref[0]
    q, k, v, g = whole(core, a_ref[:, 0:16], b_ref[...], oa_ref[:, 0:16], ob_ref[...])
    stats = stats_of(core, a_ref, oa_ref)
    lse, dlt = col_ref[:, 0:1], col_ref[:, 1:2]
    dq = dq_ref[...] + query_side(sub_ref[0], sub_ref[3], k, v, lse, dlt)
    dk, dv = key_side(sub_ref[1], sub_ref[2], q, g, stats)
    parts = (dq * SCALE, (dk_ref[...] + dk) * SCALE, dv_ref[...] + dv)
    for i, part in enumerate(parts):
        rows = part.reshape(GROUP, 8, HD).astype(BF)
        for to, z in enumerate(OUT_ORDER):
            at = IN_ORDER.index(z) * 4
            o_ref[4 * to:4 * to + 4, 8 * i:8 * i + 8, :] = rows[at:at + 4]


def far_grads(*args):
    return pl.pallas_call(
        far_kernel,
        in_specs=[SM] + [VM] * 9,
        out_specs=VM,
        out_shape=jax.ShapeDtypeStruct((GROUP, 24, HD), BF),
        compiler_params=small(),
        name="far_grads",
    )(*args)


def combine_kernel(w_ref, dq_ref, dk_ref, dv_ref, off_ref, oq_hbm, ok_hbm, ov_hbm, out_ref, sems):
    row = lax.broadcasted_iota(jnp.int32, (PICK, RATE, HD), 1)
    stores = []
    for group in range(4):
        for h in range(4 * group, 4 * group + 4):
            hit = row == off_ref[h:h + 1, :].reshape(1, 1, TOK)
            first = OUT_ORDER.index(IN_ORDER[h // 2]) * 4 + h % 2 * 2
            for part, src in enumerate((dq_ref, dk_ref, dv_ref)):
                rows = slice(part * 8, (part + 1) * 8)
                w = jnp.concatenate([w_ref[first, rows, :].astype(F32), w_ref[first + 1, rows, :].astype(F32)], axis=0)
                local = src[:, h * HD:(h + 1) * HD].astype(F32).reshape(PICK, RATE, HD)
                total = local + jnp.where(hit, w[:, None, :], 0.0)
                out_ref[part, :, h * HD:(h + 1) * HD] = total.reshape(TOK, HD).astype(BF)
        cols = pl.ds(group * 4 * HD, 4 * HD)
        for part, dst in enumerate((oq_hbm, ok_hbm, ov_hbm)):
            store = pltpu.make_async_copy(out_ref.at[part, :, cols], dst.at[0, :, cols], sems.at[group, part])
            store.start()
            stores.append(store)
    for store in stores:
        store.wait()


def combine(wide, local):
    shape = jax.ShapeDtypeStruct((1, TOK, HEADS * HD), BF)
    return pl.pallas_call(
        combine_kernel,
        in_specs=[VM] * 5,
        out_specs=[pl.BlockSpec(memory_space=pltpu.HBM)] * 3,
        out_shape=[shape, shape, shape],
        scratch_shapes=[pltpu.VMEM((3, TOK, HEADS * HD), BF), pltpu.SemaphoreType.DMA((4, 3))],
        compiler_params=small(),
        name="combine",
    )(wide, *local)


def place_of(z, x, c):
    return (z * NX + x) * NC + c


def column(half, place):
    return place if half == 0 else NX - 1 - place


def groups_of(order):
    return [[place_of(z, column(half, p), c) for z in order for p in range(2) for c in range(NC)] for half in range(2)]


IN_ORDER = (5, 4, 3, 2, 1, 0, 7, 6)
OUT_ORDER = IN_ORDER


def move(value, route):
    count, seats = lax.axis_size("section"), lax.axis_size("seq")
    pairs = []
    for s in range(count):
        for z in range(NZ):
            for x in range(NX):
                for c in range(NC):
                    target = route(s, x, c)
                    if target is not None:
                        ts, tx, tc = target
                        pairs.append((s * seats + place_of(z, x, c), (ts % count) * seats + place_of(z, tx, tc)))
    return lax.ppermute(value, ("section", "seq"), pairs)


def swap(value, order):
    return lax.all_to_all(value, "seq", 0, 0, axis_index_groups=groups_of(order), tiled=True)


def body(queries, key_rows, value_rows, grad_out, log_sums, deltas, offsets):
    seat = lax.axis_index("seq").astype(jnp.int32)
    x = seat // NC % NX
    core = (seat % NC).reshape(1)
    z = seat // (NX * NC)
    turn = sum(jnp.where(z == at, i, 0) for i, at in enumerate(IN_ORDER))
    pos = (turn * 4 + jnp.where(x < 2, x, NX - 1 - x) * 2 + seat % NC).reshape(1)
    picked = pick_all(pos, offsets, log_sums, deltas, queries, key_rows, value_rows, grad_out)
    mine = swap(picked, IN_ORDER)
    offs = spread_offsets(offsets)
    a, b = mine[:, :MAIN], mine[:, MAIN:]
    far_a = move(a, lambda s, x, c: (s, 3 - x, c))
    far_b = move(b, lambda s, x, c: (s - c, 3 - x, c))
    own_b = move(b, lambda s, x, c: (s - c, x, c))
    other_b = move(own_b, lambda s, x, c: (s, x, 1 - c))
    other_a = move(a, lambda s, x, c: (s, x, 1 - c))
    grad = move(grad_out, lambda s, x, c: (s - 1, x, c))
    other_far_a = move(far_a, lambda s, x, c: (s, x, 1 - c))
    other_far_b = move(far_b, lambda s, x, c: (s, x, 1 - c))
    local = local_grads(queries, key_rows, value_rows, grad, log_sums, deltas)
    part = near_grads(core, a, own_b, other_a, other_b)
    back = swap(far_grads(core, far_a, far_b, other_far_a, other_far_b, *part), OUT_ORDER)
    return tuple(combine(back, (*local, offs)))


def solution(mesh):
    rows = P("section", "seq", None)
    stats = P("section", None, "seq")
    return jax.shard_map(
        body,
        mesh=mesh,
        in_specs=(rows, rows, rows, rows, stats, stats, P("seq", None)),
        out_specs=(rows, rows, rows),
        check_vma=False,
    )
```

```python
import jax
import jax.numpy as jnp
from jax import lax
from jax.experimental import pallas as pl
from jax.experimental.pallas import tpu as pltpu
from jax.sharding import PartitionSpec as P


HEADS = 16
HD = 128
PICK = 16
RATE = 8
TOK = 128
NZ, NX, NC = 8, 4, 2
ROWS = 40
MAIN = 24
GROUP = 32
HALF = GROUP * PICK // 2
SCALE = HD ** (-0.5)
BF = jnp.bfloat16
F32 = jnp.float32

VM = pl.BlockSpec(memory_space=pltpu.VMEM)
SM = pl.BlockSpec(memory_space=pltpu.SMEM)


def dot(a, b):
    return lax.dot_general(a, b, (((1,), (0,)), ((), ())), preferred_element_type=F32)


def dot_t(a, b):
    return lax.dot_general(a, b, (((1,), (1,)), ((), ())), preferred_element_type=F32)


def dot_l(a, b):
    return lax.dot_general(a, b, (((0,), (0,)), ((), ())), preferred_element_type=F32)


def chooser(off):
    row = lax.broadcasted_iota(jnp.int32, (PICK, TOK), 0)
    tok = lax.broadcasted_iota(jnp.int32, (PICK, TOK), 1)
    return jnp.where(tok == row * RATE + off, 1.0, 0.0).astype(BF)


def small(mib=12):
    return pltpu.CompilerParams(vmem_limit_bytes=mib << 20)


def pick_kernel(pos_ref, off_hbm, l_hbm, d_hbm, q_hbm, k_hbm, v_hbm, g_hbm, o_hbm, off_ref, l_ref, d_ref, x_ref, o_ref, sems, out_sems):
    loads = [
        pltpu.make_async_copy(src, dst, sems.at[i])
        for i, (src, dst) in enumerate(
            (
                (off_hbm, off_ref),
                (l_hbm.at[0], l_ref),
                (d_hbm.at[0], d_ref),
                (q_hbm.at[0], x_ref.at[0]),
                (k_hbm.at[0], x_ref.at[1]),
                (v_hbm.at[0], x_ref.at[2]),
                (g_hbm.at[0], x_ref.at[3]),
            )
        )
    ]
    for load in loads:
        load.start()
    n = pos_ref[0]
    src = lax.broadcasted_iota(jnp.int32, (TOK, TOK), 0)
    dst = lax.broadcasted_iota(jnp.int32, (TOK, TOK), 1)
    place = jnp.where(dst == (n % 8) * PICK + src // RATE, 1.0, 0.0).astype(BF)
    for load in loads[:3]:
        load.wait()
    head = lax.broadcasted_iota(jnp.int32, (HEADS, TOK), 0)
    lane = lax.broadcasted_iota(jnp.int32, (HEADS, TOK), 1)
    off = jnp.zeros((HEADS, TOK), jnp.int32)
    for h in range(HEADS):
        off = jnp.where(head == h, off_ref[0, h], off)
    hit = (lane % RATE) == off
    lses = dot(jnp.where(hit, l_ref[...].astype(F32), 0.0).astype(BF), place)
    dlts = dot(jnp.where(hit, d_ref[...].astype(F32), 0.0).astype(BF), place)
    row = lax.broadcasted_iota(jnp.int32, (8, HD), 0)
    for h in range(HEADS):
        lse = jnp.broadcast_to(lses[h:h + 1], (8, HD))
        dlt = jnp.broadcast_to(dlts[h:h + 1], (8, HD))
        stats = jnp.where(row == n // 8, lse, jnp.where(row == 4 + n // 8, dlt, 0.0))
        o_ref[h, 0, 16:MAIN] = stats.astype(BF)
        o_ref[h, 1, 16:MAIN] = jnp.zeros((8, HD), BF)
    choose = [chooser(off_ref[0, h]) for h in range(HEADS)]
    stores = []
    for core in range(2):
        for part, first in ((2 * core, 0), (2 * core + 1, MAIN)):
            loads[3 + part].wait()
            for h in range(HEADS):
                rows = dot(choose[h], x_ref[part, :, h * HD:(h + 1) * HD])
                o_ref[h, core, first:first + 16] = rows.astype(BF)
        store = pltpu.make_async_copy(o_ref.at[:, core], o_hbm.at[:, core], out_sems.at[core])
        store.start()
        stores.append(store)
    for store in stores:
        store.wait()


def pick_all(pos, offsets, lse, delta, query, key, value, grad):
    raw = pl.BlockSpec(memory_space=pltpu.HBM)
    return pl.pallas_call(
        pick_kernel,
        in_specs=[SM] + [raw] * 7,
        out_specs=raw,
        out_shape=jax.ShapeDtypeStruct((HEADS, 2, ROWS, HD), BF),
        scratch_shapes=[
            pltpu.SMEM((1, HEADS), jnp.int32),
            pltpu.VMEM((HEADS, TOK), BF),
            pltpu.VMEM((HEADS, TOK), BF),
            pltpu.VMEM((4, TOK, HEADS * HD), BF),
            pltpu.VMEM((HEADS, 2, ROWS, HD), BF),
            pltpu.SemaphoreType.DMA((7,)),
            pltpu.SemaphoreType.DMA((2,)),
        ],
        name="pick_all",
    )(pos, offsets, lse, delta, query, key, value, grad).reshape(GROUP, ROWS, HD)


def score_kernel(off_ref, q_ref, k_ref, l_ref, p_ref, offs_ref, st_ref):
    step = pl.program_id(0)

    @pl.when(step == 0)
    def _():
        st_ref[...] = l_ref[0].astype(F32)
        for h in range(HEADS):
            offs_ref[h:h + 1, :] = jnp.full((1, TOK), off_ref[0, h], jnp.int32)

    lses = st_ref[pl.ds(pl.multiple_of(step * 4, 4), 4), :]
    for i in range(4):
        cols = slice(i * HD, (i + 1) * HD)
        p_ref[i] = jnp.exp(dot_t(k_ref[0, :, cols], q_ref[0, :, cols]) * SCALE - lses[i:i + 1])


def local_scores(offsets, query, key, lse):
    wide = pl.BlockSpec((1, TOK, 4 * HD), lambda i: (0, 0, i))
    stat = pl.BlockSpec((1, HEADS, TOK), lambda i: (0, 0, 0))
    return pl.pallas_call(
        score_kernel,
        grid=(4,),
        in_specs=[SM, wide, wide, stat],
        out_specs=[pl.BlockSpec((4, TOK, TOK), lambda i: (i, 0, 0)), pl.BlockSpec((HEADS, TOK), lambda i: (0, 0))],
        out_shape=[jax.ShapeDtypeStruct((HEADS, TOK, TOK), F32), jax.ShapeDtypeStruct((HEADS, TOK), jnp.int32)],
        scratch_shapes=[pltpu.VMEM((HEADS, TOK), F32)],
        compiler_params=small(),
        cost_estimate=pl.CostEstimate(flops=16 * 2 * 128 ** 3 * 4, bytes_accessed=2097152, transcendentals=262144),
        name="local_scores",
    )(offsets, query, key, lse)


def local_kernel(p_ref, q_ref, k_ref, v_ref, g_ref, d_ref, dq_ref, dk_ref, dv_ref, st_ref):
    step = pl.program_id(0)

    @pl.when(step == 0)
    def _():
        st_ref[...] = d_ref[0].astype(F32)

    dlts = st_ref[pl.ds(pl.multiple_of(step * 4, 4), 4), :]
    for i in range(4):
        cols = slice(i * HD, (i + 1) * HD)
        q, k, v, g = q_ref[0, :, cols], k_ref[0, :, cols], v_ref[0, :, cols], g_ref[0, :, cols]
        p = p_ref[i]
        ds = (p * (dot_t(v, g) - dlts[i:i + 1])).astype(BF)
        dv_ref[:, cols] = dot(p.astype(BF), g).astype(BF)
        dk_ref[:, cols] = (dot(ds, q) * SCALE).astype(BF)
        dq_ref[:, cols] = (dot_l(ds, k) * SCALE).astype(BF)


def local_grads(probs, query, key, value, grad, delta):
    wide = pl.BlockSpec((1, TOK, 4 * HD), lambda i: (0, 0, i))
    out = pl.BlockSpec((TOK, 4 * HD), lambda i: (0, i))
    stat = pl.BlockSpec((1, HEADS, TOK), lambda i: (0, 0, 0))
    shape = jax.ShapeDtypeStruct((TOK, HEADS * HD), BF)
    return pl.pallas_call(
        local_kernel,
        grid=(4,),
        in_specs=[pl.BlockSpec((4, TOK, TOK), lambda i: (i, 0, 0)), wide, wide, wide, wide, stat],
        out_specs=[out, out, out],
        out_shape=[shape, shape, shape],
        scratch_shapes=[pltpu.VMEM((HEADS, TOK), F32)],
        compiler_params=small(),
        cost_estimate=pl.CostEstimate(flops=16 * 4 * 2 * 128 ** 3 * 4, bytes_accessed=4718592, transcendentals=0),
        name="local_grads",
    )(probs, query, key, value, grad, delta)


def query_side(q, g, k, v, lse, dlt):
    p = jnp.exp(dot_t(q, k) * SCALE - lse)
    ds = (p * (dot_t(g, v) - dlt)).astype(BF)
    return dot(ds, k)


def key_side(k, v, q, g, stats):
    lse = jnp.concatenate([stats[i:i + 1] for i in range(4)], axis=1)
    dlt = jnp.concatenate([stats[i:i + 1] for i in range(4, 8)], axis=1)
    p = jnp.exp(dot_t(k, q) * SCALE - lse)
    ds = (p * (dot_t(v, g) - dlt)).astype(BF)
    return dot(ds, q), dot(p.astype(BF), g)


def flat(rows):
    return rows.reshape(GROUP * PICK, HD)


def whole(core, mine_a, mine_b, other_a, other_b):
    zero = core == 0
    q = jnp.where(zero, mine_a, other_a)
    v = jnp.where(zero, other_a, mine_a)
    k = jnp.where(zero, mine_b, other_b)
    g = jnp.where(zero, other_b, mine_b)
    return flat(q), flat(k), flat(v), flat(g)


def stats_of(core, mine_a, other_a):
    return jnp.sum(jnp.where(core == 0, mine_a[:, 16:MAIN], other_a[:, 16:MAIN]).astype(F32), axis=0)


def share(core, rows):
    width = rows.shape[-1]
    t = rows.astype(F32).reshape(GROUP, 2, 8, width)
    return jnp.where(core == 0, t[:, 0], t[:, 1]).reshape(HALF, width)


def near_kernel(core_ref, a_ref, b_ref, oa_ref, ob_ref, sub_ref, col_ref, dq_ref, dk_ref, dv_ref):
    core = core_ref[0]
    q, k, v, g = whole(core, a_ref[:, 0:16], b_ref[...], oa_ref[:, 0:16], ob_ref[...])
    stats = stats_of(core, a_ref, oa_ref)
    turned = jnp.transpose(jnp.concatenate([stats, jnp.zeros((HD - 8, HD), F32)], axis=0))
    lse = share(core, jnp.concatenate([turned[:, i:i + 1] for i in range(4)], axis=0))
    dlt = share(core, jnp.concatenate([turned[:, i:i + 1] for i in range(4, 8)], axis=0))
    sq, sk, sv, sg = (share(core, rows).astype(BF) for rows in (q, k, v, g))
    for i, rows in enumerate((sq, sk, sv, sg)):
        sub_ref[i] = rows
    lane = lax.broadcasted_iota(jnp.int32, (HALF, HD), 1)
    col_ref[...] = jnp.where(lane == 0, lse, dlt)
    dq_ref[...] = query_side(sq, sg, k, v, lse, dlt)
    dk_ref[...], dv_ref[...] = key_side(sk, sv, q, g, stats)


def near_grads(*args):
    part = jax.ShapeDtypeStruct((HALF, HD), F32)
    return pl.pallas_call(
        near_kernel,
        in_specs=[SM] + [VM] * 4,
        out_specs=[VM] * 5,
        out_shape=[jax.ShapeDtypeStruct((4, HALF, HD), BF)] + [part] * 4,
        compiler_params=small(),
        cost_estimate=pl.CostEstimate(flops=14 * 2 * 256 * 256 * 128 * 2, bytes_accessed=1572864, transcendentals=262144),
        name="near_grads",
    )(*args)


def far_kernel(core_ref, a_ref, b_ref, oa_ref, ob_ref, sub_ref, col_ref, dq_ref, dk_ref, dv_ref, o_ref):
    core = core_ref[0]
    q, k, v, g = whole(core, a_ref[:, 0:16], b_ref[...], oa_ref[:, 0:16], ob_ref[...])
    stats = stats_of(core, a_ref, oa_ref)
    lse, dlt = col_ref[:, 0:1], col_ref[:, 1:2]
    dq = dq_ref[...] + query_side(sub_ref[0], sub_ref[3], k, v, lse, dlt)
    dk, dv = key_side(sub_ref[1], sub_ref[2], q, g, stats)
    parts = (dq * SCALE, (dk_ref[...] + dk) * SCALE, dv_ref[...] + dv)
    for i, part in enumerate(parts):
        rows = part.reshape(GROUP, 8, HD).astype(BF)
        for to, z in enumerate(OUT_ORDER):
            at = IN_ORDER.index(z) * 4
            o_ref[4 * to:4 * to + 4, 8 * i:8 * i + 8, :] = rows[at:at + 4]


def far_grads(*args):
    return pl.pallas_call(
        far_kernel,
        in_specs=[SM] + [VM] * 9,
        out_specs=VM,
        out_shape=jax.ShapeDtypeStruct((GROUP, 24, HD), BF),
        compiler_params=small(),
        name="far_grads",
    )(*args)


def combine_kernel(w_ref, dq_ref, dk_ref, dv_ref, off_ref, oq_hbm, ok_hbm, ov_hbm, out_ref, sems):
    row = lax.broadcasted_iota(jnp.int32, (PICK, RATE, HD), 1)
    stores = []
    for group in range(4):
        for h in range(4 * group, 4 * group + 4):
            hit = row == off_ref[h:h + 1, :].reshape(1, 1, TOK)
            first = OUT_ORDER.index(IN_ORDER[h // 2]) * 4 + h % 2 * 2
            for part, src in enumerate((dq_ref, dk_ref, dv_ref)):
                rows = slice(part * 8, (part + 1) * 8)
                w = jnp.concatenate([w_ref[first, rows, :].astype(F32), w_ref[first + 1, rows, :].astype(F32)], axis=0)
                local = src[:, h * HD:(h + 1) * HD].astype(F32).reshape(PICK, RATE, HD)
                total = local + jnp.where(hit, w[:, None, :], 0.0)
                out_ref[part, :, h * HD:(h + 1) * HD] = total.reshape(TOK, HD).astype(BF)
        cols = pl.ds(group * 4 * HD, 4 * HD)
        for part, dst in enumerate((oq_hbm, ok_hbm, ov_hbm)):
            store = pltpu.make_async_copy(out_ref.at[part, :, cols], dst.at[0, :, cols], sems.at[group, part])
            store.start()
            stores.append(store)
    for store in stores:
        store.wait()


def combine(wide, local):
    shape = jax.ShapeDtypeStruct((1, TOK, HEADS * HD), BF)
    return pl.pallas_call(
        combine_kernel,
        in_specs=[VM] * 5,
        out_specs=[pl.BlockSpec(memory_space=pltpu.HBM)] * 3,
        out_shape=[shape, shape, shape],
        scratch_shapes=[pltpu.VMEM((3, TOK, HEADS * HD), BF), pltpu.SemaphoreType.DMA((4, 3))],
        compiler_params=small(),
        name="combine",
    )(wide, *local)


def place_of(z, x, c):
    return (z * NX + x) * NC + c


def column(half, place):
    return place if half == 0 else NX - 1 - place


def groups_of(order):
    return [[place_of(z, column(half, p), c) for z in order for p in range(2) for c in range(NC)] for half in range(2)]


IN_ORDER = (5, 4, 3, 2, 1, 0, 7, 6)
OUT_ORDER = IN_ORDER


def move(value, route):
    count, seats = lax.axis_size("section"), lax.axis_size("seq")
    pairs = []
    for s in range(count):
        for z in range(NZ):
            for x in range(NX):
                for c in range(NC):
                    target = route(s, x, c)
                    if target is not None:
                        ts, tx, tc = target
                        pairs.append((s * seats + place_of(z, x, c), (ts % count) * seats + place_of(z, tx, tc)))
    return lax.ppermute(value, ("section", "seq"), pairs)


def swap(value, order):
    return lax.all_to_all(value, "seq", 0, 0, axis_index_groups=groups_of(order), tiled=True)


def body(queries, key_rows, value_rows, grad_out, log_sums, deltas, offsets):
    seat = lax.axis_index("seq").astype(jnp.int32)
    x = seat // NC % NX
    core = (seat % NC).reshape(1)
    z = seat // (NX * NC)
    turn = sum(jnp.where(z == at, i, 0) for i, at in enumerate(IN_ORDER))
    pos = (turn * 4 + jnp.where(x < 2, x, NX - 1 - x) * 2 + seat % NC).reshape(1)
    picked = pick_all(pos, offsets, log_sums, deltas, queries, key_rows, value_rows, grad_out)
    mine = swap(picked, IN_ORDER)
    grad = move(grad_out, lambda s, x, c: (s - 1, x, c))
    probs, offs = local_scores(offsets, queries, key_rows, log_sums)
    a, b = mine[:, :MAIN], mine[:, MAIN:]
    far_a = move(a, lambda s, x, c: (s, 3 - x, c))
    far_b = move(b, lambda s, x, c: (s - c, 3 - x, c))
    other_a = move(a, lambda s, x, c: (s, x, 1 - c))
    own_b = move(b, lambda s, x, c: (s - c, x, c))
    other_b = move(own_b, lambda s, x, c: (s, x, 1 - c))
    other_far_a = move(far_a, lambda s, x, c: (s, x, 1 - c))
    other_far_b = move(far_b, lambda s, x, c: (s, x, 1 - c))
    local = local_grads(probs, queries, key_rows, value_rows, grad, deltas)
    part = near_grads(core, a, own_b, other_a, other_b)
    back = swap(far_grads(core, far_a, far_b, other_far_a, other_far_b, *part), OUT_ORDER)
    return tuple(combine(back, (*local, offs)))


def solution(mesh):
    rows = P("section", "seq", None)
    stats = P("section", None, "seq")
    return jax.shard_map(
        body,
        mesh=mesh,
        in_specs=(rows, rows, rows, rows, stats, stats, P("seq", None)),
        out_specs=(rows, rows, rows),
        check_vma=False,
    )
```
